32 devices in a mesh: dp: 4 (over z), fsdp: 8 (over y, x, core).
Axes of the slice: x: 2, y: 2, z: 4, core: 2. Of those that a mesh axis runs over, the one named last changes fastest.
Arguments:
- byte_embeddings: bfloat16 [49152, 512], P(('dp', 'fsdp')), may hold values from -6 to 6
- byte_item: int32 [49152], P(('dp', 'fsdp')), may hold values from 0 to 223, as said below
- byte_mask: int32 [49152], P(('dp', 'fsdp')), may hold values from 0 to 1, as said below
- w_pool: bfloat16 [1536, 512], P(('dp', 'fsdp')), may hold values from -0.15625 to 0.15625
- b_pool: bfloat16 [512], P(('dp', 'fsdp')), may hold values from -3 to 3
- ln1_gain: bfloat16 [512], P(('dp', 'fsdp')), may hold values from 0.5 to 1.5
- ln1_bias: bfloat16 [512], P(('dp', 'fsdp')), may hold values from -3 to 3
- w_qkv: bfloat16 [512, 1536], P(('dp', 'fsdp')), may hold values from -0.25 to 0.25
- pos_u: bfloat16 [512], P(('dp', 'fsdp')), may hold values from -3 to 3
- pos_v: bfloat16 [512], P(('dp', 'fsdp')), may hold values from -3 to 3
- w_pos: bfloat16 [512, 512], P(('dp', 'fsdp')), may hold values from -0.25 to 0.25
- w_out: bfloat16 [512, 512], P(('dp', 'fsdp')), may hold values from -0.75 to 0.75
- ln2_gain: bfloat16 [512], P(('dp', 'fsdp')), may hold values from 0.5 to 1.5
- ln2_bias: bfloat16 [512], P(('dp', 'fsdp')), may hold values from -3 to 3
- w_ff1: bfloat16 [512, 2048], P(('dp', 'fsdp')), may hold values from -0.25 to 0.25
- b_ff1: bfloat16 [2048], P(('dp', 'fsdp')), may hold values from -3 to 3
- w_ff2: bfloat16 [2048, 512], P(('dp', 'fsdp')), may hold values from -0.125 to 0.125
- b_ff2: bfloat16 [512], P(('dp', 'fsdp')), may hold values from -3 to 3
- w_up: bfloat16 [512, 1536], P(('dp', 'fsdp')), may hold values from -0.25 to 0.25
- b_up: bfloat16 [1536], P(('dp', 'fsdp')), may hold values from -3 to 3
- cotangent: bfloat16 [49152, 512], P(('dp', 'fsdp')), may hold values from -6 to 6
Outputs:
- block_output: bfloat16 [49152, 512], P(('dp', 'fsdp'))
- input_grad: bfloat16 [49152, 512], P(('dp', 'fsdp'))
- grad_w_pool: float32 [1536, 512], P(('dp', 'fsdp'))
- grad_b_pool: float32 [512], P(('dp', 'fsdp'))
- grad_ln1_gain: float32 [512], P(('dp', 'fsdp'))
- grad_ln1_bias: float32 [512], P(('dp', 'fsdp'))
- grad_w_qkv: float32 [512, 1536], P(('dp', 'fsdp'))
- grad_pos_u: float32 [512], P(('dp', 'fsdp'))
- grad_pos_v: float32 [512], P(('dp', 'fsdp'))
- grad_w_pos: float32 [512, 512], P(('dp', 'fsdp'))
- grad_w_out: float32 [512, 512], P(('dp', 'fsdp'))
- grad_ln2_gain: float32 [512], P(('dp', 'fsdp'))
- grad_ln2_bias: float32 [512], P(('dp', 'fsdp'))
- grad_w_ff1: float32 [512, 2048], P(('dp', 'fsdp'))
- grad_b_ff1: float32 [2048], P(('dp', 'fsdp'))
- grad_w_ff2: float32 [2048, 512], P(('dp', 'fsdp'))
- grad_b_ff2: float32 [512], P(('dp', 'fsdp'))
- grad_w_up: float32 [512, 1536], P(('dp', 'fsdp'))
- grad_b_up: float32 [1536], P(('dp', 'fsdp'))
The draws below stay inside these ranges and needn't reach their ends.
Inputs may be any that keep to these rules, and one draw needn't show every extreme that they name: `byte_item`: the bytes of one item stand together on one device, start at a multiple of 3 and carry one number; numbers never fall along the array and differ between items. Each device holds whole items of 100 to 512 triplets, then possibly one padding region with a number of its own. The numbers of device k lie in 7k to 7k + 6, and its last region carries the highest of them. `byte_mask`: zero for the last one or two bytes of some items and for a device's padding region, one elsewhere.
All inputs are finite; a program needn't handle non-finite values.
Results may differ from the reference program's by a relative error of at most 0.017.
Values may be sent and summed in bfloat16 or wider, within the bound.
No kernel may reach another device: no remote copies, remote signals or barrier semaphores. Data moves between devices by JAX's collectives and lax.ppermute only.
A program may use at most 128 MiB of HBM per device.

```python
import jax
import jax.numpy as jnp
from jax import lax

D = 512
H = 8
DH = 64
FF = 2048
TRIP_DEV = 512
ITEM_MIN = 100
SLOTS = 6
QBLK = 256
TRIPS = 16384
BYTES = 49152


def item_layout(key):
    base_key = jax.random.fold_in(key, 31)
    key_len, key_pad = jax.random.split(base_key)
    device_count = TRIPS // TRIP_DEV
    lengths = jax.random.randint(key_len, (device_count, SLOTS), ITEM_MIN, TRIP_DEV + 1)
    item_ends = jnp.cumsum(lengths, axis=1)
    places = jnp.arange(TRIP_DEV)
    trip_item = jnp.sum((item_ends[:, None, :] <= places[None, :, None]).astype(jnp.int32), axis=2)
    kept_items = jnp.sum((item_ends <= TRIP_DEV).astype(jnp.int32), axis=1)
    pad_counts = jax.random.randint(key_pad, (device_count, SLOTS + 1), 0, 3)
    pad_here = jnp.take_along_axis(pad_counts, trip_item, axis=1)
    is_last = jnp.any((item_ends[:, None, :] == places[None, :, None] + 1) & (item_ends[:, None, :] <= TRIP_DEV), axis=2)
    live_trip = trip_item < kept_items[:, None]
    column_index = jnp.arange(3)
    cut_tail = is_last[:, :, None] & (column_index[None, None, :] >= 3 - pad_here[:, :, None])
    byte_live = live_trip[:, :, None] & jnp.logical_not(cut_tail)
    device_rows = jnp.arange(device_count)[:, None]
    last_region = trip_item == trip_item[:, -1:]
    raise_last = last_region & ((device_rows > 0) | (trip_item > 0))
    numbered = jnp.where(raise_last, SLOTS, trip_item)
    item_ident = numbered + device_rows * (SLOTS + 1)
    byte_items = jnp.broadcast_to(item_ident[:, :, None], (device_count, TRIP_DEV, 3)).reshape(-1)
    return (byte_items.astype(jnp.int32), byte_live.astype(jnp.int32).reshape(-1))


def draw_byte_item(key, part):
    return item_layout(key)[0]


def draw_byte_mask(key, part):
    return item_layout(key)[1]


def strengthened(entries, key, source, target, blocks, factor):
    owner, partner = [(jnp.arange(entries.shape[axis_at]) // (entries.shape[axis_at] // blocks)).reshape([-1 if axis == axis_at else 1 for axis in range(entries.ndim)]) for axis_at in (source, target)]
    chosen = jax.random.permutation(key, blocks)[partner]
    strong = (owner == chosen) | (owner == (partner + blocks // 2) % blocks)
    return jnp.where(strong, factor * entries, entries)


def block_levels(key, extent, cuts, low, largest):
    def one(dim, blocks):
        draws = jax.random.uniform(jax.random.fold_in(jax.random.fold_in(key, 6), dim), (blocks,), jnp.float32, low / len(cuts), largest / len(cuts))
        return jnp.repeat(jnp.exp(draws), extent[dim] // blocks).reshape((-1,) + (1,) * (len(extent) - dim - 1))

    loudness = one(*cuts[0])
    for cut in cuts[1:]:
        loudness = loudness * one(*cut)
    return loudness


def centred(stream_key, dims, scale, most, cuts=(), dtype=jnp.bfloat16):
    loudness = block_levels(stream_key, dims, cuts, -0.22, 0.18) if cuts else 1.0
    entries = jax.random.normal(stream_key, dims, jnp.float32) * scale * loudness
    return jnp.minimum(jnp.maximum(entries, -most), most).astype(dtype)


def bell_draw_with(key, extent, deviation, limit, cuts, heavy, kind=jnp.bfloat16):
    drawn = deviation * jax.random.normal(key, extent, jnp.float32)
    if cuts:
        drawn = drawn * block_levels(key, extent, cuts, -0.22, 0.18)
    return jnp.clip(strengthened(drawn, jax.random.fold_in(key, 3), *heavy), -limit, limit).astype(kind)


def setup_inputs(seed: int = 0) -> dict:
    key_of = jax.random.split(jax.random.key(seed), 22)
    return {
        "byte_embeddings": centred(key_of[0], (BYTES, D), 1.0, 6.0, ((0, 32),)),
        "byte_item": draw_byte_item(jax.random.fold_in(key_of[21], 71), 0),
        "byte_mask": draw_byte_mask(jax.random.fold_in(key_of[21], 71), 0),
        "w_pool": centred(key_of[3], (3 * D, D), (3 * D) ** -0.5, 0.15625, ((0, 32),)),
        "b_pool": centred(key_of[4], (D,), 0.5, 3.0, ((0, 32),)),
        "ln1_gain": jnp.clip(1.0 + 0.1 * jax.random.normal(key_of[5], (D,), jnp.float32), 0.5, 1.5).astype(jnp.bfloat16),
        "ln1_bias": centred(key_of[6], (D,), 0.5, 3.0, ((0, 32),)),
        "w_qkv": centred(key_of[7], (D, 3 * D), D ** -0.5, 0.25, ((0, 32),)),
        "pos_u": centred(key_of[8], (D,), 0.5, 3.0, ((0, 32),)),
        "pos_v": centred(key_of[9], (D,), 0.5, 3.0, ((0, 32),)),
        "w_pos": centred(key_of[10], (D, D), D ** -0.5, 0.25, ((0, 32),)),
        "w_out": centred(key_of[11], (D, D), (D // 8) ** -0.5, 0.75, ((0, 32),)),
        "ln2_gain": jnp.clip(1.0 + 0.1 * jax.random.normal(key_of[12], (D,), jnp.float32), 0.5, 1.5).astype(jnp.bfloat16),
        "ln2_bias": centred(key_of[13], (D,), 0.5, 3.0, ((0, 32),)),
        "w_ff1": centred(key_of[14], (D, FF), D ** -0.5, 0.25, ((0, 32),)),
        "b_ff1": centred(key_of[15], (FF,), 0.5, 3.0, ((0, 32),)),
        "w_ff2": centred(key_of[16], (FF, D), FF ** -0.5, 0.125, ((0, 32),)),
        "b_ff2": centred(key_of[17], (D,), 0.5, 3.0, ((0, 32),)),
        "w_up": centred(key_of[18], (D, 3 * D), D ** -0.5, 0.25, ((0, 32),)),
        "b_up": centred(key_of[19], (3 * D,), 0.5, 3.0, ((0, 32),)),
        "cotangent": bell_draw_with(key_of[20], (BYTES, D), 1.0, 6.0, ((0, 32),), (0, 1, 32, 2.75)),
    }


eps_norm = 1e-05
big_negative = -1e+30
highest = lax.Precision.HIGHEST

@jax.custom_vjp
def low(v):
    return lax.optimization_barrier(v.astype(jnp.bfloat16)).astype(jnp.float32)

@jax.custom_vjp
def low_back(v):
    return v

def low_keep(v):
    return (low(v), None)

def low_pass(kept, grad):
    return (grad,)

def back_keep(v):
    return (v, None)

def back_low(kept, grad):
    return (low(grad),)
low.defvjp(low_keep, low_pass)
low_back.defvjp(back_keep, back_low)

def matmul_hi(left, right):
    return jnp.dot(left, right, precision=highest, preferred_element_type=jnp.float32)

def layer_norm(values, gain_row, offset):
    centre = values - lax.optimization_barrier(jnp.mean(values, axis=-1, keepdims=True))
    variance = lax.optimization_barrier(jnp.mean(centre * centre, axis=-1, keepdims=True))
    return centre * lax.rsqrt(variance + eps_norm) * gain_row + offset

def sinusoids(length_rows, feature_width):
    places = jnp.arange(length_rows).astype(jnp.float32)
    frequency = 10000.0 ** (-(2.0 * jnp.arange(feature_width // 2).astype(jnp.float32)) / feature_width)
    angles = places[:, None] * frequency[None, :]
    return (jnp.sin(angles), jnp.cos(angles))

def position_features(projected, sine_rows, cosine_rows):
    half_width = projected.shape[-1] // 2
    sine_part = projected[..., :half_width]
    cosine_part = projected[..., half_width:]
    sine_wide = sine_rows[:, None, :]
    cosine_wide = cosine_rows[:, None, :]
    return jnp.concatenate([sine_part * sine_wide + cosine_part * cosine_wide, cosine_part * sine_wide - sine_part * cosine_wide], axis=-1)

def attention_ref(query_u, keys_l, values_l, query_pos, key_pos, trip_item):
    row_total = query_u.shape[0]
    block_count = row_total // QBLK
    scale_factor = DH ** (-0.5)
    all_rows = jnp.arange(row_total)

    def one_block(pieces):
        block_query, block_pos, block_item, block_rows = pieces
        scores = (jnp.einsum('qhc,khc->hqk', block_query, keys_l, precision=highest) + jnp.einsum('qhm,km->hqk', block_pos, key_pos, precision=highest)) * scale_factor
        scores = low_back(scores)
        allowed = (block_item[:, None] == trip_item[None, :]) & (block_rows[:, None] >= all_rows[None, :])
        scores = jnp.where(allowed[None], scores, big_negative)
        row_top = lax.optimization_barrier(jnp.max(scores, axis=-1, keepdims=True))
        total_log = row_top + jnp.log(lax.optimization_barrier(jnp.sum(jnp.exp(scores - row_top), axis=-1, keepdims=True)))
        probability = low(jnp.exp(scores - total_log))
        return jnp.einsum('hqk,khc->qhc', probability, values_l, precision=highest)
    pieces = (query_u.reshape(block_count, QBLK, H, DH), query_pos.reshape(block_count, QBLK, H, query_pos.shape[-1]), trip_item.reshape(block_count, QBLK), all_rows.reshape(block_count, QBLK))
    outputs = lax.map(jax.checkpoint(one_block), pieces)
    return outputs.reshape(row_total, H, DH)

def forward_buffer(x_rows, params, item_bytes, mask_bytes):
    w_pool, b_pool, ln1_gain, ln1_bias, w_qkv, pos_u, pos_v, w_pos, w_out, ln2_gain, ln2_bias, w_ff1, b_ff1, w_ff2, b_ff2, w_up, b_up = params
    byte_total, feature_width = x_rows.shape
    row_total = byte_total // 3
    mask_col = mask_bytes.astype(jnp.float32)[:, None]
    masked = x_rows * mask_col
    same_item = jnp.concatenate([jnp.zeros((2,), jnp.bool_), item_bytes[2:] == item_bytes[:-2]])
    moved = jnp.concatenate([jnp.zeros((2, feature_width), jnp.float32), masked[:-2]], axis=0)
    shifted = jnp.where(same_item[:, None], moved, 0.0)
    pooled = low_back(matmul_hi(shifted.reshape(row_total, 3 * feature_width), w_pool) + b_pool)
    normed = low(layer_norm(pooled, ln1_gain, ln1_bias))
    qkv_all = matmul_hi(normed, w_qkv)
    queries = low_back(qkv_all[:, :feature_width]).reshape(row_total, H, DH)
    keys_l = low(low_back(qkv_all[:, feature_width:2 * feature_width])).reshape(row_total, H, DH)
    values_l = low(low_back(qkv_all[:, 2 * feature_width:])).reshape(row_total, H, DH)
    query_u = low(queries + pos_u.reshape(H, DH))
    query_v = low(queries + pos_v.reshape(H, DH))
    projected = low_back(jnp.einsum('lhc,mhc->lhm', query_v, w_pos.reshape(feature_width, H, DH), precision=highest))
    sine_rows, cosine_rows = sinusoids(row_total, feature_width)
    query_pos = low(position_features(projected, sine_rows, cosine_rows))
    key_pos = low(jnp.concatenate([cosine_rows, sine_rows], axis=-1))
    trip_item = item_bytes.reshape(row_total, 3)[:, 0]
    context = attention_ref(query_u, keys_l, values_l, query_pos, key_pos, trip_item)
    context = low(low_back(context.reshape(row_total, feature_width)))
    residual = pooled + low_back(matmul_hi(context, w_out))
    normed_two = low(layer_norm(residual, ln2_gain, ln2_bias))
    hidden_pre = low_back(matmul_hi(normed_two, w_ff1) + b_ff1)
    hidden = low(jax.nn.gelu(hidden_pre, approximate=True))
    branch = low_back(matmul_hi(hidden, w_ff2) + b_ff2)
    short_out = low(residual + branch)
    upsampled = (matmul_hi(short_out, w_up) + b_up).reshape(byte_total, feature_width)
    return mask_col * (x_rows + upsampled)

def add_up(running, addend):
    return running + addend

def reference(byte_embeddings, byte_item, byte_mask, w_pool, b_pool, ln1_gain, ln1_bias, w_qkv, pos_u, pos_v, w_pos, w_out, ln2_gain, ln2_bias, w_ff1, b_ff1, w_ff2, b_ff2, w_up, b_up, cotangent):
    params = tuple((weight_arg.astype(jnp.float32) for weight_arg in (w_pool, b_pool, ln1_gain, ln1_bias, w_qkv, pos_u, pos_v, w_pos, w_out, ln2_gain, ln2_bias, w_ff1, b_ff1, w_ff2, b_ff2, w_up, b_up)))
    byte_rows = 3 * TRIP_DEV
    feature_width = byte_embeddings.shape[1]
    buffer_count = byte_embeddings.shape[0] // byte_rows
    x_all = byte_embeddings.astype(jnp.float32).reshape(buffer_count, byte_rows, feature_width)
    item_all = byte_item.reshape(buffer_count, byte_rows)
    mask_all = byte_mask.reshape(buffer_count, byte_rows)
    cot_all = cotangent.astype(jnp.float32).reshape(buffer_count, byte_rows, feature_width)

    def per_buffer(grad_totals, pieces):
        x_rows, item_bytes, mask_bytes, cot_rows = pieces

        def forward(x_in, params_in):
            return forward_buffer(x_in, params_in, item_bytes, mask_bytes)
        output, pullback = jax.vjp(forward, x_rows, params)
        x_grad, param_grads = pullback(cot_rows)
        grad_totals = jax.tree.map(add_up, grad_totals, param_grads)
        return (grad_totals, (output.astype(jnp.bfloat16), x_grad.astype(jnp.bfloat16)))
    zeros_start = tuple((jnp.zeros_like(weight_arg) for weight_arg in params))
    totals, (outputs, x_grads) = lax.scan(per_buffer, zeros_start, (x_all, item_all, mask_all, cot_all))
    return (outputs.reshape(-1, feature_width), x_grads.reshape(-1, feature_width), totals[0], totals[1], totals[2], totals[3], totals[4], totals[5], totals[6], totals[7], totals[8], totals[9], totals[10], totals[11], totals[12], totals[13], totals[14], totals[15], totals[16])
```

```python
import jax
import jax.numpy as jnp
from jax import lax
from jax.sharding import PartitionSpec as P

H = 8
DH = 64
QBLK = 256
AXES = ("dp", "fsdp")


eps_norm = 1e-05
big_negative = -1e30


def layer_norm(values, gain_row, offset):
    centre = values - jnp.mean(values, axis=-1, keepdims=True)
    variance = jnp.mean(centre * centre, axis=-1, keepdims=True)
    return centre * lax.rsqrt(variance + eps_norm) * gain_row + offset


def gelu_tanh(values):
    return jax.nn.gelu(values, approximate=True)


def sinusoids(length_rows, feature_width):
    places = jnp.arange(length_rows).astype(jnp.float32)
    frequency = 10000.0 ** (
        -(2.0 * jnp.arange(feature_width // 2).astype(jnp.float32)) / feature_width
    )
    angles = places[:, None] * frequency[None, :]
    return (jnp.sin(angles), jnp.cos(angles))


def position_features(projected, sine_rows, cosine_rows):
    half_width = projected.shape[-1] // 2
    sine_part = projected[..., :half_width]
    cosine_part = projected[..., half_width:]
    sine_wide = sine_rows[:, None, :]
    cosine_wide = cosine_rows[:, None, :]
    return jnp.concatenate(
        [
            sine_part * sine_wide + cosine_part * cosine_wide,
            cosine_part * sine_wide - sine_part * cosine_wide,
        ],
        axis=-1,
    )


def matmul(left, right):
    return jnp.dot(left, right, preferred_element_type=jnp.float32)


def matmul_t(left, right):
    return jnp.einsum("lb,ab->la", left, right, preferred_element_type=jnp.float32)


def inner_rows(left, right):
    return jnp.einsum("la,lb->ab", left, right, preferred_element_type=jnp.float32)


def back_shift(values, same_item):
    moved = jnp.concatenate([values[2:], jnp.zeros((2, values.shape[1]), values.dtype)], axis=0)
    keep_next = jnp.concatenate([same_item[2:], jnp.zeros((2,), jnp.bool_)])
    return jnp.where(keep_next[:, None], moved, 0.0)


def block_scores(
    query_block,
    query_pos_block,
    keys_block,
    key_pos_block,
    query_items,
    key_items,
    row_start,
    scale_factor,
):
    scores = jnp.einsum(
        "qhc,khc->hqk", query_block, keys_block, preferred_element_type=jnp.float32
    ) + jnp.einsum(
        "qhm,km->hqk", query_pos_block, key_pos_block, preferred_element_type=jnp.float32
    )
    scores = scores * scale_factor
    query_rows = row_start + jnp.arange(query_block.shape[0])
    key_rows = jnp.arange(keys_block.shape[0])
    allowed = (query_items[:, None] == key_items[None, :]) & (
        query_rows[:, None] >= key_rows[None, :]
    )
    return jnp.where(allowed[None], scores, big_negative)


def key_scores(query_block, query_u, query_pos, keys_l, key_pos, trip_item, scale_factor):
    row_start = query_block * QBLK
    row_stop = row_start + QBLK
    return block_scores(
        query_u[row_start:row_stop],
        query_pos[row_start:row_stop],
        keys_l[:row_stop],
        key_pos[:row_stop],
        trip_item[row_start:row_stop],
        trip_item[:row_stop],
        row_start,
        scale_factor,
    )


class Links:
    def __init__(self, dp, fsdp):
        self.count = dp * fsdp
        fsdp_bits = fsdp.bit_length() - 1
        all_bits = self.count.bit_length() - 1
        half = (fsdp_bits - 1) // 2
        self.core = [1]
        self.minor = [1 << b for b in range(1, 1 + half)]
        self.major = [1 << b for b in range(1 + half, fsdp_bits)]
        self.deep = [1 << b for b in range(fsdp_bits, all_bits)]

    def send(self, values, bit):
        return lax.ppermute(values, AXES, [(i, i ^ bit) for i in range(self.count)])

    def order(self, bits):
        masks = [0]
        for bit in bits:
            masks = masks + [m ^ bit for m in masks]
        return masks

    def part_bits(self, part):
        if part == 0:
            return self.deep + self.minor + self.major + self.core
        return self.deep + self.major + self.minor + self.core

    def gather(self, shard, split):
        held = shard[None]
        for bit in self.deep:
            held = jnp.concatenate([held, self.send(held, bit)], axis=0)
        outs = []
        for part, rows in enumerate((slice(0, split), slice(split, shard.shape[0]))):
            piece = held[:, rows]
            for bit in self.part_bits(part)[len(self.deep) :]:
                piece = jnp.concatenate([piece, self.send(piece, bit)], axis=0)
            outs.append(piece)
        return outs

    def reduce(self, parts):
        def add(left, right):
            return left.astype(jnp.float32) + right.astype(jnp.float32)

        outs = []
        for part, held in enumerate(parts):
            for bit in reversed(self.part_bits(part)[len(self.deep) :]):
                n = held.shape[0] // 2
                held = add(held[:n], self.send(held[n:], bit)).astype(jnp.bfloat16)
            outs.append(held)
        held = jnp.concatenate(outs, axis=1)
        for bit in reversed(self.deep):
            n = held.shape[0] // 2
            total = add(held[:n], self.send(held[n:], bit))
            held = total.astype(jnp.bfloat16)
        return total[0]


def fold(shard, width):
    return jnp.concatenate(
        [shard[:, j : j + width] for j in range(0, shard.shape[1], width)], axis=0
    )


def unfold(block, count):
    rows = block.shape[-2] // count
    return jnp.concatenate(
        [block[..., j * rows : (j + 1) * rows, :] for j in range(count)], axis=-1
    )


def per_device(links, *args):
    (
        byte_embeddings,
        byte_item,
        byte_mask,
        w_pool,
        b_pool,
        ln1_gain,
        ln1_bias,
        w_qkv,
        pos_u,
        pos_v,
        w_pos,
        w_out,
        ln2_gain,
        ln2_bias,
        w_ff1,
        b_ff1,
        w_ff2,
        b_ff2,
        w_up,
        b_up,
        cotangent,
    ) = args
    n_dev = links.count
    me = lax.axis_index(AXES)
    width = w_pos.shape[1]
    r_pool = w_pool.shape[0]
    r = w_pos.shape[0]
    r_ff2 = w_ff2.shape[0]
    vectors = [b_pool, ln1_gain, ln1_bias, pos_u, pos_v, ln2_gain, ln2_bias, b_ff2, b_ff1, b_up]
    lengths = [v.shape[0] for v in vectors]
    starts = [sum(lengths[:i]) for i in range(len(lengths))]
    vec_len = sum(lengths)

    def absolute(part, piece):
        masks = jnp.array(links.order(links.part_bits(part)))
        inverse = jnp.argsort(masks)
        return jnp.take(piece, inverse[jnp.arange(n_dev) ^ me], axis=0)

    def relative(part, piece):
        masks = jnp.array(links.order(links.part_bits(part)))
        return jnp.take(piece, masks ^ me, axis=0)

    vec_row = jnp.pad(jnp.concatenate(vectors)[None], ((0, 15), (0, width - vec_len)))
    shard_a = jnp.concatenate([w_pool, vec_row, fold(w_qkv, width), w_pos], axis=0)
    split_a = r_pool + 16
    half_up = fold(w_up, width)
    shard_b = jnp.concatenate(
        [w_out, fold(w_ff1, width), half_up[:r], half_up[r:], w_ff2], axis=0
    )
    split_b = r + 4 * r + r
    got_a = [absolute(p, x) for p, x in enumerate(links.gather(shard_a, split_a))]
    got_b = [absolute(p, x) for p, x in enumerate(links.gather(shard_b, split_b))]

    def whole(block, count):
        block = unfold(block, count)
        return block.reshape(n_dev * block.shape[1], block.shape[2])

    pool_weight = whole(got_a[0][:, :r_pool], 1)
    vec_all = got_a[0][:, r_pool, :]
    (
        pool_bias,
        norm1_gain,
        norm1_bias,
        bias_u,
        bias_v,
        norm2_gain,
        norm2_bias,
        ff2_bias,
        ff1_bias,
        up_bias,
    ) = [vec_all[:, s : s + k].reshape(-1) for s, k in zip(starts, lengths)]
    qkv_weight = whole(got_a[1][:, : 3 * r], 3)
    pos_weight = whole(got_a[1][:, 3 * r :], 1)
    out_weight = whole(got_b[0][:, :r], 1)
    ff1_weight = whole(got_b[0][:, r : 5 * r], 4)
    up_weight = whole(jnp.concatenate([got_b[0][:, 5 * r :], got_b[1][:, : 2 * r]], axis=1), 3)
    ff2_weight = whole(got_b[1][:, 2 * r :], 1)

    byte_total, feature_width = byte_embeddings.shape
    row_total = byte_total // 3
    block_count = row_total // QBLK
    scale_factor = DH ** (-0.5)
    mask_col = byte_mask[:, None] > 0
    masked = jnp.where(mask_col, byte_embeddings, jnp.zeros_like(byte_embeddings))
    same_item = jnp.concatenate([jnp.zeros((2,), jnp.bool_), byte_item[2:] == byte_item[:-2]])
    moved = jnp.concatenate([jnp.zeros((2, feature_width), jnp.bfloat16), masked[:-2]], axis=0)
    shifted = jnp.where(same_item[:, None], moved, jnp.zeros_like(moved))
    grouped = shifted.reshape(row_total, 3 * feature_width)
    pooled = matmul(grouped, pool_weight) + pool_bias.astype(jnp.float32)
    normed = layer_norm(
        pooled, norm1_gain.astype(jnp.float32), norm1_bias.astype(jnp.float32)
    ).astype(jnp.bfloat16)
    qkv_all = matmul(normed, qkv_weight)
    queries = qkv_all[:, :feature_width].reshape(row_total, H, DH)
    keys_l = (
        qkv_all[:, feature_width : 2 * feature_width].astype(jnp.bfloat16).reshape(row_total, H, DH)
    )
    values_l = qkv_all[:, 2 * feature_width :].astype(jnp.bfloat16).reshape(row_total, H, DH)
    query_u = (queries + bias_u.astype(jnp.float32).reshape(H, DH)).astype(jnp.bfloat16)
    query_v = (queries + bias_v.astype(jnp.float32).reshape(H, DH)).astype(jnp.bfloat16)
    projected = jnp.einsum(
        "lhc,mhc->lhm",
        query_v,
        pos_weight.reshape(feature_width, H, DH),
        preferred_element_type=jnp.float32,
    )
    sine_rows, cosine_rows = sinusoids(row_total, feature_width)
    query_pos = position_features(projected, sine_rows, cosine_rows).astype(jnp.bfloat16)
    key_pos = jnp.concatenate([cosine_rows, sine_rows], axis=-1).astype(jnp.bfloat16)
    trip_item = byte_item.reshape(row_total, 3)[:, 0]
    contexts = []
    log_totals = []
    for query_block in range(block_count):
        key_stop = (query_block + 1) * QBLK
        scores = key_scores(
            query_block, query_u, query_pos, keys_l, key_pos, trip_item, scale_factor
        )
        row_top = jnp.max(scores, axis=-1, keepdims=True)
        total_log = row_top + jnp.log(jnp.sum(jnp.exp(scores - row_top), axis=-1, keepdims=True))
        probability = jnp.exp(scores - total_log).astype(jnp.bfloat16)
        contexts.append(
            jnp.einsum(
                "hqk,khc->qhc", probability, values_l[:key_stop], preferred_element_type=jnp.float32
            )
        )
        log_totals.append(total_log)
    context = (
        jnp.concatenate(contexts, axis=0).reshape(row_total, feature_width).astype(jnp.bfloat16)
    )
    residual = pooled + matmul(context, out_weight)
    normed_two = layer_norm(
        residual, norm2_gain.astype(jnp.float32), norm2_bias.astype(jnp.float32)
    ).astype(jnp.bfloat16)
    hidden_pre = matmul(normed_two, ff1_weight) + ff1_bias.astype(jnp.float32)
    hidden = gelu_tanh(hidden_pre).astype(jnp.bfloat16)
    branch = matmul(hidden, ff2_weight) + ff2_bias.astype(jnp.float32)
    short_out = (residual + branch).astype(jnp.bfloat16)
    upsampled = (matmul(short_out, up_weight) + up_bias.astype(jnp.float32)).reshape(
        byte_total, feature_width
    )
    block_output = jnp.where(mask_col, byte_embeddings.astype(jnp.float32) + upsampled, 0.0).astype(
        jnp.bfloat16
    )
    zero_offset = jnp.zeros((feature_width,), jnp.float32)
    up_grad = jnp.where(mask_col, cotangent, jnp.zeros_like(cotangent)).reshape(
        row_total, 3 * feature_width
    )
    grad_up_w = inner_rows(short_out, up_grad)
    grad_up_b = jnp.sum(up_grad.astype(jnp.float32), axis=0)
    short_grad = matmul_t(up_grad, up_weight)
    branch_grad = short_grad.astype(jnp.bfloat16)
    grad_ff2_w = inner_rows(hidden, branch_grad)
    grad_ff2_b = jnp.sum(branch_grad.astype(jnp.float32), axis=0)
    hidden_grad = matmul_t(branch_grad, ff2_weight)
    unused_out, gelu_pull = jax.vjp(gelu_tanh, hidden_pre)
    pre_grad = gelu_pull(hidden_grad)[0].astype(jnp.bfloat16)
    grad_ff1_w = inner_rows(normed_two, pre_grad)
    grad_ff1_b = jnp.sum(pre_grad.astype(jnp.float32), axis=0)
    norm_two_grad = matmul_t(pre_grad, ff1_weight)
    unused_two, norm_pull_two = jax.vjp(
        layer_norm, residual, norm2_gain.astype(jnp.float32), zero_offset
    )
    from_norm_two, grad_ln2_gain, grad_ln2_bias = norm_pull_two(norm_two_grad)
    residual_grad = short_grad + from_norm_two
    attn_grad = residual_grad.astype(jnp.bfloat16)
    grad_out_w = inner_rows(context, attn_grad)
    context_grad = matmul_t(attn_grad, out_weight).astype(jnp.bfloat16).reshape(row_total, H, DH)
    qu_grads = []
    pos_grads = []
    key_grad = jnp.zeros((row_total, H, DH), jnp.float32)
    value_grad = jnp.zeros((row_total, H, DH), jnp.float32)
    for query_block in range(block_count):
        row_start = query_block * QBLK
        row_stop = row_start + QBLK
        key_stop = row_stop
        pad_rows = row_total - key_stop
        scores = key_scores(
            query_block, query_u, query_pos, keys_l, key_pos, trip_item, scale_factor
        )
        probs_full = jnp.exp(scores - log_totals[query_block])
        prob_low = probs_full.astype(jnp.bfloat16)
        ctx_grad_block = context_grad[row_start:row_stop]
        prob_grad = jnp.einsum(
            "qhc,khc->hqk", ctx_grad_block, values_l[:key_stop], preferred_element_type=jnp.float32
        )
        row_inner = jnp.sum(probs_full * prob_grad, axis=-1, keepdims=True)
        score_grad = (probs_full * (prob_grad - row_inner)).astype(jnp.bfloat16)
        qu_grads.append(
            jnp.einsum(
                "hqk,khc->qhc", score_grad, keys_l[:key_stop], preferred_element_type=jnp.float32
            )
            * scale_factor
        )
        pos_grads.append(
            jnp.einsum(
                "hqk,km->qhm", score_grad, key_pos[:key_stop], preferred_element_type=jnp.float32
            )
            * scale_factor
        )
        key_part = (
            jnp.einsum(
                "hqk,qhc->khc",
                score_grad,
                query_u[row_start:row_stop],
                preferred_element_type=jnp.float32,
            )
            * scale_factor
        )
        value_part = jnp.einsum(
            "hqk,qhc->khc", prob_low, ctx_grad_block, preferred_element_type=jnp.float32
        )
        key_grad = key_grad + jnp.pad(key_part, ((0, pad_rows), (0, 0), (0, 0)))
        value_grad = value_grad + jnp.pad(value_part, ((0, pad_rows), (0, 0), (0, 0)))
    qu_grad = jnp.concatenate(qu_grads, axis=0)
    pos_grad = jnp.concatenate(pos_grads, axis=0)
    half_width = feature_width // 2
    grad_first = pos_grad[..., :half_width]
    grad_second = pos_grad[..., half_width:]
    sine_wide = sine_rows[:, None, :]
    cosine_wide = cosine_rows[:, None, :]
    proj_grad = jnp.concatenate(
        [
            grad_first * sine_wide - grad_second * cosine_wide,
            grad_first * cosine_wide + grad_second * sine_wide,
        ],
        axis=-1,
    ).astype(jnp.bfloat16)
    grad_pos_w = jnp.einsum(
        "lhm,lhc->mhc", proj_grad, query_v, preferred_element_type=jnp.float32
    ).reshape(feature_width, feature_width)
    qv_grad = jnp.einsum(
        "lhm,mhc->lhc",
        proj_grad,
        pos_weight.reshape(feature_width, H, DH),
        preferred_element_type=jnp.float32,
    )
    grad_u = jnp.sum(qu_grad, axis=0).reshape(feature_width)
    grad_v = jnp.sum(qv_grad, axis=0).reshape(feature_width)
    qkv_grad = jnp.concatenate(
        [
            (qu_grad + qv_grad).reshape(row_total, feature_width),
            key_grad.reshape(row_total, feature_width),
            value_grad.reshape(row_total, feature_width),
        ],
        axis=1,
    ).astype(jnp.bfloat16)
    grad_qkv_w = inner_rows(normed, qkv_grad)
    norm_one_grad = matmul_t(qkv_grad, qkv_weight)
    unused_one, norm_pull_one = jax.vjp(
        layer_norm, pooled, norm1_gain.astype(jnp.float32), zero_offset
    )
    from_norm_one, grad_ln1_gain, grad_ln1_bias = norm_pull_one(norm_one_grad)
    pooled_grad = (residual_grad + from_norm_one).astype(jnp.bfloat16)
    grad_pool_w = inner_rows(grouped, pooled_grad)
    grad_pool_b = jnp.sum(pooled_grad.astype(jnp.float32), axis=0)
    shift_grad = matmul_t(pooled_grad, pool_weight).reshape(byte_total, feature_width)
    input_grad = jnp.where(
        mask_col, cotangent.astype(jnp.float32) + back_shift(shift_grad, same_item), 0.0
    ).astype(jnp.bfloat16)

    def blocks(grad, count):
        rows = grad.shape[0] // n_dev
        grad = grad.astype(jnp.bfloat16).reshape(n_dev, rows, grad.shape[1])
        return jnp.concatenate(
            [grad[:, :, j * width : (j + 1) * width] for j in range(count)], axis=1
        )

    up_blocks = blocks(grad_up_w, 3)
    part_a = jnp.concatenate([blocks(grad_out_w, 1), blocks(grad_ff1_w, 4), up_blocks[:, :r]], axis=1)
    part_b = jnp.concatenate([up_blocks[:, r:], blocks(grad_ff2_w, 1)], axis=1)
    sum_b = links.reduce([relative(0, part_a), relative(1, part_b)])
    grad_vectors = [
        grad_pool_b,
        grad_ln1_gain,
        grad_ln1_bias,
        grad_u,
        grad_v,
        grad_ln2_gain,
        grad_ln2_bias,
        grad_ff2_b,
        grad_ff1_b,
        grad_up_b,
    ]
    vec = jnp.concatenate([g.reshape(n_dev, -1) for g in grad_vectors], axis=1)
    vec = jnp.pad(vec, ((0, 0), (0, width - vec_len)))
    high = vec.astype(jnp.bfloat16)
    low = (vec - high.astype(jnp.float32)).astype(jnp.bfloat16)
    vec_blocks = jnp.pad(jnp.stack([high, low], axis=1), ((0, 0), (0, 14), (0, 0)))
    part_a = jnp.concatenate([blocks(grad_pool_w, 1), vec_blocks], axis=1)
    part_b = jnp.concatenate([blocks(grad_qkv_w, 3), blocks(grad_pos_w, 1)], axis=1)
    sum_a = links.reduce([relative(0, part_a), relative(1, part_b)])
    vec_sum = sum_a[r_pool] + sum_a[r_pool + 1]
    (
        out_pool_b,
        out_ln1_gain,
        out_ln1_bias,
        out_u,
        out_v,
        out_ln2_gain,
        out_ln2_bias,
        out_ff2_b,
        out_ff1_b,
        out_up_b,
    ) = [vec_sum[s : s + k] for s, k in zip(starts, lengths)]
    return (
        block_output,
        input_grad,
        sum_a[:r_pool],
        out_pool_b,
        out_ln1_gain,
        out_ln1_bias,
        unfold(sum_a[split_a : split_a + 3 * r], 3),
        out_u,
        out_v,
        sum_a[split_a + 3 * r :],
        sum_b[:r],
        out_ln2_gain,
        out_ln2_bias,
        unfold(sum_b[r : 5 * r], 4),
        out_ff1_b,
        sum_b[split_b + 2 * r :],
        out_ff2_b,
        unfold(sum_b[5 * r : 5 * r + 3 * r], 3),
        out_up_b,
    )


def solution(mesh):
    links = Links(mesh.shape["dp"], mesh.shape["fsdp"])
    rows = P(AXES, None)
    flat = P(AXES)
    ranks = (2, 1, 1, 2, 1, 1, 1, 2, 1, 1, 2, 2, 1, 1, 2, 1, 2, 1, 2, 1, 2)
    out_ranks = (2, 2, 2, 1, 1, 1, 2, 1, 1, 2, 2, 1, 1, 2, 1, 2, 1, 2, 1)
    return jax.shard_map(
        lambda *args: per_device(links, *args),
        mesh=mesh,
        in_specs=tuple(rows if k == 2 else flat for k in ranks),
        out_specs=tuple(rows if k == 2 else flat for k in out_ranks),
        check_vma=False,
    )
```

```python
import jax
import jax.numpy as jnp
from jax import lax
from jax.experimental import pallas as pl
from jax.experimental.pallas import tpu as pltpu
from jax.sharding import PartitionSpec as P

H = 8
DH = 64
QBLK = 256
AXES = ("dp", "fsdp")


eps_norm = 1e-05
big_negative = -1e30

F32 = jnp.float32
BF16 = jnp.bfloat16
BLOCKS = 32
PAIRS = 4
CH = 64
VMEM = pl.BlockSpec(memory_space=pltpu.VMEM)
SMEM = pl.BlockSpec(memory_space=pltpu.SMEM)
ANY = pl.BlockSpec(memory_space=pl.ANY)
GELU_C = 0.7978845608028654
ROWS_A = 128
ROWS_B = 192
VEC = slice(48, 64)


def mm(left, right, cl=1, cr=0):
    return lax.dot_general(left, right, (((cl,), (cr,)), ((), ())), preferred_element_type=F32)


def weight(ref, start, rows):
    block = ref[:, start : start + rows, :]
    return block.reshape(block.shape[0] * rows, block.shape[2])


def weight_ff2(ref, start, j):
    block = ref[8 * j : 8 * j + 8, start : start + 64, :]
    return block.reshape(512, block.shape[2])


def load_pieces(me, plan, refs, dest, sem):
    copies = []
    for (masks, first, rows), ref in zip(plan, refs):
        for k, m in enumerate(masks):
            copies.append(
                pltpu.make_async_copy(ref.at[k], dest.at[me ^ m, pl.ds(first, rows)], sem)
            )
    for c in copies:
        c.start()


def wait_whole(dest, sem):
    pltpu.make_async_copy(dest, dest, sem).wait()


def lane_half(shape, s):
    return (lax.broadcasted_iota(jnp.int32, shape, len(shape) - 1) // DH) == s


def norm_stats(x):
    width = x.shape[-1]
    mean = jnp.sum(x, axis=-1, keepdims=True) * (1.0 / width)
    centre = x - mean
    var = jnp.sum(centre * centre, axis=-1, keepdims=True) * (1.0 / width)
    rstd = lax.rsqrt(var + eps_norm)
    return centre * rstd, rstd


def norm_back(dy, xhat, rstd, gain):
    width = dy.shape[-1]
    d = dy * gain
    m1 = jnp.sum(d, axis=-1, keepdims=True) * (1.0 / width)
    m2 = jnp.sum(d * xhat, axis=-1, keepdims=True) * (1.0 / width)
    return rstd * (d - m1 - xhat * m2)


def forward_kernel(plan, n_pieces, me_ref, *refs):
    pieces = refs[:n_pieces]
    (grouped, item_col, item_row, sine, cosine, key_pos) = refs[n_pieces : n_pieces + 6]
    (pooled, normed, qu, qv, keys, vals, prob, ctx, vecs, w_out_hbm) = refs[
        n_pieces + 6 : n_pieces + 16
    ]
    (w, w_pos, bias, proj, qcat, kcat, tmp, sem, sem2) = refs[n_pieces + 16 :]
    me = me_ref[0]
    rows = grouped.shape[0]
    load_pieces(me, plan, pieces, w, sem)
    for r in range(0, rows, CH):
        row = r + lax.broadcasted_iota(jnp.int32, (CH, rows), 0)
        col = lax.broadcasted_iota(jnp.int32, (CH, rows), 1)
        allowed = (item_col[r : r + CH, :] == item_row[...]) & (row >= col)
        bias[r : r + CH, :] = jnp.where(allowed, 0.0, big_negative)
    kcat[:, 0:rows] = key_pos[...]
    wait_whole(w, sem)
    keep = pltpu.make_async_copy(w, w_out_hbm, sem2)
    keep.start()
    vec = jnp.sum(w[:, VEC, :].astype(F32), axis=0)
    vecs[...] = vec
    tmp[...] = mm(grouped[...], weight(w, 0, 48))
    for r in range(0, rows, CH):
        x = tmp[r : r + CH, :] + vec[0:1]
        pooled[r : r + CH, :] = x
        xhat, rstd = norm_stats(x)
        normed[r : r + CH, :] = (xhat * vec[1:2] + vec[2:3]).astype(BF16)
    tmp[...] = mm(normed[...], weight(w, 64, 16))
    for r in range(0, rows, CH):
        x = tmp[r : r + CH, :]
        u = (x + vec[3:4]).astype(BF16)
        v = (x + vec[4:5]).astype(BF16)
        for p in range(PAIRS):
            qu[p, r : r + CH, :] = u[:, 128 * p : 128 * p + 128]
            qv[p, r : r + CH, :] = v[:, 128 * p : 128 * p + 128]
    x = mm(normed[...], weight(w, 80, 16)).astype(BF16)
    for p in range(PAIRS):
        keys[p] = x[:, 128 * p : 128 * p + 128]
    x = mm(normed[...], weight(w, 96, 16)).astype(BF16)
    for p in range(PAIRS):
        vals[p] = x[:, 128 * p : 128 * p + 128]
    x = weight(w, 112, 16)
    for p in range(PAIRS):
        w_pos[p] = x[:, 128 * p : 128 * p + 128]

    @pl.loop(0, PAIRS)
    def _(p):
        kcat[:, rows : rows + 128] = keys[p]
        for s in range(2):
            half = lane_half((rows, 128), s)
            zero = jnp.zeros((rows, 128), BF16)
            proj[...] = mm(jnp.where(half, qv[p], zero), w_pos[p], 1, 1)
            for r in range(0, rows, CH):
                a = proj[r : r + CH, 0:256]
                b = proj[r : r + CH, 256:512]
                si = sine[r : r + CH, :]
                co = cosine[r : r + CH, :]
                qcat[r : r + CH, 0:256] = (a * si + b * co).astype(BF16)
                qcat[r : r + CH, 256:512] = (b * si - a * co).astype(BF16)
            qcat[:, 512:640] = jnp.where(half, qu[p], zero)
            for q in range(rows // QBLK):
                first, stop = q * QBLK, (q + 1) * QBLK
                tmp[0:QBLK, 0:stop] = mm(qcat[first:stop, :], kcat[0:stop, :], 1, 1)
                for r in range(0, QBLK, CH):
                    x = tmp[r : r + CH, 0:stop] * (DH ** (-0.5)) + bias[
                        first + r : first + r + CH, 0:stop
                    ]
                    e = jnp.exp(x - jnp.max(x, axis=-1, keepdims=True))
                    inv = 1.0 / jnp.sum(e, axis=-1, keepdims=True)
                    prob[2 * p + s, first + r : first + r + CH, 0:stop] = (e * inv).astype(BF16)
                out = mm(prob[2 * p + s, first:stop, 0:stop], vals[p, 0:stop, :]).astype(BF16)
                if s == 0:
                    ctx[p, first:stop, :] = out
                else:
                    ctx[p, first:stop, :] = jnp.where(
                        lane_half((QBLK, 128), 1), out, ctx[p, first:stop, :]
                    )

    keep.wait()


def join(ref):
    return jnp.concatenate([ref[p] for p in range(PAIRS)], axis=1)


def store_blocks(grads, place, grad, first, rows=16, start=0):
    for k in range(grad.shape[0] // rows):
        grads[place[start + k], first : first + rows, :] = grad[k * rows : (k + 1) * rows].astype(BF16)


class Half:
    def __init__(self, ref, part):
        self.ref = ref
        self.part = part

    def __getitem__(self, d):
        return self.ref[self.part, d]


def middle_kernel(plan, n_pieces, me_ref, place_ref, *refs):
    pieces = refs[:n_pieces]
    (pooled, ctx, up_grad, vecs) = refs[n_pieces : n_pieces + 4]
    (res_grad, cg, short_out, vec_grads, w_up_hbm, keep_hbm, send_hbm) = refs[
        n_pieces + 4 : n_pieces + 11
    ]
    (w, grads, xhat, rstd, n2, hidden, slope, acc, tmp, sgrad, bg, sem, sem2) = refs[n_pieces + 11 :]
    me = me_ref[0]
    place_a, place_b = Half(place_ref, 0), Half(place_ref, 1)
    rows = pooled.shape[0]
    load_pieces(me, plan, pieces, w, sem)
    wait_whole(w, sem)
    keep_up = pltpu.make_async_copy(w.at[:, 80:128], w_up_hbm, sem2.at[0])
    keep_up.start()
    gain2, bias2 = vecs[5:6, :], vecs[6:7, :]
    acc[...] = pooled[...] + mm(join(ctx), weight(w, 0, 16))
    for r in range(0, rows, CH):
        xh, rs = norm_stats(acc[r : r + CH, :])
        xhat[r : r + CH, :] = xh
        rstd[r : r + CH, :] = jnp.broadcast_to(rs, (CH, 128))
        n2[r : r + CH, :] = (xh * gain2 + bias2).astype(BF16)
    for j in range(4):
        tmp[...] = mm(n2[...], weight(w, 16 + 16 * j, 16))
        b1 = vecs[8 + j : 9 + j, :]
        for r in range(0, rows, CH):
            x = tmp[r : r + CH, :] + b1
            x2 = x * x
            t = jnp.tanh(GELU_C * (x + 0.044715 * (x * x2)))
            hidden[j, r : r + CH, :] = (0.5 * x * (1.0 + t)).astype(BF16)
            slope[j, r : r + CH, :] = 0.5 * (1.0 + t) + (0.5 * GELU_C) * x * (1.0 - t * t) * (
                1.0 + (3.0 * 0.044715) * x2
            )
        acc[...] += mm(hidden[j], weight_ff2(w, 128, j))
    b2 = vecs[7:8, :]
    for r in range(0, rows, CH):
        short_out[r : r + CH, :] = (acc[r : r + CH, :] + b2).astype(BF16)
    sgrad[...] = (
        mm(up_grad[:, 0:512], weight(w, 80, 16), 1, 1)
        + mm(up_grad[:, 512:1024], weight(w, 96, 16), 1, 1)
        + mm(up_grad[:, 1024:1536], weight(w, 112, 16), 1, 1)
    )
    bg[...] = sgrad[...].astype(BF16)
    store_blocks(grads, place_a, mm(short_out[...], up_grad[:, 0:512], 0, 0), 80)
    store_blocks(grads, place_b, mm(short_out[...], up_grad[:, 512:1024], 0, 0), 96)
    store_blocks(grads, place_b, mm(short_out[...], up_grad[:, 1024:1536], 0, 0), 112)
    vec_grads[...] = jnp.zeros(vec_grads.shape, F32)
    for j in range(3):
        vec_grads[12 + j : 13 + j, :] = jnp.sum(
            up_grad[:, 512 * j : 512 * j + 512].astype(F32), axis=0, keepdims=True
        )
    vec_grads[7:8, :] = jnp.sum(bg[...].astype(F32), axis=0, keepdims=True)
    for j in range(4):
        store_blocks(grads, place_b, mm(hidden[j], bg[...], 0, 0), 128, 64, 8 * j)
        tmp[...] = mm(bg[...], weight_ff2(w, 128, j), 1, 1)
        total = jnp.zeros((1, 512), F32)
        for r in range(0, rows, CH):
            x = (tmp[r : r + CH, :] * slope[j, r : r + CH, :]).astype(BF16)
            hidden[j, r : r + CH, :] = x
            total = total + jnp.sum(x.astype(F32), axis=0, keepdims=True)
        vec_grads[8 + j : 9 + j, :] = total
        store_blocks(grads, place_a, mm(n2[...], hidden[j], 0, 0), 16 + 16 * j)
        back = mm(hidden[j], weight(w, 16 + 16 * j, 16), 1, 1)
        if j == 0:
            acc[...] = back
        else:
            acc[...] += back
    dgain = jnp.zeros((1, 512), F32)
    dbias = jnp.zeros((1, 512), F32)
    for r in range(0, rows, CH):
        dy = acc[r : r + CH, :]
        xh = xhat[r : r + CH, :]
        dgain = dgain + jnp.sum(dy * xh, axis=0, keepdims=True)
        dbias = dbias + jnp.sum(dy, axis=0, keepdims=True)
        x = sgrad[r : r + CH, :] + norm_back(dy, xh, rstd[r : r + CH, 0:1], gain2)
        res_grad[r : r + CH, :] = x
        bg[r : r + CH, :] = x.astype(BF16)
    vec_grads[5:6, :] = dgain
    vec_grads[6:7, :] = dbias
    store_blocks(grads, place_a, mm(join(ctx), bg[...], 0, 0), 0)
    out_keep = pltpu.make_async_copy(grads.at[0 : BLOCKS // 2], keep_hbm, sem2.at[1])
    out_send = pltpu.make_async_copy(grads.at[BLOCKS // 2 : BLOCKS], send_hbm, sem2.at[2])
    out_send.start()
    out_keep.start()
    x = mm(bg[...], weight(w, 0, 16), 1, 1).astype(BF16)
    for p in range(PAIRS):
        cg[p] = x[:, 128 * p : 128 * p + 128]
    keep_up.wait()
    out_send.wait()
    out_keep.wait()


def attention_back_kernel(
    prob, cg, vals, keys, qu, qv, key_pos, sine, cosine, w_hbm, vec_in,
    q_grad, k_grad, v_grad, pos_w_grad, vec_grads,
    w_pos, pgrad, sg, posg, sem,
):
    rows = key_pos.shape[0]
    copies = [
        pltpu.make_async_copy(
            w_hbm.at[:, 112:128, 128 * p : 128 * p + 128], w_pos.at[p], sem.at[p]
        )
        for p in range(PAIRS)
    ]
    for c in copies:
        c.start()
    for c in copies:
        c.wait()
    vec_grads[...] = vec_in[...]
    n_q = rows // QBLK

    @pl.loop(0, PAIRS)
    def _(p):
        wp = w_pos[p].reshape(rows, 128)
        u_sums = []
        v_sums = []
        for s in range(2):
            h = 2 * p + s
            half = lane_half((rows, 128), s)
            zero = jnp.zeros((rows, 128), BF16)
            cgm = jnp.where(half, cg[p], zero)
            qum = jnp.where(half, qu[p], zero)
            qvm = jnp.where(half, qv[p], zero)
            for q in range(n_q):
                first, stop = q * QBLK, (q + 1) * QBLK
                pgrad[first:stop, 0:stop] = mm(cgm[first:stop], vals[p, 0:stop, :], 1, 1)
                for r in range(first, stop, CH):
                    pr = prob[h, r : r + CH, 0:stop].astype(F32)
                    t = pr * pgrad[r : r + CH, 0:stop]
                    inner = jnp.sum(t, axis=-1, keepdims=True)
                    sg[r : r + CH, 0:stop] = ((t - pr * inner) * (DH ** (-0.5))).astype(BF16)
                posg[first:stop, :] = mm(sg[first:stop, 0:stop], key_pos[0:stop, :])
                qg = mm(sg[first:stop, 0:stop], keys[p, 0:stop, :])
                half_q = lane_half((QBLK, 128), s)
                if s == 0:
                    q_grad[p, first:stop, :] = qg
                else:
                    q_grad[p, first:stop, :] = jnp.where(half_q, qg, q_grad[p, first:stop, :])
                kg = mm(sg[first:stop, 0:stop], qum[first:stop], 0, 0)
                vg = mm(prob[h, first:stop, 0:stop], cgm[first:stop], 0, 0)
                if s == 0 and q == n_q - 1:
                    pass
                if s == 0 and q == 0:
                    k_grad[p] = jnp.zeros((rows, 128), F32)
                    v_grad[p] = jnp.zeros((rows, 128), F32)
                k_grad[p, 0:stop, :] += kg
                v_grad[p, 0:stop, :] += vg
            for r in range(0, rows, CH):
                a = posg[r : r + CH, 0:256]
                b = posg[r : r + CH, 256:512]
                si = sine[r : r + CH, :]
                co = cosine[r : r + CH, :]
                pgrad[r : r + CH, 0:256] = a * si - b * co
                pgrad[r : r + CH, 256:512] = a * co + b * si
            sg_full = pgrad[...].astype(BF16)
            gw = mm(sg_full, qvm, 0, 0)
            if s == 0:
                pos_w_grad[p] = gw
            else:
                pos_w_grad[p] += gw
            qvg = jnp.where(half, mm(sg_full, wp), 0.0)
            v_sums.append(jnp.sum(qvg, axis=0, keepdims=True))
            u_sums.append(
                jnp.sum(jnp.where(half, q_grad[p], 0.0), axis=0, keepdims=True)
            )
            q_grad[p] += qvg
        u_row = u_sums[0] + u_sums[1]
        v_row = v_sums[0] + v_sums[1]
        for k in range(PAIRS):

            @pl.when(p == k)
            def _():
                vec_grads[3:4, 128 * k : 128 * k + 128] = u_row
                vec_grads[4:5, 128 * k : 128 * k + 128] = v_row


def last_kernel(
    place_ref, q_grad, k_grad, v_grad, pos_w_grad, normed, grouped, pooled, res_grad, w_hbm, vecs, vec_in,
    pg, w_pool_out, keep_hbm, send_hbm,
    w, grads, qkvg, acc, vec, sem,
):
    place_a, place_b = Half(place_ref, 0), Half(place_ref, 1)
    rows = pooled.shape[0]
    load = pltpu.make_async_copy(w_hbm.at[:, 0:112], w, sem.at[0])
    load.start()
    vec[...] = vec_in[...]
    for j, ref in enumerate((q_grad, k_grad, v_grad)):
        for p in range(PAIRS):
            qkvg[j, :, 128 * p : 128 * p + 128] = ref[p].astype(BF16)
    for j in range(3):
        store_blocks(grads, place_b, mm(normed[...], qkvg[j], 0, 0), 64 + 16 * j)
    store_blocks(grads, place_b, join(pos_w_grad), 112)
    load.wait()
    keep_pool = pltpu.make_async_copy(w.at[:, 0:48], w_pool_out, sem.at[1])
    keep_pool.start()
    acc[...] = (
        mm(qkvg[0], weight(w, 64, 16), 1, 1)
        + mm(qkvg[1], weight(w, 80, 16), 1, 1)
        + mm(qkvg[2], weight(w, 96, 16), 1, 1)
    )
    gain1 = vecs[1:2, :]
    dgain = jnp.zeros((1, 512), F32)
    dbias = jnp.zeros((1, 512), F32)
    dpool = jnp.zeros((1, 512), F32)
    for r in range(0, rows, CH):
        dy = acc[r : r + CH, :]
        xh, rs = norm_stats(pooled[r : r + CH, :])
        dgain = dgain + jnp.sum(dy * xh, axis=0, keepdims=True)
        dbias = dbias + jnp.sum(dy, axis=0, keepdims=True)
        x = (res_grad[r : r + CH, :] + norm_back(dy, xh, rs, gain1)).astype(BF16)
        pg[r : r + CH, :] = x
        dpool = dpool + jnp.sum(x.astype(F32), axis=0, keepdims=True)
    vec[0:1, :] = dpool
    vec[1:2, :] = dgain
    vec[2:3, :] = dbias
    table = vec[...].astype(BF16)
    for d in range(BLOCKS):
        grads[place_a[d], VEC, :] = table
    for j in range(3):
        g = mm(grouped[:, 512 * j : 512 * j + 512], pg[...], 0, 0)
        for k in range(32):
            granule = 32 * j + k
            d, sub = granule // 3, granule % 3
            grads[place_a[d], 16 * sub : 16 * sub + 16, :] = g[16 * k : 16 * k + 16].astype(BF16)
    out_send = pltpu.make_async_copy(grads.at[BLOCKS // 2 : BLOCKS], send_hbm, sem.at[2])
    out_keep = pltpu.make_async_copy(grads.at[0 : BLOCKS // 2], keep_hbm, sem.at[3])
    out_send.start()
    out_keep.start()
    keep_pool.wait()
    out_send.wait()
    out_keep.wait()


def bytes_kernel(emb, cot, cols, short_out, w_up, vecs, pg, w_pool, out, grad, tmp):
    rows = emb.shape[0]
    for j in range(3):
        tmp[...] = mm(short_out[...], weight(w_up, 16 * j, 16))
        up_bias = vecs[12 + j : 13 + j, :]
        for r in range(0, rows, CH):
            x = emb[r : r + CH, 512 * j : 512 * j + 512].astype(F32) + tmp[r : r + CH, :] + up_bias
            out[r : r + CH, 512 * j : 512 * j + 512] = jnp.where(
                cols[r : r + CH, j : j + 1] > 0, x, 0.0
            ).astype(BF16)
    pool = weight(w_pool, 0, 48)
    for j in range(3):
        src = (j + 2) % 3
        tmp[...] = mm(pg[...], pool[512 * src : 512 * src + 512, :], 1, 1)
        if j > 0:
            tmp[...] = pltpu.roll(tmp[...], rows - 1, 0)
        for r in range(0, rows, CH):
            x = tmp[r : r + CH, :]
            if j > 0:
                x = jnp.where(cols[r : r + CH, 3:4] > 0, x, 0.0)
            x = cot[r : r + CH, 512 * j : 512 * j + 512].astype(F32) + x
            grad[r : r + CH, 512 * j : 512 * j + 512] = jnp.where(
                cols[r : r + CH, j : j + 1] > 0, x, 0.0
            ).astype(BF16)


class Links:
    def __init__(self, dp, fsdp):
        self.count = dp * fsdp
        fsdp_bits = fsdp.bit_length() - 1
        all_bits = self.count.bit_length() - 1
        half = (fsdp_bits - 1) // 2
        self.core = [1]
        self.minor = [1 << b for b in range(1, 1 + half)]
        self.major = [1 << b for b in range(1 + half, fsdp_bits)]
        self.deep = [1 << b for b in range(fsdp_bits, all_bits)]

    def send(self, values, bit):
        return lax.ppermute(values, AXES, [(i, i ^ bit) for i in range(self.count)])

    def order(self, bits):
        masks = [0]
        for bit in bits:
            masks = masks + [m ^ bit for m in masks]
        return masks

    def part_bits(self, part):
        if part == 0:
            return self.deep + self.minor + self.major + self.core
        return self.deep + self.major + self.minor + self.core

    def gather(self, shard, split):
        held = shard[None]
        for bit in self.deep[:-1]:
            held = jnp.concatenate([held, self.send(held, bit)], axis=0)
        other = self.send(held, self.deep[-1])
        pieces = []
        for part, rows in enumerate((slice(0, split), slice(split, shard.shape[0]))):
            near = self.part_bits(part)[len(self.deep) : -1]
            piece = jnp.concatenate([held[:, rows], other[:, rows]], axis=0)
            masks = self.order(self.deep)
            for bit in near[:-1]:
                piece = jnp.concatenate([piece, self.send(piece, bit)], axis=0)
                masks = masks + [m ^ bit for m in masks]
            far = self.send(piece, near[-1])
            far_masks = [m ^ near[-1] for m in masks]
            pieces.append((masks, rows.start, piece))
            pieces.append((far_masks, rows.start, far))
        return pieces + [
            ([m ^ 1 for m in masks], first, self.send(piece, 1)) for masks, first, piece in pieces
        ]

    def reduce(self, keep, send, split):
        def add(left, right):
            return left.astype(jnp.float32) + right.astype(jnp.float32)

        got = self.send(send, 1)
        n = keep.shape[0]
        mine = [(keep[:, :split], got[:, :split]), (keep[:, split:], got[:, split:])]
        near = len(self.minor) + len(self.major)
        for step in range(near):
            n = n // 2
            sent = []
            for part in range(2):
                bit = self.part_bits(part)[: -1][-1 - step]
                left, right = mine[part]
                out = add(left[n:], right[n:]).astype(jnp.bfloat16)
                sent.append(self.send(out, bit))
            for part in range(2):
                left, right = mine[part]
                mine[part] = (add(left[:n], right[:n]).astype(jnp.bfloat16), sent[part])
        held = jnp.concatenate([add(*mine[0]), add(*mine[1])], axis=1)
        for bit in reversed(self.deep):
            n = held.shape[0] // 2
            held = add(held[:n], self.send(held[n:].astype(jnp.bfloat16), bit))
        return held[0]


def fold(shard, width):
    return jnp.concatenate(
        [shard[..., j : j + width] for j in range(0, shard.shape[-1], width)], axis=-2
    )


def unfold(block, count):
    rows = block.shape[-2] // count
    return jnp.concatenate(
        [block[..., j * rows : (j + 1) * rows, :] for j in range(count)], axis=-1
    )


def reblock(blocks, layout, count):
    m = blocks.shape[0]
    outs = []
    for first, rows, k in layout:
        x = unfold(blocks[:, first : first + rows], k)
        x = x.reshape(m * x.shape[1], x.shape[2]).reshape(count, -1, x.shape[2])
        outs.append(fold(x, blocks.shape[2]))
    return jnp.concatenate(outs, axis=1)


def layout_of(parts):
    out = []
    first = 0
    for rows, k in parts:
        out.append((first, rows, k))
        first += rows
    return out


def per_device(links, *args):
    (
        byte_embeddings,
        byte_item,
        byte_mask,
        w_pool,
        b_pool,
        ln1_gain,
        ln1_bias,
        w_qkv,
        pos_u,
        pos_v,
        w_pos,
        w_out,
        ln2_gain,
        ln2_bias,
        w_ff1,
        b_ff1,
        w_ff2,
        b_ff2,
        w_up,
        b_up,
        cotangent,
    ) = args
    n_dev = links.count
    me = lax.axis_index(AXES).astype(jnp.int32)
    width = w_pos.shape[1]
    r_pool, r, r_ff2 = w_pool.shape[0], w_pos.shape[0], w_ff2.shape[0]
    direct = n_dev == BLOCKS
    vectors = [b_pool, ln1_gain, ln1_bias, pos_u, pos_v, ln2_gain, ln2_bias, b_ff2, b_ff1, b_up]
    lengths = [v.shape[0] for v in vectors]
    vec_rows = [v * n_dev // width for v in lengths]
    vec_first = [sum(vec_rows[:i]) for i in range(len(vec_rows))]

    flat = jnp.arange(n_dev * lengths[8])
    table = []
    for v in vectors:
        k = v.shape[0]
        spread = jnp.where(flat[: n_dev * k] // k == me, jnp.tile(v, n_dev), jnp.zeros((), v.dtype))
        table.append(spread.reshape(-1, width))
    table.append(jnp.zeros((16 - sum(vec_rows), width), jnp.bfloat16))
    shard_a = jnp.concatenate([w_pool] + table + [fold(w_qkv, width), w_pos], axis=0)
    split_a = r_pool + 16
    shard_b = jnp.concatenate(
        [w_out, fold(w_ff1, width), fold(w_up, width), w_ff2], axis=0
    )
    split_b = 6 * r
    shard_a, shard_b = lax.optimization_barrier((shard_a, shard_b))
    pieces_a = links.gather(shard_a, split_a)
    pieces_b = links.gather(shard_b, split_b)
    layout_a = layout_of([(r_pool, 1), (16, 0), (3 * r, 3), (r, 1)])
    layout_b = layout_of([(r, 1), (4 * r, 4), (3 * r, 3), (r_ff2, 1)])
    layout_a32 = layout_of([(48, 1), (16, 0), (48, 3), (16, 1)])
    layout_b32 = layout_of([(16, 1), (64, 4), (48, 3), (64, 1)])

    if direct:
        base = me[None]
        order = [links.order(links.part_bits(p)) for p in range(2)]
        inverse = jnp.array([[o.index(m) for m in range(n_dev)] for o in order], jnp.int32)
        place = jnp.take(inverse, jnp.arange(n_dev) ^ me, axis=1)
    else:

        def canonical(pieces, layout):
            rows = {}
            for masks, first, arr in pieces:
                rows.setdefault(first, []).append((masks, arr))
            parts = []
            for first in sorted(rows):
                masks = sum([m for m, _ in rows[first]], [])
                arr = jnp.concatenate([a for _, a in rows[first]], axis=0)
                inverse = jnp.array([masks.index(m) for m in range(n_dev)])
                parts.append(jnp.take(arr, inverse[jnp.arange(n_dev) ^ me], axis=0))
            blocks = jnp.concatenate(parts, axis=1)
            outs = []
            for first, rows_, k in layout:
                if k == 0:
                    total = jnp.sum(blocks[:, first : first + rows_].astype(F32), axis=0)
                    outs.append(
                        jnp.concatenate(
                            [total[None], jnp.zeros((BLOCKS - 1,) + total.shape, F32)], axis=0
                        ).astype(BF16)
                    )
                else:
                    outs.append(reblock(blocks, [(first, rows_, k)], BLOCKS))
            return [(list(range(BLOCKS)), 0, jnp.concatenate(outs, axis=1))]

        pieces_a = canonical(pieces_a, layout_a)
        pieces_b = canonical(pieces_b, layout_b)
        base = jnp.zeros((1,), jnp.int32)
        place = jnp.tile(jnp.arange(BLOCKS, dtype=jnp.int32)[None], (2, 1))

    byte_total = byte_embeddings.shape[0]
    rows = byte_total // 3
    emb = byte_embeddings.reshape(rows, 3 * width)
    cot = cotangent.reshape(rows, 3 * width)
    mask3 = byte_mask.reshape(rows, 3)
    item = byte_item.reshape(rows, 3)[:, 0]
    same = item[1:] == item[:-1]
    no = jnp.zeros((1,), jnp.bool_)
    same_before = jnp.concatenate([no, same])[:, None]
    same_after = jnp.concatenate([same, no])[:, None]
    cols = jnp.concatenate([mask3, same_after.astype(jnp.int32)], axis=1)
    item_f = item.astype(F32)
    live = [mask3[:, j : j + 1] > 0 for j in range(3)]
    zero = jnp.zeros((), jnp.bfloat16)
    masked = [jnp.where(live[j], emb[:, j * width : (j + 1) * width], zero) for j in range(3)]
    up_grad = jnp.concatenate(
        [jnp.where(live[j], cot[:, j * width : (j + 1) * width], zero) for j in range(3)], axis=1
    )

    def down(x):
        moved = jnp.concatenate([jnp.zeros((1, width), x.dtype), x[:-1]], axis=0)
        return jnp.where(same_before, moved, zero)

    grouped = jnp.concatenate([down(masked[1]), down(masked[2]), masked[0]], axis=1)
    places = jnp.arange(rows).astype(F32)
    frequency = 10000.0 ** (-(2.0 * jnp.arange(width // 2).astype(F32)) / width)
    angles = places[:, None] * frequency[None, :]
    sine, cosine = jnp.sin(angles), jnp.cos(angles)
    key_pos = jnp.concatenate([cosine, sine], axis=1).astype(BF16)

    params = pltpu.CompilerParams(vmem_limit_bytes=60 << 20)
    sds = jax.ShapeDtypeStruct
    pair_bf = sds((PAIRS, rows, 128), BF16)
    pair_f = sds((PAIRS, rows, 128), F32)
    square = sds((rows, width), F32)
    table_f = sds((16, width), F32)

    plan_a = [(m, f, a.shape[1]) for m, f, a in pieces_a]
    n_a = len(plan_a)
    pooled, normed, qu, qv, keys, vals, prob, ctx, vecs, wa = pl.pallas_call(
        lambda *refs: forward_kernel(plan_a, n_a, *refs),
        out_shape=(
            square,
            sds((rows, width), BF16),
            pair_bf,
            pair_bf,
            pair_bf,
            pair_bf,
            sds((H, rows, rows), BF16),
            pair_bf,
            table_f,
            sds((BLOCKS, ROWS_A, width), BF16),
        ),
        in_specs=[SMEM] + [ANY] * n_a + [VMEM] * 6,
        out_specs=[VMEM] * 9 + [ANY],
        scratch_shapes=[
            pltpu.VMEM((BLOCKS, ROWS_A, width), BF16),
            pltpu.VMEM((PAIRS, width, 128), BF16),
            pltpu.VMEM((rows, rows), F32),
            pltpu.VMEM((rows, width), F32),
            pltpu.VMEM((rows, width + 128), BF16),
            pltpu.VMEM((rows, width + 128), BF16),
            pltpu.VMEM((rows, width), F32),
            pltpu.SemaphoreType.DMA,
            pltpu.SemaphoreType.DMA,
        ],
        compiler_params=params,
        name="forward",
    )(base, *[a for _, _, a in pieces_a], grouped, item_f[:, None], item_f[None, :], sine, cosine, key_pos)

    plan_b = [(m, f, a.shape[1]) for m, f, a in pieces_b]
    n_b = len(plan_b)
    half = BLOCKS // 2
    res_grad, cg, short_out, vec_grads, w_up_abs, keep_b, send_b = pl.pallas_call(
        lambda *refs: middle_kernel(plan_b, n_b, *refs),
        out_shape=(
            square,
            pair_bf,
            sds((rows, width), BF16),
            table_f,
            sds((BLOCKS, 48, width), BF16),
            sds((half, ROWS_B, width), BF16),
            sds((half, ROWS_B, width), BF16),
        ),
        in_specs=[SMEM, SMEM] + [ANY] * n_b + [VMEM] * 4,
        out_specs=[VMEM] * 4 + [ANY] * 3,
        scratch_shapes=[
            pltpu.VMEM((BLOCKS, ROWS_B, width), BF16),
            pltpu.VMEM((BLOCKS, ROWS_B, width), BF16),
            pltpu.VMEM((rows, width), F32),
            pltpu.VMEM((rows, 128), F32),
            pltpu.VMEM((rows, width), BF16),
            pltpu.VMEM((4, rows, 512), BF16),
            pltpu.VMEM((4, rows, 512), F32),
            pltpu.VMEM((rows, width), F32),
            pltpu.VMEM((rows, width), F32),
            pltpu.VMEM((rows, width), F32),
            pltpu.VMEM((rows, width), BF16),
            pltpu.SemaphoreType.DMA,
            pltpu.SemaphoreType.DMA((3,)),
        ],
        compiler_params=params,
        name="middle",
    )(base, place, *[a for _, _, a in pieces_b], pooled, ctx, up_grad, vecs)

    q_grad, k_grad, v_grad, pos_w_grad, vec_grads = pl.pallas_call(
        attention_back_kernel,
        out_shape=(pair_f, pair_f, pair_f, sds((PAIRS, width, 128), F32), table_f),
        in_specs=[VMEM] * 9 + [ANY, VMEM],
        out_specs=[VMEM] * 5,
        scratch_shapes=[
            pltpu.VMEM((PAIRS, BLOCKS, 16, 128), BF16),
            pltpu.VMEM((rows, width), F32),
            pltpu.VMEM((rows, rows), BF16),
            pltpu.VMEM((rows, width), F32),
            pltpu.SemaphoreType.DMA((PAIRS,)),
        ],
        compiler_params=params,
        name="attention_back",
    )(prob, cg, vals, keys, qu, qv, key_pos, sine, cosine, wa, vec_grads)

    pooled_grad, w_pool_abs, keep_a, send_a = pl.pallas_call(
        last_kernel,
        out_shape=(
            sds((rows, width), BF16),
            sds((BLOCKS, 48, width), BF16),
            sds((half, ROWS_A, width), BF16),
            sds((half, ROWS_A, width), BF16),
        ),
        in_specs=[SMEM] + [VMEM] * 8 + [ANY] + [VMEM] * 2,
        out_specs=[VMEM] + [ANY] * 3,
        scratch_shapes=[
            pltpu.VMEM((BLOCKS, 112, width), BF16),
            pltpu.VMEM((BLOCKS, ROWS_A, width), BF16),
            pltpu.VMEM((3, rows, width), BF16),
            pltpu.VMEM((rows, width), F32),
            pltpu.VMEM((16, width), F32),
            pltpu.SemaphoreType.DMA((4,)),
        ],
        compiler_params=params,
        name="last",
    )(place, q_grad, k_grad, v_grad, pos_w_grad, normed, grouped, pooled, res_grad, wa, vecs, vec_grads)

    out3, grad3 = pl.pallas_call(
        bytes_kernel,
        out_shape=(sds((rows, 3 * width), BF16), sds((rows, 3 * width), BF16)),
        in_specs=[VMEM] * 8,
        out_specs=[VMEM] * 2,
        scratch_shapes=[pltpu.VMEM((rows, width), F32)],
        compiler_params=params,
        name="bytes",
    )(emb, cot, cols, short_out, w_up_abs, vecs, pooled_grad, w_pool_abs)
    block_output = out3.reshape(byte_total, width)
    input_grad = grad3.reshape(byte_total, width)

    if direct:
        sum_b = links.reduce(keep_b, send_b, split_b)
        sum_a = links.reduce(keep_a, send_a, split_a)
    else:

        def owned(keep, send, layout, split):
            blocks = jnp.concatenate([keep, send], axis=0)
            outs = []
            for first, rows_, k in layout:
                if k == 0:
                    outs.append(jnp.tile(blocks[:1, first : first + rows_], (n_dev, 1, 1)))
                else:
                    outs.append(reblock(blocks, [(first, rows_, k)], n_dev))
            full = jnp.concatenate(outs, axis=1)
            parts = []
            for part, rows_ in enumerate((slice(0, split), slice(split, full.shape[1]))):
                masks = jnp.array(links.order(links.part_bits(part)))
                parts.append(jnp.take(full[:, rows_], masks ^ me, axis=0))
            full = jnp.concatenate(parts, axis=1)
            return links.reduce(full[: n_dev // 2], full[n_dev // 2 :], split)

        sum_b = owned(keep_b, send_b, layout_b32, split_b)
        sum_a = owned(keep_a, send_a, layout_a32, split_a)
    vec_sum = sum_a[r_pool : r_pool + 16]
    vec_out = []
    for first, k, n in zip(vec_first, lengths, vec_rows):
        line = vec_sum[first : first + n].reshape(-1)
        vec_out.append(lax.dynamic_slice(line, (me * k,), (k,)))
    (
        out_pool_b,
        out_ln1_gain,
        out_ln1_bias,
        out_u,
        out_v,
        out_ln2_gain,
        out_ln2_bias,
        out_ff2_b,
        out_ff1_b,
        out_up_b,
    ) = vec_out
    return (
        block_output,
        input_grad,
        sum_a[:r_pool],
        out_pool_b,
        out_ln1_gain,
        out_ln1_bias,
        unfold(sum_a[split_a : split_a + 3 * r], 3),
        out_u,
        out_v,
        sum_a[split_a + 3 * r :],
        sum_b[:r],
        out_ln2_gain,
        out_ln2_bias,
        unfold(sum_b[r : 5 * r], 4),
        out_ff1_b,
        sum_b[8 * r :],
        out_ff2_b,
        unfold(sum_b[5 * r : 8 * r], 3),
        out_up_b,
    )


def solution(mesh):
    links = Links(mesh.shape["dp"], mesh.shape["fsdp"])
    rows = P(AXES, None)
    flat = P(AXES)
    ranks = (2, 1, 1, 2, 1, 1, 1, 2, 1, 1, 2, 2, 1, 1, 2, 1, 2, 1, 2, 1, 2)
    out_ranks = (2, 2, 2, 1, 1, 1, 2, 1, 1, 2, 2, 1, 1, 2, 1, 2, 1, 2, 1)
    return jax.shard_map(
        lambda *args: per_device(links, *args),
        mesh=mesh,
        in_specs=tuple(rows if k == 2 else flat for k in ranks),
        out_specs=tuple(rows if k == 2 else flat for k in out_ranks),
        check_vma=False,
    )
```

```python
import jax
import jax.numpy as jnp
from jax import lax
from jax.experimental import pallas as pl
from jax.experimental.pallas import tpu as pltpu
from jax.sharding import PartitionSpec as P

H = 8
DH = 64
QBLK = 256
AXES = ("dp", "fsdp")


eps_norm = 1e-05
big_negative = -1e30

F32 = jnp.float32
BF16 = jnp.bfloat16
BLOCKS = 32
PAIRS = 4
CH = 64
VMEM = pl.BlockSpec(memory_space=pltpu.VMEM)
SMEM = pl.BlockSpec(memory_space=pltpu.SMEM)
ANY = pl.BlockSpec(memory_space=pl.ANY)
GELU_C = 0.7978845608028654
ROWS_A = 128
ROWS_B = 192
VEC = slice(48, 64)


def mm(left, right, cl=1, cr=0):
    return lax.dot_general(left, right, (((cl,), (cr,)), ((), ())), preferred_element_type=F32)


def weight(ref, start, rows):
    block = ref[:, start : start + rows, :]
    return block.reshape(block.shape[0] * rows, block.shape[2])


def weight_ff2(ref, start, j):
    block = ref[8 * j : 8 * j + 8, start : start + 64, :]
    return block.reshape(512, block.shape[2])


def load_pieces(me, plan, refs, dest, sem):
    copies = []
    for (mask, step), ref in zip(plan, refs):
        for k in range(ref.shape[0]):
            copies.append(pltpu.make_async_copy(ref.at[k], dest.at[step * k + (me ^ mask)], sem))
    for c in copies:
        c.start()


def wait_whole(dest, sem):
    pltpu.make_async_copy(dest, dest, sem).wait()


def lane_half(shape, s):
    return (lax.broadcasted_iota(jnp.int32, shape, len(shape) - 1) // DH) == s


def norm_stats(x):
    width = x.shape[-1]
    mean = jnp.sum(x, axis=-1, keepdims=True) * (1.0 / width)
    centre = x - mean
    var = jnp.sum(centre * centre, axis=-1, keepdims=True) * (1.0 / width)
    rstd = lax.rsqrt(var + eps_norm)
    return centre * rstd, rstd


def norm_back(dy, xhat, rstd, gain):
    width = dy.shape[-1]
    d = dy * gain
    m1 = jnp.sum(d, axis=-1, keepdims=True) * (1.0 / width)
    m2 = jnp.sum(d * xhat, axis=-1, keepdims=True) * (1.0 / width)
    return rstd * (d - m1 - xhat * m2)


def forward_kernel(plan, n_pieces, me_ref, *refs):
    pieces = refs[:n_pieces]
    (grouped, item_col, item_row, sine, cosine, key_pos) = refs[n_pieces : n_pieces + 6]
    (pooled, normed, qu, qv, keys, vals, prob, ctx, vecs, w_out_hbm) = refs[
        n_pieces + 6 : n_pieces + 16
    ]
    (w, w_pos, bias, proj, qcat, kcat, tmp, sem, sem2) = refs[n_pieces + 16 :]
    me = me_ref[0]
    rows = grouped.shape[0]
    load_pieces(me, plan, pieces, w, sem)
    for r in range(0, rows, CH):
        row = r + lax.broadcasted_iota(jnp.int32, (CH, rows), 0)
        col = lax.broadcasted_iota(jnp.int32, (CH, rows), 1)
        allowed = (item_col[r : r + CH, :] == item_row[...]) & (row >= col)
        bias[r : r + CH, :] = jnp.where(allowed, 0.0, big_negative)
    kcat[:, 0:rows] = key_pos[...]
    wait_whole(w, sem)
    keep = pltpu.make_async_copy(w, w_out_hbm, sem2)
    keep.start()
    vec = jnp.sum(w[:, VEC, :].astype(F32), axis=0)
    vecs[...] = vec
    tmp[...] = mm(grouped[...], weight(w, 0, 48))
    for r in range(0, rows, CH):
        x = tmp[r : r + CH, :] + vec[0:1]
        pooled[r : r + CH, :] = x
        xhat, rstd = norm_stats(x)
        normed[r : r + CH, :] = (xhat * vec[1:2] + vec[2:3]).astype(BF16)
    tmp[...] = mm(normed[...], weight(w, 64, 16))
    for r in range(0, rows, CH):
        x = tmp[r : r + CH, :]
        u = (x + vec[3:4]).astype(BF16)
        v = (x + vec[4:5]).astype(BF16)
        for p in range(PAIRS):
            qu[p, r : r + CH, :] = u[:, 128 * p : 128 * p + 128]
            qv[p, r : r + CH, :] = v[:, 128 * p : 128 * p + 128]
    x = mm(normed[...], weight(w, 80, 16)).astype(BF16)
    for p in range(PAIRS):
        keys[p] = x[:, 128 * p : 128 * p + 128]
    x = mm(normed[...], weight(w, 96, 16)).astype(BF16)
    for p in range(PAIRS):
        vals[p] = x[:, 128 * p : 128 * p + 128]
    x = weight(w, 112, 16)
    for p in range(PAIRS):
        w_pos[p] = x[:, 128 * p : 128 * p + 128]

    @pl.loop(0, PAIRS)
    def _(p):
        kcat[:, rows : rows + 128] = keys[p]
        for s in range(2):
            half = lane_half((rows, 128), s)
            zero = jnp.zeros((rows, 128), BF16)
            proj[...] = mm(jnp.where(half, qv[p], zero), w_pos[p], 1, 1)
            for r in range(0, rows, CH):
                a = proj[r : r + CH, 0:256]
                b = proj[r : r + CH, 256:512]
                si = sine[r : r + CH, :]
                co = cosine[r : r + CH, :]
                qcat[r : r + CH, 0:256] = (a * si + b * co).astype(BF16)
                qcat[r : r + CH, 256:512] = (b * si - a * co).astype(BF16)
            qcat[:, 512:640] = jnp.where(half, qu[p], zero)
            for q in range(rows // QBLK):
                first, stop = q * QBLK, (q + 1) * QBLK
                tmp[0:QBLK, 0:stop] = mm(qcat[first:stop, :], kcat[0:stop, :], 1, 1)
                for r in range(0, QBLK, CH):
                    x = tmp[r : r + CH, 0:stop] * (DH ** (-0.5)) + bias[
                        first + r : first + r + CH, 0:stop
                    ]
                    e = jnp.exp(x - jnp.max(x, axis=-1, keepdims=True))
                    inv = 1.0 / jnp.sum(e, axis=-1, keepdims=True)
                    prob[2 * p + s, first + r : first + r + CH, 0:stop] = (e * inv).astype(BF16)
                out = mm(prob[2 * p + s, first:stop, 0:stop], vals[p, 0:stop, :]).astype(BF16)
                if s == 0:
                    ctx[p, first:stop, :] = out
                else:
                    ctx[p, first:stop, :] = jnp.where(
                        lane_half((QBLK, 128), 1), out, ctx[p, first:stop, :]
                    )

    keep.wait()


def join(ref):
    return jnp.concatenate([ref[p] for p in range(PAIRS)], axis=1)


def store_blocks(grads, place, grad, first, rows=16, start=0):
    for k in range(grad.shape[0] // rows):
        grads[place[start + k], first : first + rows, :] = grad[k * rows : (k + 1) * rows].astype(BF16)


def middle_kernel(plan, n_pieces, me_ref, place_ref, *refs):
    pieces = refs[:n_pieces]
    (pooled, ctx, up_grad, vecs) = refs[n_pieces : n_pieces + 4]
    (res_grad, cg, short_out, vec_grads, w_up_hbm, keep_hbm, send_hbm) = refs[
        n_pieces + 4 : n_pieces + 11
    ]
    (w, grads, xhat, rstd, n2, hidden, slope, acc, tmp, sgrad, bg, sem, sem2) = refs[n_pieces + 11 :]
    me = me_ref[0]
    rows = pooled.shape[0]
    load_pieces(me, plan, pieces, w, sem)
    wait_whole(w, sem)
    keep_up = pltpu.make_async_copy(w.at[:, 80:128], w_up_hbm, sem2.at[0])
    keep_up.start()
    gain2, bias2 = vecs[5:6, :], vecs[6:7, :]
    acc[...] = pooled[...] + mm(join(ctx), weight(w, 0, 16))
    for r in range(0, rows, CH):
        xh, rs = norm_stats(acc[r : r + CH, :])
        xhat[r : r + CH, :] = xh
        rstd[r : r + CH, :] = jnp.broadcast_to(rs, (CH, 128))
        n2[r : r + CH, :] = (xh * gain2 + bias2).astype(BF16)
    for j in range(4):
        tmp[...] = mm(n2[...], weight(w, 16 + 16 * j, 16))
        b1 = vecs[8 + j : 9 + j, :]
        for r in range(0, rows, CH):
            x = tmp[r : r + CH, :] + b1
            x2 = x * x
            t = jnp.tanh(GELU_C * (x + 0.044715 * (x * x2)))
            hidden[j, r : r + CH, :] = (0.5 * x * (1.0 + t)).astype(BF16)
            slope[j, r : r + CH, :] = 0.5 * (1.0 + t) + (0.5 * GELU_C) * x * (1.0 - t * t) * (
                1.0 + (3.0 * 0.044715) * x2
            )
        acc[...] += mm(hidden[j], weight_ff2(w, 128, j))
    b2 = vecs[7:8, :]
    for r in range(0, rows, CH):
        short_out[r : r + CH, :] = (acc[r : r + CH, :] + b2).astype(BF16)
    sgrad[...] = (
        mm(up_grad[:, 0:512], weight(w, 80, 16), 1, 1)
        + mm(up_grad[:, 512:1024], weight(w, 96, 16), 1, 1)
        + mm(up_grad[:, 1024:1536], weight(w, 112, 16), 1, 1)
    )
    bg[...] = sgrad[...].astype(BF16)
    store_blocks(grads, place_ref, mm(short_out[...], up_grad[:, 0:512], 0, 0), 80)
    store_blocks(grads, place_ref, mm(short_out[...], up_grad[:, 512:1024], 0, 0), 96)
    store_blocks(grads, place_ref, mm(short_out[...], up_grad[:, 1024:1536], 0, 0), 112)
    vec_grads[...] = jnp.zeros(vec_grads.shape, F32)
    for j in range(3):
        vec_grads[12 + j : 13 + j, :] = jnp.sum(
            up_grad[:, 512 * j : 512 * j + 512].astype(F32), axis=0, keepdims=True
        )
    vec_grads[7:8, :] = jnp.sum(bg[...].astype(F32), axis=0, keepdims=True)
    for j in range(4):
        store_blocks(grads, place_ref, mm(hidden[j], bg[...], 0, 0), 128, 64, 8 * j)
        tmp[...] = mm(bg[...], weight_ff2(w, 128, j), 1, 1)
        total = jnp.zeros((1, 512), F32)
        for r in range(0, rows, CH):
            x = (tmp[r : r + CH, :] * slope[j, r : r + CH, :]).astype(BF16)
            hidden[j, r : r + CH, :] = x
            total = total + jnp.sum(x.astype(F32), axis=0, keepdims=True)
        vec_grads[8 + j : 9 + j, :] = total
        store_blocks(grads, place_ref, mm(n2[...], hidden[j], 0, 0), 16 + 16 * j)
        back = mm(hidden[j], weight(w, 16 + 16 * j, 16), 1, 1)
        if j == 0:
            acc[...] = back
        else:
            acc[...] += back
    dgain = jnp.zeros((1, 512), F32)
    dbias = jnp.zeros((1, 512), F32)
    for r in range(0, rows, CH):
        dy = acc[r : r + CH, :]
        xh = xhat[r : r + CH, :]
        dgain = dgain + jnp.sum(dy * xh, axis=0, keepdims=True)
        dbias = dbias + jnp.sum(dy, axis=0, keepdims=True)
        x = sgrad[r : r + CH, :] + norm_back(dy, xh, rstd[r : r + CH, 0:1], gain2)
        res_grad[r : r + CH, :] = x
        bg[r : r + CH, :] = x.astype(BF16)
    vec_grads[5:6, :] = dgain
    vec_grads[6:7, :] = dbias
    store_blocks(grads, place_ref, mm(join(ctx), bg[...], 0, 0), 0)
    out_keep = pltpu.make_async_copy(grads.at[0 : BLOCKS // 2], keep_hbm, sem2.at[1])
    out_send = pltpu.make_async_copy(grads.at[BLOCKS // 2 : BLOCKS], send_hbm, sem2.at[2])
    out_send.start()
    out_keep.start()
    x = mm(bg[...], weight(w, 0, 16), 1, 1).astype(BF16)
    for p in range(PAIRS):
        cg[p] = x[:, 128 * p : 128 * p + 128]
    keep_up.wait()
    out_send.wait()
    out_keep.wait()


def tail_kernel(
    place_ref, prob, cg, vals, keys, qu, qv, key_pos, sine, cosine, normed, grouped, pooled, res_grad, vecs, vec_in, w_hbm,
    pg, w_pool_out, keep_hbm, send_hbm,
    w_pos, pgrad, sg, posg, qg, qkvg, pos_w_grad, w, grads, acc, vec, prob_v, sem, prob_sem,
):
    rows = key_pos.shape[0]
    n_q = rows // QBLK
    load = pltpu.make_async_copy(w_hbm, w, sem.at[0])
    load.start()

    def fetch(p):
        return pltpu.make_async_copy(prob.at[pl.ds(2 * p, 2)], prob_v.at[p % 2], prob_sem.at[p % 2])

    fetch(0).start()
    vec[...] = vec_in[...]
    load.wait()
    x = weight(w, 112, 16)
    for p in range(PAIRS):
        w_pos[p] = x[:, 128 * p : 128 * p + 128]

    @pl.loop(0, PAIRS)
    def _(p):
        @pl.when(p + 1 < PAIRS)
        def _():
            fetch(p + 1).start()

        fetch(p).wait()
        slot = p % 2
        u_sums = []
        v_sums = []
        for s in range(2):
            half = lane_half((rows, 128), s)
            zero = jnp.zeros((rows, 128), BF16)
            cgm = jnp.where(half, cg[p], zero)
            qum = jnp.where(half, qu[p], zero)
            qvm = jnp.where(half, qv[p], zero)
            for q in range(n_q):
                first, stop = q * QBLK, (q + 1) * QBLK
                pgrad[first:stop, 0:stop] = mm(cgm[first:stop], vals[p, 0:stop, :], 1, 1)
                for r in range(first, stop, CH):
                    pr = prob_v[slot, s, r : r + CH, 0:stop].astype(F32)
                    t = pr * pgrad[r : r + CH, 0:stop]
                    inner = jnp.sum(t, axis=-1, keepdims=True)
                    sg[r : r + CH, 0:stop] = ((t - pr * inner) * (DH ** (-0.5))).astype(BF16)
                posg[first:stop, :] = mm(sg[first:stop, 0:stop], key_pos[0:stop, :])
                part = mm(sg[first:stop, 0:stop], keys[p, 0:stop, :])
                if s == 0:
                    qg[p, first:stop, :] = part
                else:
                    qg[p, first:stop, :] = jnp.where(
                        lane_half((QBLK, 128), 1), part, qg[p, first:stop, :]
                    )
                kg = mm(sg[first:stop, 0:stop], qum[first:stop], 0, 0)
                vg = mm(prob_v[slot, s, first:stop, 0:stop], cgm[first:stop], 0, 0)
                if s == 0 and q == 0:
                    qg[PAIRS + p] = jnp.zeros((rows, 128), F32)
                    qg[2 * PAIRS + p] = jnp.zeros((rows, 128), F32)
                qg[PAIRS + p, 0:stop, :] += kg
                qg[2 * PAIRS + p, 0:stop, :] += vg
            for r in range(0, rows, CH):
                a = posg[r : r + CH, 0:256]
                b = posg[r : r + CH, 256:512]
                si = sine[r : r + CH, :]
                co = cosine[r : r + CH, :]
                sg[r : r + CH, 0:256] = (a * si - b * co).astype(BF16)
                sg[r : r + CH, 256:512] = (a * co + b * si).astype(BF16)
            gw = mm(sg[...], qvm, 0, 0)
            if s == 0:
                pos_w_grad[p] = gw
            else:
                pos_w_grad[p] += gw
            qvg = jnp.where(half, mm(sg[...], w_pos[p]), 0.0)
            v_sums.append(jnp.sum(qvg, axis=0, keepdims=True))
            u_sums.append(jnp.sum(jnp.where(half, qg[p], 0.0), axis=0, keepdims=True))
            qg[p] += qvg
        u_row = u_sums[0] + u_sums[1]
        v_row = v_sums[0] + v_sums[1]
        for k in range(PAIRS):

            @pl.when(p == k)
            def _():
                vec[3:4, 128 * k : 128 * k + 128] = u_row
                vec[4:5, 128 * k : 128 * k + 128] = v_row

    for j in range(3):
        for p in range(PAIRS):
            qkvg[j, :, 128 * p : 128 * p + 128] = qg[PAIRS * j + p].astype(BF16)
    for j in range(3):
        store_blocks(grads, place_ref, mm(normed[...], qkvg[j], 0, 0), 64 + 16 * j)
    store_blocks(grads, place_ref, join(pos_w_grad), 112)
    keep_pool = pltpu.make_async_copy(w.at[:, 0:48], w_pool_out, sem.at[1])
    keep_pool.start()
    acc[...] = (
        mm(qkvg[0], weight(w, 64, 16), 1, 1)
        + mm(qkvg[1], weight(w, 80, 16), 1, 1)
        + mm(qkvg[2], weight(w, 96, 16), 1, 1)
    )
    gain1 = vecs[1:2, :]
    dgain = jnp.zeros((1, 512), F32)
    dbias = jnp.zeros((1, 512), F32)
    dpool = jnp.zeros((1, 512), F32)
    for r in range(0, rows, CH):
        dy = acc[r : r + CH, :]
        xh, rs = norm_stats(pooled[r : r + CH, :])
        dgain = dgain + jnp.sum(dy * xh, axis=0, keepdims=True)
        dbias = dbias + jnp.sum(dy, axis=0, keepdims=True)
        x = (res_grad[r : r + CH, :] + norm_back(dy, xh, rs, gain1)).astype(BF16)
        pg[r : r + CH, :] = x
        dpool = dpool + jnp.sum(x.astype(F32), axis=0, keepdims=True)
    vec[0:1, :] = dpool
    vec[1:2, :] = dgain
    vec[2:3, :] = dbias
    table = vec[...].astype(BF16)
    for d in range(BLOCKS):
        grads[place_ref[d], VEC, :] = table
    for j in range(3):
        g = mm(grouped[:, 512 * j : 512 * j + 512], pg[...], 0, 0)
        for k in range(32):
            granule = 32 * j + k
            d, sub = granule // 3, granule % 3
            grads[place_ref[d], 16 * sub : 16 * sub + 16, :] = g[16 * k : 16 * k + 16].astype(BF16)
    out_send = pltpu.make_async_copy(grads.at[BLOCKS // 2 : BLOCKS], send_hbm, sem.at[2])
    out_keep = pltpu.make_async_copy(grads.at[0 : BLOCKS // 2], keep_hbm, sem.at[3])
    out_send.start()
    out_keep.start()
    keep_pool.wait()
    out_send.wait()
    out_keep.wait()


def bytes_kernel(emb, cot, cols, short_out, w_up, vecs, pg, w_pool, out, grad, tmp):
    rows = emb.shape[0]
    for j in range(3):
        tmp[...] = mm(short_out[...], weight(w_up, 16 * j, 16))
        up_bias = vecs[12 + j : 13 + j, :]
        for r in range(0, rows, CH):
            x = emb[r : r + CH, 512 * j : 512 * j + 512].astype(F32) + tmp[r : r + CH, :] + up_bias
            out[r : r + CH, 512 * j : 512 * j + 512] = jnp.where(
                cols[r : r + CH, j : j + 1] > 0, x, 0.0
            ).astype(BF16)
    pool = weight(w_pool, 0, 48)
    for j in range(3):
        src = (j + 2) % 3
        tmp[...] = mm(pg[...], pool[512 * src : 512 * src + 512, :], 1, 1)
        if j > 0:
            tmp[...] = pltpu.roll(tmp[...], rows - 1, 0)
        for r in range(0, rows, CH):
            x = tmp[r : r + CH, :]
            if j > 0:
                x = jnp.where(cols[r : r + CH, 3:4] > 0, x, 0.0)
            x = cot[r : r + CH, 512 * j : 512 * j + 512].astype(F32) + x
            grad[r : r + CH, 512 * j : 512 * j + 512] = jnp.where(
                cols[r : r + CH, j : j + 1] > 0, x, 0.0
            ).astype(BF16)


def pack_kernel(me_ref, *refs):
    (w_pool, w_qkv, w_pos, w_out, w_ff1, w_ff2, w_up) = refs[:7]
    vectors = refs[7:17]
    out_a, out_b = refs[17:]
    me = me_ref[0]
    out_a[0:48, :] = w_pool[...]
    for j in range(3):
        out_a[64 + 16 * j : 80 + 16 * j, :] = w_qkv[:, 512 * j : 512 * j + 512]
        out_b[80 + 16 * j : 96 + 16 * j, :] = w_up[:, 512 * j : 512 * j + 512]
    out_a[112:128, :] = w_pos[...]
    out_b[0:16, :] = w_out[...]
    for j in range(4):
        out_b[16 + 16 * j : 32 + 16 * j, :] = w_ff1[:, 512 * j : 512 * j + 512]
    out_b[128:192, :] = w_ff2[...]

    def spread(x, first):
        k = x.shape[1]
        lane = first + lax.broadcasted_iota(jnp.int32, (k, 512), 1)
        row = lax.broadcasted_iota(jnp.int32, (k, 512), 0)
        pick = jnp.where(lane % k == row, 1.0, 0.0).astype(BF16)
        own = (first + lax.broadcasted_iota(jnp.int32, (x.shape[0], 512), 1)) // k == me
        return jnp.where(own, mm(x, pick), 0.0)

    lines = [spread(v[...], 0) for v in vectors[:8]]
    lines += [spread(vectors[8][...], 512 * j) for j in range(4)]
    lines += [spread(vectors[9][...], 512 * j) for j in range(3)]
    lines.append(jnp.zeros((1, 512), F32))
    out_a[VEC, :] = jnp.concatenate(lines, axis=0).astype(BF16)


class Links:
    def __init__(self, dp, fsdp):
        self.dp = dp
        self.fsdp = fsdp
        self.count = dp * fsdp
        self.near = [2 * m for m in range(fsdp // 2)]

    def send(self, values, mask):
        return lax.ppermute(values, AXES, [(i, i ^ mask) for i in range(self.count)])

    def deep(self, blocks):
        return lax.all_to_all(blocks, "dp", 0, 0, tiled=True)

    def gather_deep(self, shard):
        return self.deep(jnp.broadcast_to(shard[None], (self.dp,) + shard.shape))

    def gather_near(self, held):
        return [held] + [self.send(held, m) for m in self.near[1:]]

    def gather_core(self, pieces):
        outs = list(zip(self.near, pieces))
        return outs + [(m ^ 1, self.send(p, 1)) for m, p in outs]

    def places(self, me):
        owner = jnp.arange(self.count, dtype=jnp.int32)
        differ = (owner ^ me) % self.fsdp
        return ((differ % 2) * (self.fsdp // 2) + differ // 2) * self.dp + owner // self.fsdp

    def total_core(self, keep, got):
        n = self.dp
        outs = []
        for k in range(len(self.near)):
            total = add(keep[k * n : k * n + n], got[k * n : k * n + n])
            outs.append(total if k == 0 else total.astype(BF16))
        return outs

    def start_near(self, totals):
        return totals[:1] + [self.send(t, m) for t, m in zip(totals[1:], self.near[1:])]

    def total_near(self, parts):
        total = parts[0]
        for x in parts[1:]:
            total = total + x.astype(F32)
        return total.astype(BF16)

    def total_deep(self, parts):
        return jnp.sum(parts.astype(F32), axis=0)

    def reduce(self, keep, send):
        near = self.start_near(self.total_core(keep, self.send(send, 1)))
        return self.total_deep(self.deep(self.total_near(near)))


def add(left, right):
    return left.astype(F32) + right.astype(F32)


def cost(us):
    return pl.CostEstimate(flops=us * 10**9, transcendentals=0, bytes_accessed=us * 10**6)


def add(left, right):
    return left.astype(F32) + right.astype(F32)


def fold(shard, width):
    return jnp.concatenate(
        [shard[..., j : j + width] for j in range(0, shard.shape[-1], width)], axis=-2
    )


def unfold(block, count):
    rows = block.shape[-2] // count
    return jnp.concatenate(
        [block[..., j * rows : (j + 1) * rows, :] for j in range(count)], axis=-1
    )


def reblock(blocks, layout, count):
    m = blocks.shape[0]
    outs = []
    for first, rows, k in layout:
        x = unfold(blocks[:, first : first + rows], k)
        x = x.reshape(m * x.shape[1], x.shape[2]).reshape(count, -1, x.shape[2])
        outs.append(fold(x, blocks.shape[2]))
    return jnp.concatenate(outs, axis=1)


def layout_of(parts):
    out = []
    first = 0
    for rows, k in parts:
        out.append((first, rows, k))
        first += rows
    return out


def per_device(links, *args):
    (
        byte_embeddings,
        byte_item,
        byte_mask,
        w_pool,
        b_pool,
        ln1_gain,
        ln1_bias,
        w_qkv,
        pos_u,
        pos_v,
        w_pos,
        w_out,
        ln2_gain,
        ln2_bias,
        w_ff1,
        b_ff1,
        w_ff2,
        b_ff2,
        w_up,
        b_up,
        cotangent,
    ) = args
    n_dev = links.count
    me = lax.axis_index(AXES).astype(jnp.int32)
    width = w_pos.shape[1]
    r_pool, r, r_ff2 = w_pool.shape[0], w_pos.shape[0], w_ff2.shape[0]
    direct = n_dev == BLOCKS
    vectors = [b_pool, ln1_gain, ln1_bias, pos_u, pos_v, ln2_gain, ln2_bias, b_ff2, b_ff1, b_up]
    lengths = [v.shape[0] for v in vectors]
    vec_rows = [v * n_dev // width for v in lengths]
    vec_first = [sum(vec_rows[:i]) for i in range(len(vec_rows))]

    params = pltpu.CompilerParams(vmem_limit_bytes=60 << 20)
    sds = jax.ShapeDtypeStruct
    if direct:
        shard_a, shard_b = pl.pallas_call(
            pack_kernel,
            out_shape=(sds((ROWS_A, width), BF16), sds((ROWS_B, width), BF16)),
            in_specs=[SMEM] + [VMEM] * 17,
            out_specs=[VMEM] * 2,
            compiler_params=params,
            cost_estimate=cost(3),
        name="pack",
        )(me[None], w_pool, w_qkv, w_pos, w_out, w_ff1, w_ff2, w_up, *[v[None] for v in vectors])
    else:
        flat = jnp.arange(n_dev * lengths[8])
        table = []
        for v in vectors:
            k = v.shape[0]
            spread = jnp.where(flat[: n_dev * k] // k == me, jnp.tile(v, n_dev), jnp.zeros((), v.dtype))
            table.append(spread.reshape(-1, width))
        table.append(jnp.zeros((16 - sum(vec_rows), width), BF16))
        shard_a = jnp.concatenate([w_pool] + table + [fold(w_qkv, width), w_pos], axis=0)
        shard_b = jnp.concatenate([w_out, fold(w_ff1, width), fold(w_up, width), w_ff2], axis=0)
    split_a = r_pool + 16
    held_a = links.gather_deep(shard_a)
    shard_b, held_a = lax.optimization_barrier((shard_b, held_a))
    held_b = links.gather_deep(shard_b)
    pieces_a = links.gather_core(links.gather_near(held_a))
    layout_a = layout_of([(r_pool, 1), (16, 0), (3 * r, 3), (r, 1)])
    layout_b = layout_of([(r, 1), (4 * r, 4), (3 * r, 3), (r_ff2, 1)])
    layout_a32 = layout_of([(48, 1), (16, 0), (48, 3), (16, 1)])
    layout_b32 = layout_of([(16, 1), (64, 4), (48, 3), (64, 1)])

    if direct:
        base = (me % links.fsdp)[None]
        place = links.places(me)
    else:

        def canonical(pieces, layout):
            masks = [m for m, _ in pieces]
            arr = jnp.stack([a for _, a in pieces])
            inverse = jnp.array([masks.index(m) for m in range(links.fsdp)])
            arr = jnp.take(arr, inverse[jnp.arange(links.fsdp) ^ (me % links.fsdp)], axis=0)
            blocks = jnp.swapaxes(arr, 0, 1).reshape((n_dev,) + arr.shape[2:])
            outs = []
            for first, rows_, k in layout:
                if k == 0:
                    total = jnp.sum(blocks[:, first : first + rows_].astype(F32), axis=0)
                    outs.append(
                        jnp.concatenate(
                            [total[None], jnp.zeros((BLOCKS - 1,) + total.shape, F32)], axis=0
                        ).astype(BF16)
                    )
                else:
                    outs.append(reblock(blocks, [(first, rows_, k)], BLOCKS))
            return [(0, jnp.concatenate(outs, axis=1))]

        pieces_a = canonical(pieces_a, layout_a)
        base = jnp.zeros((1,), jnp.int32)
        place = jnp.arange(BLOCKS, dtype=jnp.int32)

    byte_total = byte_embeddings.shape[0]
    rows = byte_total // 3
    emb = byte_embeddings.reshape(rows, 3 * width)
    cot = cotangent.reshape(rows, 3 * width)
    mask3 = byte_mask.reshape(rows, 3)
    item = byte_item.reshape(rows, 3)[:, 0]
    same = item[1:] == item[:-1]
    no = jnp.zeros((1,), jnp.bool_)
    same_before = jnp.concatenate([no, same])[:, None]
    same_after = jnp.concatenate([same, no])[:, None]
    cols = jnp.concatenate([mask3, same_after.astype(jnp.int32)], axis=1)
    item_f = item.astype(F32)
    live = [mask3[:, j : j + 1] > 0 for j in range(3)]
    zero = jnp.zeros((), jnp.bfloat16)
    masked = [jnp.where(live[j], emb[:, j * width : (j + 1) * width], zero) for j in range(3)]
    up_grad = jnp.concatenate(
        [jnp.where(live[j], cot[:, j * width : (j + 1) * width], zero) for j in range(3)], axis=1
    )

    def down(x):
        moved = jnp.concatenate([jnp.zeros((1, width), x.dtype), x[:-1]], axis=0)
        return jnp.where(same_before, moved, zero)

    grouped = jnp.concatenate([down(masked[1]), down(masked[2]), masked[0]], axis=1)
    places = jnp.arange(rows).astype(F32)
    frequency = 10000.0 ** (-(2.0 * jnp.arange(width // 2).astype(F32)) / width)
    angles = places[:, None] * frequency[None, :]
    sine, cosine = jnp.sin(angles), jnp.cos(angles)
    key_pos = jnp.concatenate([cosine, sine], axis=1).astype(BF16)

    grouped, held_b = lax.optimization_barrier((grouped, held_b))
    near_b = links.gather_near(held_b)
    pair_bf = sds((PAIRS, rows, 128), BF16)
    pair_f = sds((PAIRS, rows, 128), F32)
    square = sds((rows, width), F32)
    table_f = sds((16, width), F32)

    step = links.fsdp if direct else 1
    plan_a = [(m, step) for m, _ in pieces_a]
    n_a = len(plan_a)
    forward = pl.pallas_call(
        lambda *refs: forward_kernel(plan_a, n_a, *refs),
        out_shape=(
            square,
            sds((rows, width), BF16),
            pair_bf,
            pair_bf,
            pair_bf,
            pair_bf,
            sds((H, rows, rows), BF16),
            pair_bf,
            table_f,
            sds((BLOCKS, ROWS_A, width), BF16),
        ),
        in_specs=[SMEM] + [ANY] * n_a + [VMEM] * 6,
        out_specs=[VMEM] * 9 + [ANY],
        scratch_shapes=[
            pltpu.VMEM((BLOCKS, ROWS_A, width), BF16),
            pltpu.VMEM((PAIRS, width, 128), BF16),
            pltpu.VMEM((rows, rows), F32),
            pltpu.VMEM((rows, width), F32),
            pltpu.VMEM((rows, width + 128), BF16),
            pltpu.VMEM((rows, width + 128), BF16),
            pltpu.VMEM((rows, width), F32),
            pltpu.SemaphoreType.DMA,
            pltpu.SemaphoreType.DMA,
        ],
        compiler_params=params,
        cost_estimate=cost(20),
        name="forward",
    )
    pooled, normed, qu, qv, keys, vals, prob, ctx, vecs, wa = forward(base, *[a for _, a in pieces_a], grouped, item_f[:, None], item_f[None, :], sine, cosine, key_pos)
    pooled, near_b = lax.optimization_barrier((pooled, near_b))
    pieces_b = links.gather_core(near_b)
    if not direct:
        pieces_b = canonical(pieces_b, layout_b)


    plan_b = [(m, step) for m, _ in pieces_b]
    n_b = len(plan_b)
    half = BLOCKS // 2
    res_grad, cg, short_out, vec_grads, w_up_abs, keep_b, send_b = pl.pallas_call(
        lambda *refs: middle_kernel(plan_b, n_b, *refs),
        out_shape=(
            square,
            pair_bf,
            sds((rows, width), BF16),
            table_f,
            sds((BLOCKS, 48, width), BF16),
            sds((half, ROWS_B, width), BF16),
            sds((half, ROWS_B, width), BF16),
        ),
        in_specs=[SMEM, SMEM] + [ANY] * n_b + [VMEM] * 4,
        out_specs=[VMEM] * 4 + [ANY] * 3,
        scratch_shapes=[
            pltpu.VMEM((BLOCKS, ROWS_B, width), BF16),
            pltpu.VMEM((BLOCKS, ROWS_B, width), BF16),
            pltpu.VMEM((rows, width), F32),
            pltpu.VMEM((rows, 128), F32),
            pltpu.VMEM((rows, width), BF16),
            pltpu.VMEM((4, rows, 512), BF16),
            pltpu.VMEM((4, rows, 512), F32),
            pltpu.VMEM((rows, width), F32),
            pltpu.VMEM((rows, width), F32),
            pltpu.VMEM((rows, width), F32),
            pltpu.VMEM((rows, width), BF16),
            pltpu.SemaphoreType.DMA,
            pltpu.SemaphoreType.DMA((3,)),
        ],
        compiler_params=params,
        cost_estimate=cost(20),
        name="middle",
    )(base, place, *[a for _, a in pieces_b], pooled, ctx, up_grad, vecs)

    if direct:
        got_b = links.send(send_b, 1)
        totals_b = links.total_core(keep_b, got_b)
        cg, totals_b = lax.optimization_barrier((cg, totals_b))
        near_sums_b = links.start_near(totals_b)

    pooled_grad, w_pool_abs, keep_a, send_a = pl.pallas_call(
        tail_kernel,
        out_shape=(
            sds((rows, width), BF16),
            sds((BLOCKS, 48, width), BF16),
            sds((half, ROWS_A, width), BF16),
            sds((half, ROWS_A, width), BF16),
        ),
        in_specs=[SMEM, ANY] + [VMEM] * 14 + [ANY],
        out_specs=[VMEM] + [ANY] * 3,
        scratch_shapes=[
            pltpu.VMEM((PAIRS, width, 128), BF16),
            pltpu.VMEM((rows, width), F32),
            pltpu.VMEM((rows, rows), BF16),
            pltpu.VMEM((rows, width), F32),
            pltpu.VMEM((3 * PAIRS, rows, 128), F32),
            pltpu.VMEM((3, rows, width), BF16),
            pltpu.VMEM((PAIRS, width, 128), F32),
            pltpu.VMEM((BLOCKS, ROWS_A, width), BF16),
            pltpu.VMEM((BLOCKS, ROWS_A, width), BF16),
            pltpu.VMEM((rows, width), F32),
            pltpu.VMEM((16, width), F32),
            pltpu.VMEM((2, 2, rows, rows), BF16),
            pltpu.SemaphoreType.DMA((4,)),
            pltpu.SemaphoreType.DMA((2,)),
        ],
        compiler_params=params,
        cost_estimate=cost(27),
        name="tail",
    )(
        place, prob, cg, vals, keys, qu, qv, key_pos, sine, cosine, normed, grouped, pooled, res_grad, vecs,
        vec_grads, wa,
    )
    if direct:
        pooled_grad, send_a, near_sums_b = lax.optimization_barrier((pooled_grad, send_a, near_sums_b))
        got_a = links.send(send_a, 1)
        deep_b = links.deep(links.total_near(near_sums_b))
        near_sums_a = links.start_near(links.total_core(keep_a, got_a))

    out3, grad3 = pl.pallas_call(
        bytes_kernel,
        out_shape=(sds((rows, 3 * width), BF16), sds((rows, 3 * width), BF16)),
        in_specs=[VMEM] * 8,
        out_specs=[VMEM] * 2,
        scratch_shapes=[pltpu.VMEM((rows, width), F32)],
        compiler_params=params,
        cost_estimate=cost(7),
        name="bytes",
    )(emb, cot, cols, short_out, w_up_abs, vecs, pooled_grad, w_pool_abs)
    block_output = out3.reshape(byte_total, width)
    input_grad = grad3.reshape(byte_total, width)

    if direct:
        sum_b = links.total_deep(deep_b)
        sum_a = links.total_deep(links.deep(links.total_near(near_sums_a)))
    else:

        def owned(keep, send, layout):
            blocks = jnp.concatenate([keep, send], axis=0)
            outs = []
            for first, rows_, k in layout:
                if k == 0:
                    outs.append(jnp.tile(blocks[:1, first : first + rows_], (n_dev, 1, 1)))
                else:
                    outs.append(reblock(blocks, [(first, rows_, k)], n_dev))
            full = jnp.concatenate(outs, axis=1)
            full = jnp.zeros_like(full).at[links.places(me)].set(full)
            return links.reduce(full[: n_dev // 2], full[n_dev // 2 :])

        sum_b = owned(keep_b, send_b, layout_b32)
        sum_a = owned(keep_a, send_a, layout_a32)
    vec_sum = sum_a[r_pool : r_pool + 16]
    vec_out = []
    for first, k, n in zip(vec_first, lengths, vec_rows):
        line = vec_sum[first : first + n].reshape(-1)
        vec_out.append(lax.dynamic_slice(line, (me * k,), (k,)))
    (
        out_pool_b,
        out_ln1_gain,
        out_ln1_bias,
        out_u,
        out_v,
        out_ln2_gain,
        out_ln2_bias,
        out_ff2_b,
        out_ff1_b,
        out_up_b,
    ) = vec_out
    return (
        block_output,
        input_grad,
        sum_a[:r_pool],
        out_pool_b,
        out_ln1_gain,
        out_ln1_bias,
        unfold(sum_a[split_a : split_a + 3 * r], 3),
        out_u,
        out_v,
        sum_a[split_a + 3 * r :],
        sum_b[:r],
        out_ln2_gain,
        out_ln2_bias,
        unfold(sum_b[r : 5 * r], 4),
        out_ff1_b,
        sum_b[8 * r :],
        out_ff2_b,
        unfold(sum_b[5 * r : 8 * r], 3),
        out_up_b,
    )


def solution(mesh):
    links = Links(mesh.shape["dp"], mesh.shape["fsdp"])
    rows = P(AXES, None)
    flat = P(AXES)
    ranks = (2, 1, 1, 2, 1, 1, 1, 2, 1, 1, 2, 2, 1, 1, 2, 1, 2, 1, 2, 1, 2)
    out_ranks = (2, 2, 2, 1, 1, 1, 2, 1, 1, 2, 2, 1, 1, 2, 1, 2, 1, 2, 1)
    return jax.shard_map(
        lambda *args: per_device(links, *args),
        mesh=mesh,
        in_specs=tuple(rows if k == 2 else flat for k in ranks),
        out_specs=tuple(rows if k == 2 else flat for k in out_ranks),
        check_vma=False,
    )
```

```python
import jax
import jax.numpy as jnp
from jax import lax
from jax.experimental import pallas as pl
from jax.experimental.pallas import tpu as pltpu
from jax.sharding import PartitionSpec as P

H = 8
DH = 64
QBLK = 256
AXES = ("dp", "fsdp")


eps_norm = 1e-05
big_negative = -1e30

F32 = jnp.float32
BF16 = jnp.bfloat16
BLOCKS = 32
PAIRS = 4
SENDS_B = 1
CH = 64
VMEM = pl.BlockSpec(memory_space=pltpu.VMEM)
SMEM = pl.BlockSpec(memory_space=pltpu.SMEM)
ANY = pl.BlockSpec(memory_space=pl.ANY)
GELU_C = 0.7978845608028654
ROWS_A = 128
ROWS_B = 192
ROWS_C = 48
VEC = slice(48, 64)


def mm(left, right, cl=1, cr=0):
    return lax.dot_general(left, right, (((cl,), (cr,)), ((), ())), preferred_element_type=F32)


def weight(ref, start, rows):
    block = ref[:, start : start + rows, :]
    return block.reshape(block.shape[0] * rows, block.shape[2])


def weight_ff2(ref, start, j):
    block = ref[8 * j : 8 * j + 8, start : start + 64, :]
    return block.reshape(512, block.shape[2])


def load_pieces(me, plan, refs, dest, sem):
    copies = []
    for (first, blocks), ref in zip(plan, refs):
        for k, (base, mask) in enumerate(blocks):
            rows = pl.ds(first, ref.shape[1])
            copies.append(pltpu.make_async_copy(ref.at[k], dest.at[base + (me ^ mask), rows], sem))
    for c in copies:
        c.start()


def wait_whole(dest, sem):
    pltpu.make_async_copy(dest, dest, sem).wait()


def lane_half(shape, s):
    return (lax.broadcasted_iota(jnp.int32, shape, len(shape) - 1) // DH) == s


def norm_stats(x):
    width = x.shape[-1]
    mean = jnp.sum(x, axis=-1, keepdims=True) * (1.0 / width)
    centre = x - mean
    var = jnp.sum(centre * centre, axis=-1, keepdims=True) * (1.0 / width)
    rstd = lax.rsqrt(var + eps_norm)
    return centre * rstd, rstd


def norm_back(dy, xhat, rstd, gain):
    width = dy.shape[-1]
    d = dy * gain
    m1 = jnp.sum(d, axis=-1, keepdims=True) * (1.0 / width)
    m2 = jnp.sum(d * xhat, axis=-1, keepdims=True) * (1.0 / width)
    return rstd * (d - m1 - xhat * m2)


def forward_kernel(plan, n_pieces, me_ref, *refs):
    pieces = refs[:n_pieces]
    (grouped, item_col, item_row, sine, cosine, key_pos) = refs[n_pieces : n_pieces + 6]
    (pooled, normed, qu, qv, keys, vals, prob, ctx, vecs, w_out_hbm) = refs[
        n_pieces + 6 : n_pieces + 16
    ]
    (w, w_pos, bias, proj, qcat, kcat, tmp, sem, sem2) = refs[n_pieces + 16 :]
    me = me_ref[0]
    rows = grouped.shape[0]
    load_pieces(me, plan, pieces, w, sem)
    for r in range(0, rows, CH):
        row = r + lax.broadcasted_iota(jnp.int32, (CH, rows), 0)
        col = lax.broadcasted_iota(jnp.int32, (CH, rows), 1)
        allowed = (item_col[r : r + CH, :] == item_row[...]) & (row >= col)
        bias[r : r + CH, :] = jnp.where(allowed, 0.0, big_negative)
    kcat[:, 0:rows] = key_pos[...]
    wait_whole(w, sem)
    keep = pltpu.make_async_copy(w, w_out_hbm, sem2)
    keep.start()
    vec = jnp.sum(w[:, VEC, :].astype(F32), axis=0)
    vecs[...] = vec
    tmp[...] = mm(grouped[...], weight(w, 0, 48))
    for r in range(0, rows, CH):
        x = tmp[r : r + CH, :] + vec[0:1]
        pooled[r : r + CH, :] = x
        xhat, rstd = norm_stats(x)
        normed[r : r + CH, :] = (xhat * vec[1:2] + vec[2:3]).astype(BF16)
    tmp[...] = mm(normed[...], weight(w, 64, 16))
    for r in range(0, rows, CH):
        x = tmp[r : r + CH, :]
        u = (x + vec[3:4]).astype(BF16)
        v = (x + vec[4:5]).astype(BF16)
        for p in range(PAIRS):
            qu[p, r : r + CH, :] = u[:, 128 * p : 128 * p + 128]
            qv[p, r : r + CH, :] = v[:, 128 * p : 128 * p + 128]
    x = mm(normed[...], weight(w, 80, 16)).astype(BF16)
    for p in range(PAIRS):
        keys[p] = x[:, 128 * p : 128 * p + 128]
    x = mm(normed[...], weight(w, 96, 16)).astype(BF16)
    for p in range(PAIRS):
        vals[p] = x[:, 128 * p : 128 * p + 128]
    x = weight(w, 112, 16)
    for p in range(PAIRS):
        w_pos[p] = x[:, 128 * p : 128 * p + 128]

    @pl.loop(0, PAIRS)
    def _(p):
        kcat[:, rows : rows + 128] = keys[p]
        for s in range(2):
            half = lane_half((rows, 128), s)
            zero = jnp.zeros((rows, 128), BF16)
            proj[...] = mm(jnp.where(half, qv[p], zero), w_pos[p], 1, 1)
            for r in range(0, rows, CH):
                a = proj[r : r + CH, 0:256]
                b = proj[r : r + CH, 256:512]
                si = sine[r : r + CH, :]
                co = cosine[r : r + CH, :]
                qcat[r : r + CH, 0:256] = (a * si + b * co).astype(BF16)
                qcat[r : r + CH, 256:512] = (b * si - a * co).astype(BF16)
            qcat[:, 512:640] = jnp.where(half, qu[p], zero)
            for q in range(rows // QBLK):
                first, stop = q * QBLK, (q + 1) * QBLK
                tmp[0:QBLK, 0:stop] = mm(qcat[first:stop, :], kcat[0:stop, :], 1, 1)
                for r in range(0, QBLK, CH):
                    x = tmp[r : r + CH, 0:stop] * (DH ** (-0.5)) + bias[
                        first + r : first + r + CH, 0:stop
                    ]
                    e = jnp.exp(x - jnp.max(x, axis=-1, keepdims=True))
                    inv = 1.0 / jnp.sum(e, axis=-1, keepdims=True)
                    prob[2 * p + s, first + r : first + r + CH, 0:stop] = (e * inv).astype(BF16)
                out = mm(prob[2 * p + s, first:stop, 0:stop], vals[p, 0:stop, :]).astype(BF16)
                if s == 0:
                    ctx[p, first:stop, :] = out
                else:
                    ctx[p, first:stop, :] = jnp.where(
                        lane_half((QBLK, 128), 1), out, ctx[p, first:stop, :]
                    )

    keep.wait()


def join(ref):
    return jnp.concatenate([ref[p] for p in range(PAIRS)], axis=1)


def store_blocks(grads, place_ref, line, grad, first, rows=16, start=0):
    for k in range(grad.shape[0] // rows):
        grads[place_ref[line, start + k], first : first + rows, :] = grad[k * rows : (k + 1) * rows].astype(BF16)


def put_blocks(grads, keep_hbm, send_hbm, sem, first):
    half = BLOCKS // 2
    copies = []
    start = half
    for j, ref in enumerate(send_hbm):
        stop = start + ref.shape[0]
        copies.append(pltpu.make_async_copy(grads.at[start:stop], ref, sem.at[first + 1 + j]))
        start = stop
    copies.append(pltpu.make_async_copy(grads.at[0:half], keep_hbm, sem.at[first]))
    for c in copies:
        c.start()
    return copies


def middle_kernel(plan, n_pieces, me_ref, place_ref, *refs):
    pieces = refs[:n_pieces]
    (pooled, ctx, up_grad, vecs) = refs[n_pieces : n_pieces + 4]
    (res_grad, cg, short_out, vec_grads, w_up_hbm, keep_hbm) = refs[n_pieces + 4 : n_pieces + 10]
    send_hbm = refs[n_pieces + 10 : n_pieces + 10 + SENDS_B]
    (w, grads, xhat, rstd, n2, hidden, slope, acc, tmp, sgrad, bg, sem, sem2) = refs[
        n_pieces + 10 + SENDS_B :
    ]
    me = me_ref[0]
    rows = pooled.shape[0]
    load_pieces(me, plan, pieces, w, sem)
    wait_whole(w, sem)
    keep_up = pltpu.make_async_copy(w.at[:, 144:192], w_up_hbm, sem2.at[0])
    keep_up.start()
    gain2, bias2 = vecs[5:6, :], vecs[6:7, :]
    acc[...] = pooled[...] + mm(join(ctx), weight(w, 0, 16))
    for r in range(0, rows, CH):
        xh, rs = norm_stats(acc[r : r + CH, :])
        xhat[r : r + CH, :] = xh
        rstd[r : r + CH, :] = jnp.broadcast_to(rs, (CH, 128))
        n2[r : r + CH, :] = (xh * gain2 + bias2).astype(BF16)
    for j in range(4):
        tmp[...] = mm(n2[...], weight(w, 16 + 16 * j, 16))
        b1 = vecs[8 + j : 9 + j, :]
        for r in range(0, rows, CH):
            x = tmp[r : r + CH, :] + b1
            x2 = x * x
            t = jnp.tanh(GELU_C * (x + 0.044715 * (x * x2)))
            hidden[j, r : r + CH, :] = (0.5 * x * (1.0 + t)).astype(BF16)
            slope[j, r : r + CH, :] = 0.5 * (1.0 + t) + (0.5 * GELU_C) * x * (1.0 - t * t) * (
                1.0 + (3.0 * 0.044715) * x2
            )
        acc[...] += mm(hidden[j], weight_ff2(w, 80, j))
    b2 = vecs[7:8, :]
    for r in range(0, rows, CH):
        short_out[r : r + CH, :] = (acc[r : r + CH, :] + b2).astype(BF16)
    sgrad[...] = (
        mm(up_grad[:, 0:512], weight(w, 144, 16), 1, 1)
        + mm(up_grad[:, 512:1024], weight(w, 160, 16), 1, 1)
        + mm(up_grad[:, 1024:1536], weight(w, 176, 16), 1, 1)
    )
    bg[...] = sgrad[...].astype(BF16)
    store_blocks(grads, place_ref, 0, mm(short_out[...], up_grad[:, 0:512], 0, 0), 144)
    store_blocks(grads, place_ref, 0, mm(short_out[...], up_grad[:, 512:1024], 0, 0), 160)
    store_blocks(grads, place_ref, 0, mm(short_out[...], up_grad[:, 1024:1536], 0, 0), 176)
    vec_grads[...] = jnp.zeros(vec_grads.shape, F32)
    for j in range(3):
        vec_grads[12 + j : 13 + j, :] = jnp.sum(
            up_grad[:, 512 * j : 512 * j + 512].astype(F32), axis=0, keepdims=True
        )
    vec_grads[7:8, :] = jnp.sum(bg[...].astype(F32), axis=0, keepdims=True)
    for j in range(4):
        store_blocks(grads, place_ref, 0, mm(hidden[j], bg[...], 0, 0), 80, 64, 8 * j)
        tmp[...] = mm(bg[...], weight_ff2(w, 80, j), 1, 1)
        total = jnp.zeros((1, 512), F32)
        for r in range(0, rows, CH):
            x = (tmp[r : r + CH, :] * slope[j, r : r + CH, :]).astype(BF16)
            hidden[j, r : r + CH, :] = x
            total = total + jnp.sum(x.astype(F32), axis=0, keepdims=True)
        vec_grads[8 + j : 9 + j, :] = total
        store_blocks(grads, place_ref, 0, mm(n2[...], hidden[j], 0, 0), 16 + 16 * j)
        back = mm(hidden[j], weight(w, 16 + 16 * j, 16), 1, 1)
        if j == 0:
            acc[...] = back
        else:
            acc[...] += back
    dgain = jnp.zeros((1, 512), F32)
    dbias = jnp.zeros((1, 512), F32)
    for r in range(0, rows, CH):
        dy = acc[r : r + CH, :]
        xh = xhat[r : r + CH, :]
        dgain = dgain + jnp.sum(dy * xh, axis=0, keepdims=True)
        dbias = dbias + jnp.sum(dy, axis=0, keepdims=True)
        x = sgrad[r : r + CH, :] + norm_back(dy, xh, rstd[r : r + CH, 0:1], gain2)
        res_grad[r : r + CH, :] = x
        bg[r : r + CH, :] = x.astype(BF16)
    vec_grads[5:6, :] = dgain
    vec_grads[6:7, :] = dbias
    store_blocks(grads, place_ref, 0, mm(join(ctx), bg[...], 0, 0), 0)
    outs = put_blocks(grads, keep_hbm, send_hbm, sem2, 1)
    x = mm(bg[...], weight(w, 0, 16), 1, 1).astype(BF16)
    for p in range(PAIRS):
        cg[p] = x[:, 128 * p : 128 * p + 128]
    keep_up.wait()
    for c in outs:
        c.wait()


def tail_kernel(
    place_ref, prob, cg, vals, keys, qu, qv, key_pos, sine, cosine, normed, grouped, pooled, res_grad, vecs, vec_in, w_hbm,
    pg, w_pool_out, keep_hbm, send0, send1, send2, send3,
    w_pos, pgrad, sg, posg, qg, qkvg, pos_w_grad, w, grads, acc, vec, prob_v, sem, prob_sem,
):
    rows = key_pos.shape[0]
    n_q = rows // QBLK
    load = pltpu.make_async_copy(w_hbm, w, sem.at[0])
    load.start()

    def fetch(p):
        return pltpu.make_async_copy(prob.at[pl.ds(2 * p, 2)], prob_v.at[p % 2], prob_sem.at[p % 2])

    fetch(0).start()
    vec[...] = vec_in[...]
    load.wait()
    x = weight(w, 112, 16)
    for p in range(PAIRS):
        w_pos[p] = x[:, 128 * p : 128 * p + 128]

    @pl.loop(0, PAIRS)
    def _(p):
        @pl.when(p + 1 < PAIRS)
        def _():
            fetch(p + 1).start()

        fetch(p).wait()
        slot = p % 2
        u_sums = []
        v_sums = []
        for s in range(2):
            half = lane_half((rows, 128), s)
            zero = jnp.zeros((rows, 128), BF16)
            cgm = jnp.where(half, cg[p], zero)
            qum = jnp.where(half, qu[p], zero)
            qvm = jnp.where(half, qv[p], zero)
            for q in range(n_q):
                first, stop = q * QBLK, (q + 1) * QBLK
                pgrad[first:stop, 0:stop] = mm(cgm[first:stop], vals[p, 0:stop, :], 1, 1)
                for r in range(first, stop, CH):
                    pr = prob_v[slot, s, r : r + CH, 0:stop].astype(F32)
                    t = pr * pgrad[r : r + CH, 0:stop]
                    inner = jnp.sum(t, axis=-1, keepdims=True)
                    sg[r : r + CH, 0:stop] = ((t - pr * inner) * (DH ** (-0.5))).astype(BF16)
                posg[first:stop, :] = mm(sg[first:stop, 0:stop], key_pos[0:stop, :])
                part = mm(sg[first:stop, 0:stop], keys[p, 0:stop, :])
                if s == 0:
                    qg[p, first:stop, :] = part
                else:
                    qg[p, first:stop, :] = jnp.where(
                        lane_half((QBLK, 128), 1), part, qg[p, first:stop, :]
                    )
                kg = mm(sg[first:stop, 0:stop], qum[first:stop], 0, 0)
                vg = mm(prob_v[slot, s, first:stop, 0:stop], cgm[first:stop], 0, 0)
                if s == 0 and q == 0:
                    qg[PAIRS + p] = jnp.zeros((rows, 128), F32)
                    qg[2 * PAIRS + p] = jnp.zeros((rows, 128), F32)
                qg[PAIRS + p, 0:stop, :] += kg
                qg[2 * PAIRS + p, 0:stop, :] += vg
            for r in range(0, rows, CH):
                a = posg[r : r + CH, 0:256]
                b = posg[r : r + CH, 256:512]
                si = sine[r : r + CH, :]
                co = cosine[r : r + CH, :]
                sg[r : r + CH, 0:256] = (a * si - b * co).astype(BF16)
                sg[r : r + CH, 256:512] = (a * co + b * si).astype(BF16)
            gw = mm(sg[...], qvm, 0, 0)
            if s == 0:
                pos_w_grad[p] = gw
            else:
                pos_w_grad[p] += gw
            qvg = jnp.where(half, mm(sg[...], w_pos[p]), 0.0)
            v_sums.append(jnp.sum(qvg, axis=0, keepdims=True))
            u_sums.append(jnp.sum(jnp.where(half, qg[p], 0.0), axis=0, keepdims=True))
            qg[p] += qvg
        u_row = u_sums[0] + u_sums[1]
        v_row = v_sums[0] + v_sums[1]
        for k in range(PAIRS):

            @pl.when(p == k)
            def _():
                vec[3:4, 128 * k : 128 * k + 128] = u_row
                vec[4:5, 128 * k : 128 * k + 128] = v_row

    for j in range(3):
        for p in range(PAIRS):
            qkvg[j, :, 128 * p : 128 * p + 128] = qg[PAIRS * j + p].astype(BF16)
    for j in range(3):
        store_blocks(grads, place_ref, 1, mm(normed[...], qkvg[j], 0, 0), 64 + 16 * j)
    store_blocks(grads, place_ref, 1, join(pos_w_grad), 112)
    keep_pool = pltpu.make_async_copy(w.at[:, 0:48], w_pool_out, sem.at[1])
    keep_pool.start()
    acc[...] = (
        mm(qkvg[0], weight(w, 64, 16), 1, 1)
        + mm(qkvg[1], weight(w, 80, 16), 1, 1)
        + mm(qkvg[2], weight(w, 96, 16), 1, 1)
    )
    gain1 = vecs[1:2, :]
    dgain = jnp.zeros((1, 512), F32)
    dbias = jnp.zeros((1, 512), F32)
    dpool = jnp.zeros((1, 512), F32)
    for r in range(0, rows, CH):
        dy = acc[r : r + CH, :]
        xh, rs = norm_stats(pooled[r : r + CH, :])
        dgain = dgain + jnp.sum(dy * xh, axis=0, keepdims=True)
        dbias = dbias + jnp.sum(dy, axis=0, keepdims=True)
        x = (res_grad[r : r + CH, :] + norm_back(dy, xh, rs, gain1)).astype(BF16)
        pg[r : r + CH, :] = x
        dpool = dpool + jnp.sum(x.astype(F32), axis=0, keepdims=True)
    vec[0:1, :] = dpool
    vec[1:2, :] = dgain
    vec[2:3, :] = dbias
    table = vec[...].astype(BF16)
    for d in range(BLOCKS):
        grads[place_ref[1, d], VEC, :] = table
    for j in range(3):
        g = mm(grouped[:, 512 * j : 512 * j + 512], pg[...], 0, 0)
        for k in range(32):
            granule = 32 * j + k
            d, sub = granule // 3, granule % 3
            grads[place_ref[1, d], 16 * sub : 16 * sub + 16, :] = g[16 * k : 16 * k + 16].astype(BF16)
    outs = put_blocks(grads, keep_hbm, (send0, send1, send2, send3), sem, 2)
    keep_pool.wait()
    for c in outs:
        c.wait()


def bytes_kernel(emb, cot, cols, short_out, w_up, vecs, pg, w_pool, out, grad, tmp):
    rows = emb.shape[0]
    for j in range(3):
        tmp[...] = mm(short_out[...], weight(w_up, 16 * j, 16))
        up_bias = vecs[12 + j : 13 + j, :]
        for r in range(0, rows, CH):
            x = emb[r : r + CH, 512 * j : 512 * j + 512].astype(F32) + tmp[r : r + CH, :] + up_bias
            out[r : r + CH, 512 * j : 512 * j + 512] = jnp.where(
                cols[r : r + CH, j : j + 1] > 0, x, 0.0
            ).astype(BF16)
    pool = weight(w_pool, 0, 48)
    for j in range(3):
        src = (j + 2) % 3
        tmp[...] = mm(pg[...], pool[512 * src : 512 * src + 512, :], 1, 1)
        if j > 0:
            tmp[...] = pltpu.roll(tmp[...], rows - 1, 0)
        for r in range(0, rows, CH):
            x = tmp[r : r + CH, :]
            if j > 0:
                x = jnp.where(cols[r : r + CH, 3:4] > 0, x, 0.0)
            x = cot[r : r + CH, 512 * j : 512 * j + 512].astype(F32) + x
            grad[r : r + CH, 512 * j : 512 * j + 512] = jnp.where(
                cols[r : r + CH, j : j + 1] > 0, x, 0.0
            ).astype(BF16)


def pack_kernel(me_ref, *refs):
    (w_pool, w_qkv, w_pos, w_out, w_ff1, w_ff2, w_up) = refs[:7]
    vectors = refs[7:17]
    all_a, all_b, out_c, out_a, out_b, sem = refs[17:]
    me = me_ref[0]
    out_a[0:48, :] = w_pool[...]
    for j in range(3):
        out_a[64 + 16 * j : 80 + 16 * j, :] = w_qkv[:, 512 * j : 512 * j + 512]
        out_c[0, 16 * j : 16 + 16 * j, :] = w_up[:, 512 * j : 512 * j + 512]
    out_a[112:128, :] = w_pos[...]
    out_b[0:16, :] = w_out[...]
    for j in range(4):
        out_b[16 + 16 * j : 32 + 16 * j, :] = w_ff1[:, 512 * j : 512 * j + 512]
    out_b[80:144, :] = w_ff2[...]

    def spread(x, first):
        k = x.shape[1]
        lane = first + lax.broadcasted_iota(jnp.int32, (k, 512), 1)
        row = lax.broadcasted_iota(jnp.int32, (k, 512), 0)
        pick = jnp.where(lane % k == row, 1.0, 0.0).astype(BF16)
        own = (first + lax.broadcasted_iota(jnp.int32, (x.shape[0], 512), 1)) // k == me
        return jnp.where(own, mm(x, pick), 0.0)

    lines = [spread(v[...], 0) for v in vectors[:8]]
    lines += [spread(vectors[8][...], 512 * j) for j in range(4)]
    lines += [spread(vectors[9][...], 512 * j) for j in range(3)]
    lines.append(jnp.zeros((1, 512), F32))
    out_a[VEC, :] = jnp.concatenate(lines, axis=0).astype(BF16)
    copies = []
    for j in range(all_a.shape[0]):
        copies.append(pltpu.make_async_copy(out_a, all_a.at[j], sem.at[j]))
    for j in range(all_b.shape[0]):
        copies.append(pltpu.make_async_copy(out_b, all_b.at[j], sem.at[all_a.shape[0] + j]))
    for c in copies:
        c.start()
    for c in copies:
        c.wait()


def finish_b_kernel(parts, out, ff1, up, ff2):
    total = parts[0].astype(F32)
    for j in range(1, parts.shape[0]):
        total = total + parts[j].astype(F32)
    out[...] = total[0:16]
    for j in range(4):
        ff1[:, 512 * j : 512 * j + 512] = total[16 + 16 * j : 32 + 16 * j]
    for j in range(3):
        up[:, 512 * j : 512 * j + 512] = total[144 + 16 * j : 160 + 16 * j]
    ff2[...] = total[80:144]


def finish_a_kernel(me_ref, parts, pool, qkv, pos, *vectors):
    me = me_ref[0]
    total = parts[0].astype(F32)
    for j in range(1, parts.shape[0]):
        total = total + parts[j].astype(F32)
    pool[...] = total[0:48]
    for j in range(3):
        qkv[:, 512 * j : 512 * j + 512] = total[64 + 16 * j : 80 + 16 * j]
    pos[...] = total[112:128]
    table = total[VEC]
    lines = pltpu.roll(table[0:8], 512 - 16 * me, 1)
    for j in range(8):
        vectors[j][...] = lines[j : j + 1, 0:16]
    row = lax.broadcasted_iota(jnp.int32, (16, 512), 0)

    def line(j):
        return jnp.sum(jnp.where(row == j, table, 0.0), axis=0, keepdims=True)

    def part(first, length):
        j, off = first // 512, first % 512
        here = pltpu.roll(jnp.broadcast_to(line(j), (8, 512)), 512 - off, 1)
        there = pltpu.roll(jnp.broadcast_to(line(j + 1), (8, 512)), 512 - off, 1)
        lane = lax.broadcasted_iota(jnp.int32, (8, 512), 1)
        return jnp.where(lane < 512 - off, here, there)[0:1, 0:length]

    vectors[8][...] = part(8 * 512 + 64 * me, 64)
    vectors[9][...] = part(12 * 512 + 48 * me, 48)


class Links:
    def __init__(self, dp, fsdp):
        self.dp = dp
        self.fsdp = fsdp
        self.count = dp * fsdp
        self.near = [2 * m for m in range(fsdp // 2)]

    def send(self, values, mask):
        return lax.ppermute(values, AXES, [(i, i ^ mask) for i in range(self.count)])

    def deep(self, blocks):
        return lax.all_to_all(blocks, "dp", 0, 0, tiled=True)

    def gather_near(self, held):
        return [held] + [self.send(held, m) for m in self.near[1:]]

    def gather_core(self, pieces):
        return pieces + [
            (first, [(z, m ^ 1) for z, m in blocks], self.send(array, 1)) for first, blocks, array in pieces
        ]

    def near_pieces(self, first, near):
        return [(first, [(z, m) for z in range(self.dp)], x) for m, x in zip(self.near, near)]

    def places(self, me, relative):
        owner = jnp.arange(self.count, dtype=jnp.int32)
        differ = (owner ^ me) % self.fsdp
        place = differ // 2 if relative else owner % self.fsdp // 2
        return (differ % 2 * (self.fsdp // 2) + place) * self.dp + owner // self.fsdp

    def split_core(self, keep, got):
        n = self.dp
        return [
            add(keep[k * n : k * n + n], got[k]).astype(BF16)
            for k in range(len(self.near))
        ]

    def start_near(self, totals):
        return totals[:1] + [self.send(t, m) for t, m in zip(totals[1:], self.near[1:])]

    def swap_near(self, blocks):
        groups = [list(range(c, self.fsdp, 2)) for c in range(2)]
        return lax.all_to_all(blocks, "fsdp", 0, 0, axis_index_groups=groups, tiled=True)

    def total_core(self, keep, got):
        outs = []
        first = 0
        for x in got:
            outs.append(add(keep[first : first + x.shape[0]], x).astype(BF16))
            first += x.shape[0]
        return jnp.concatenate(outs, axis=0) if len(outs) > 1 else outs[0]

    def total_near(self, parts):
        if not isinstance(parts, list):
            parts = [parts[k : k + self.dp] for k in range(0, parts.shape[0], self.dp)]
        total = parts[0].astype(F32)
        for x in parts[1:]:
            total = total + x.astype(F32)
        return total.astype(BF16)

    def total_deep(self, parts):
        return jnp.sum(parts.astype(F32), axis=0)

    def reduce(self, keep, send):
        near = self.swap_near(self.total_core(keep, [self.send(send, 1)]))
        return self.total_deep(self.deep(self.total_near(near)))


def add(left, right):
    return left.astype(F32) + right.astype(F32)


def cost(us):
    return pl.CostEstimate(flops=us * 10**9, transcendentals=0, bytes_accessed=us * 10**6)


def add(left, right):
    return left.astype(F32) + right.astype(F32)


def fold(shard, width):
    return jnp.concatenate(
        [shard[..., j : j + width] for j in range(0, shard.shape[-1], width)], axis=-2
    )


def unfold(block, count):
    rows = block.shape[-2] // count
    return jnp.concatenate(
        [block[..., j * rows : (j + 1) * rows, :] for j in range(count)], axis=-1
    )


def reblock(blocks, layout, count):
    m = blocks.shape[0]
    outs = []
    for first, rows, k in layout:
        x = unfold(blocks[:, first : first + rows], k)
        x = x.reshape(m * x.shape[1], x.shape[2]).reshape(count, -1, x.shape[2])
        outs.append(fold(x, blocks.shape[2]))
    return jnp.concatenate(outs, axis=1)


def layout_of(parts):
    out = []
    first = 0
    for rows, k in parts:
        out.append((first, rows, k))
        first += rows
    return out


def per_device(links, *args):
    (
        byte_embeddings,
        byte_item,
        byte_mask,
        w_pool,
        b_pool,
        ln1_gain,
        ln1_bias,
        w_qkv,
        pos_u,
        pos_v,
        w_pos,
        w_out,
        ln2_gain,
        ln2_bias,
        w_ff1,
        b_ff1,
        w_ff2,
        b_ff2,
        w_up,
        b_up,
        cotangent,
    ) = args
    n_dev = links.count
    me = lax.axis_index(AXES).astype(jnp.int32)
    width = w_pos.shape[1]
    r_pool, r, r_ff2 = w_pool.shape[0], w_pos.shape[0], w_ff2.shape[0]
    direct = n_dev == BLOCKS
    vectors = [b_pool, ln1_gain, ln1_bias, pos_u, pos_v, ln2_gain, ln2_bias, b_ff2, b_ff1, b_up]
    lengths = [v.shape[0] for v in vectors]
    vec_rows = [v * n_dev // width for v in lengths]
    vec_first = [sum(vec_rows[:i]) for i in range(len(vec_rows))]

    params = pltpu.CompilerParams(vmem_limit_bytes=60 << 20)
    sds = jax.ShapeDtypeStruct
    if direct:
        shard_a, shard_b, shard_c = pl.pallas_call(
            pack_kernel,
            out_shape=(
                sds((links.dp, ROWS_A, width), BF16),
                sds((links.dp, ROWS_B - ROWS_C, width), BF16),
                sds((1, ROWS_C, width), BF16),
            ),
            in_specs=[SMEM] + [VMEM] * 17,
            out_specs=[ANY] * 2 + [VMEM],
            scratch_shapes=[
                pltpu.VMEM((ROWS_A, width), BF16),
                pltpu.VMEM((ROWS_B - ROWS_C, width), BF16),
                pltpu.SemaphoreType.DMA((2 * links.dp,)),
            ],
            compiler_params=params,
            cost_estimate=cost(3),
        name="pack",
        )(me[None], w_pool, w_qkv, w_pos, w_out, w_ff1, w_ff2, w_up, *[v[None] for v in vectors])
    else:
        flat = jnp.arange(n_dev * lengths[8])
        table = []
        for v in vectors:
            k = v.shape[0]
            spread = jnp.where(flat[: n_dev * k] // k == me, jnp.tile(v, n_dev), jnp.zeros((), v.dtype))
            table.append(spread.reshape(-1, width))
        table.append(jnp.zeros((16 - sum(vec_rows), width), BF16))
        shard_a = jnp.concatenate([w_pool] + table + [fold(w_qkv, width), w_pos], axis=0)
        shard_b = jnp.concatenate([w_out, fold(w_ff1, width), w_ff2], axis=0)
        shard_c = fold(w_up, width)[None]
        shard_a, shard_b = [
            jnp.broadcast_to(x[None], (links.dp,) + x.shape) for x in (shard_a, shard_b)
        ]
    split_a = r_pool + 16
    byte_total = byte_embeddings.shape[0]
    rows = byte_total // 3
    emb = byte_embeddings.reshape(rows, 3 * width)
    cot = cotangent.reshape(rows, 3 * width)
    mask3 = byte_mask.reshape(rows, 3)
    item = byte_item.reshape(rows, 3)[:, 0]
    same = item[1:] == item[:-1]
    no = jnp.zeros((1,), jnp.bool_)
    same_before = jnp.concatenate([no, same])[:, None]
    same_after = jnp.concatenate([same, no])[:, None]
    cols = jnp.concatenate([mask3, same_after.astype(jnp.int32)], axis=1)
    item_f = item.astype(F32)
    live = [mask3[:, j : j + 1] > 0 for j in range(3)]
    zero = jnp.zeros((), jnp.bfloat16)
    masked = [jnp.where(live[j], emb[:, j * width : (j + 1) * width], zero) for j in range(3)]
    up_grad = jnp.concatenate(
        [jnp.where(live[j], cot[:, j * width : (j + 1) * width], zero) for j in range(3)], axis=1
    )

    def down(x):
        moved = jnp.concatenate([jnp.zeros((1, width), x.dtype), x[:-1]], axis=0)
        return jnp.where(same_before, moved, zero)

    grouped = jnp.concatenate([down(masked[1]), down(masked[2]), masked[0]], axis=1)
    places = jnp.arange(rows).astype(F32)
    frequency = 10000.0 ** (-(2.0 * jnp.arange(width // 2).astype(F32)) / width)
    angles = places[:, None] * frequency[None, :]
    sine, cosine = jnp.sin(angles), jnp.cos(angles)
    key_pos = jnp.concatenate([cosine, sine], axis=1).astype(BF16)

    held_a = links.deep(shard_a)
    held_c = jnp.concatenate(links.gather_near(shard_c), axis=0)
    held_a, held_c, shard_b, emb, cot, cols, up_grad, grouped, sine, cosine, key_pos = lax.optimization_barrier(
        (held_a, held_c, shard_b, emb, cot, cols, up_grad, grouped, sine, cosine, key_pos)
    )
    pieces_a = links.gather_core(links.near_pieces(0, links.gather_near(held_a)))
    held_b = links.deep(shard_b)
    grouped, held_b = lax.optimization_barrier((grouped, held_b))
    near_b = links.gather_near(held_b)
    deep_c = links.deep(jnp.concatenate([held_c] * links.dp, axis=0))
    layout_a = layout_of([(r_pool, 1), (16, 0), (3 * r, 3), (r, 1)])
    layout_b = layout_of([(r, 1), (4 * r, 4), (r_ff2, 1), (3 * r, 3)])
    layout_a32 = layout_of([(48, 1), (16, 0), (48, 3), (16, 1)])
    layout_b32 = layout_of([(16, 1), (64, 4), (64, 1), (48, 3)])

    if direct:
        base = (me % links.fsdp)[None]
        place = jnp.stack([links.places(me, False), links.places(me, True)])
    else:

        def canonical(pieces, layout):
            lines = {}
            for first, blocks, array in pieces:
                for j, (z, m) in enumerate(blocks):
                    lines.setdefault(first, {})[m, z] = array[j]
            parts = []
            for first in sorted(lines):
                arr = jnp.stack(
                    [jnp.stack([lines[first][m, z] for m in range(links.fsdp)]) for z in range(links.dp)]
                )
                arr = jnp.take(arr, jnp.arange(links.fsdp) ^ (me % links.fsdp), axis=1)
                parts.append(arr.reshape((n_dev,) + arr.shape[2:]))
            blocks = jnp.concatenate(parts, axis=1)
            outs = []
            for first, rows_, k in layout:
                if k == 0:
                    total = jnp.sum(blocks[:, first : first + rows_].astype(F32), axis=0)
                    outs.append(
                        jnp.concatenate(
                            [total[None], jnp.zeros((BLOCKS - 1,) + total.shape, F32)], axis=0
                        ).astype(BF16)
                    )
                else:
                    outs.append(reblock(blocks, [(first, rows_, k)], BLOCKS))
            return [(0, [(d, 0) for d in range(BLOCKS)], jnp.concatenate(outs, axis=1))]

        pieces_a = canonical(pieces_a, layout_a)
        base = jnp.zeros((1,), jnp.int32)
        place = jnp.tile(jnp.arange(BLOCKS, dtype=jnp.int32)[None], (2, 1))

    pair_bf = sds((PAIRS, rows, 128), BF16)
    pair_f = sds((PAIRS, rows, 128), F32)
    square = sds((rows, width), F32)
    table_f = sds((16, width), F32)

    step = links.fsdp if direct else 1
    plan_a = [(first, [(z * step, m) for z, m in blocks]) for first, blocks, _ in pieces_a]
    n_a = len(plan_a)
    forward = pl.pallas_call(
        lambda *refs: forward_kernel(plan_a, n_a, *refs),
        out_shape=(
            square,
            sds((rows, width), BF16),
            pair_bf,
            pair_bf,
            pair_bf,
            pair_bf,
            sds((H, rows, rows), BF16),
            pair_bf,
            table_f,
            sds((BLOCKS, ROWS_A, width), BF16),
        ),
        in_specs=[SMEM] + [ANY] * n_a + [VMEM] * 6,
        out_specs=[VMEM] * 9 + [ANY],
        scratch_shapes=[
            pltpu.VMEM((BLOCKS, ROWS_A, width), BF16),
            pltpu.VMEM((PAIRS, width, 128), BF16),
            pltpu.VMEM((rows, rows), F32),
            pltpu.VMEM((rows, width), F32),
            pltpu.VMEM((rows, width + 128), BF16),
            pltpu.VMEM((rows, width + 128), BF16),
            pltpu.VMEM((rows, width), F32),
            pltpu.SemaphoreType.DMA,
            pltpu.SemaphoreType.DMA,
        ],
        compiler_params=params,
        cost_estimate=cost(20),
        name="forward",
    )
    pooled, normed, qu, qv, keys, vals, prob, ctx, vecs, wa = forward(base, *[a for _, _, a in pieces_a], grouped, item_f[:, None], item_f[None, :], sine, cosine, key_pos)
    pooled, near_b, deep_c = lax.optimization_barrier((pooled, near_b, deep_c))
    blocks_c = [(z, m) for z in range(links.dp) for m in links.near]
    pieces_b = links.gather_core(links.near_pieces(0, near_b) + [(shard_b.shape[1], blocks_c, deep_c)])
    if not direct:
        pieces_b = canonical(pieces_b, layout_b)

    plan_b = [(first, [(z * step, m) for z, m in blocks]) for first, blocks, _ in pieces_b]
    n_b = len(plan_b)
    half = BLOCKS // 2
    res_grad, cg, short_out, vec_grads, w_up_abs, keep_b, *send_b = pl.pallas_call(
        lambda *refs: middle_kernel(plan_b, n_b, *refs),
        out_shape=(
            square,
            pair_bf,
            sds((rows, width), BF16),
            table_f,
            sds((BLOCKS, 48, width), BF16),
            sds((half, ROWS_B, width), BF16),
        )
        + (sds((half // SENDS_B, ROWS_B, width), BF16),) * SENDS_B,
        in_specs=[SMEM, SMEM] + [ANY] * n_b + [VMEM] * 4,
        out_specs=[VMEM] * 4 + [ANY] * (2 + SENDS_B),
        scratch_shapes=[
            pltpu.VMEM((BLOCKS, ROWS_B, width), BF16),
            pltpu.VMEM((BLOCKS, ROWS_B, width), BF16),
            pltpu.VMEM((rows, width), F32),
            pltpu.VMEM((rows, 128), F32),
            pltpu.VMEM((rows, width), BF16),
            pltpu.VMEM((4, rows, 512), BF16),
            pltpu.VMEM((4, rows, 512), F32),
            pltpu.VMEM((rows, width), F32),
            pltpu.VMEM((rows, width), F32),
            pltpu.VMEM((rows, width), F32),
            pltpu.VMEM((rows, width), BF16),
            pltpu.SemaphoreType.DMA,
            pltpu.SemaphoreType.DMA((2 + SENDS_B,)),
        ],
        compiler_params=params,
        cost_estimate=cost(20),
        name="middle",
    )(base, place, *[a for _, _, a in pieces_b], pooled, ctx, up_grad, vecs)

    if direct:
        total_b = links.total_core(keep_b, [links.send(x, 1) for x in send_b])
        cg, total_b = lax.optimization_barrier((cg, total_b))
        near_b = links.swap_near(total_b)

    pooled_grad, w_pool_abs, keep_a, *send_a = pl.pallas_call(
        tail_kernel,
        out_shape=(
            sds((rows, width), BF16),
            sds((BLOCKS, 48, width), BF16),
            sds((half, ROWS_A, width), BF16),
        )
        + (sds((half // 4, ROWS_A, width), BF16),) * 4,
        in_specs=[SMEM, ANY] + [VMEM] * 14 + [ANY],
        out_specs=[VMEM] + [ANY] * 6,
        scratch_shapes=[
            pltpu.VMEM((PAIRS, width, 128), BF16),
            pltpu.VMEM((rows, width), F32),
            pltpu.VMEM((rows, rows), BF16),
            pltpu.VMEM((rows, width), F32),
            pltpu.VMEM((3 * PAIRS, rows, 128), F32),
            pltpu.VMEM((3, rows, width), BF16),
            pltpu.VMEM((PAIRS, width, 128), F32),
            pltpu.VMEM((BLOCKS, ROWS_A, width), BF16),
            pltpu.VMEM((BLOCKS, ROWS_A, width), BF16),
            pltpu.VMEM((rows, width), F32),
            pltpu.VMEM((16, width), F32),
            pltpu.VMEM((2, 2, rows, rows), BF16),
            pltpu.SemaphoreType.DMA((7,)),
            pltpu.SemaphoreType.DMA((2,)),
        ],
        compiler_params=params,
        cost_estimate=cost(27),
        name="tail",
    )(
        place, prob, cg, vals, keys, qu, qv, key_pos, sine, cosine, normed, grouped, pooled, res_grad, vecs,
        vec_grads, wa,
    )
    if direct:
        got_a = [links.send(x, 1) for x in send_a]
        totals_a = links.split_core(keep_a, got_a)
    out3, grad3 = pl.pallas_call(
        bytes_kernel,
        out_shape=(sds((rows, 3 * width), BF16), sds((rows, 3 * width), BF16)),
        in_specs=[VMEM] * 8,
        out_specs=[VMEM] * 2,
        scratch_shapes=[pltpu.VMEM((rows, width), F32)],
        compiler_params=params,
        cost_estimate=cost(1),
        name="bytes",
    )(emb, cot, cols, short_out, w_up_abs, vecs, pooled_grad, w_pool_abs)
    if direct:
        totals_a, near_b, out3, grad3 = lax.optimization_barrier((totals_a, near_b, out3, grad3))
        near_a = links.start_near(totals_a)
        deep_b = links.deep(links.total_near(near_b))
    block_output = out3.reshape(byte_total, width)
    input_grad = grad3.reshape(byte_total, width)

    if direct:
        deep_a = links.deep(links.total_near(near_a))
        g_out, g_ff1, g_up, g_ff2 = pl.pallas_call(
            finish_b_kernel,
            out_shape=tuple(sds(w.shape, F32) for w in (w_out, w_ff1, w_up, w_ff2)),
            in_specs=[VMEM],
            out_specs=[VMEM] * 4,
            compiler_params=params,
            name="finish_b",
        )(deep_b)
        g_pool, g_qkv, g_pos, *vec_out = pl.pallas_call(
            finish_a_kernel,
            out_shape=tuple(sds(w.shape, F32) for w in (w_pool, w_qkv, w_pos))
            + tuple(sds((1, n), F32) for n in lengths),
            in_specs=[SMEM, VMEM],
            out_specs=[VMEM] * 13,
            compiler_params=params,
            name="finish_a",
        )(me[None], deep_a)
        vec_out = [v.reshape(-1) for v in vec_out]
    else:

        def owned(keep, send, layout):
            blocks = jnp.concatenate([keep, *send], axis=0)
            outs = []
            for first, rows_, k in layout:
                if k == 0:
                    outs.append(jnp.tile(blocks[:1, first : first + rows_], (n_dev, 1, 1)))
                else:
                    outs.append(reblock(blocks, [(first, rows_, k)], n_dev))
            full = jnp.concatenate(outs, axis=1)
            full = jnp.zeros_like(full).at[links.places(me, False)].set(full)
            return links.reduce(full[: n_dev // 2], full[n_dev // 2 :])

        sum_b = owned(keep_b, send_b, layout_b32)
        sum_a = owned(keep_a, send_a, layout_a32)
        vec_sum = sum_a[r_pool : r_pool + 16]
        vec_out = []
        for first, k, n in zip(vec_first, lengths, vec_rows):
            line = vec_sum[first : first + n].reshape(-1)
            vec_out.append(lax.dynamic_slice(line, (me * k,), (k,)))
        g_pool, g_pos, g_out, g_ff2 = sum_a[:r_pool], sum_a[split_a + 3 * r :], sum_b[:r], sum_b[5 * r : 5 * r + r_ff2]
        g_qkv = unfold(sum_a[split_a : split_a + 3 * r], 3)
        g_ff1 = unfold(sum_b[r : 5 * r], 4)
        g_up = unfold(sum_b[5 * r + r_ff2 :], 3)
    (
        out_pool_b,
        out_ln1_gain,
        out_ln1_bias,
        out_u,
        out_v,
        out_ln2_gain,
        out_ln2_bias,
        out_ff2_b,
        out_ff1_b,
        out_up_b,
    ) = vec_out
    return (
        block_output,
        input_grad,
        g_pool,
        out_pool_b,
        out_ln1_gain,
        out_ln1_bias,
        g_qkv,
        out_u,
        out_v,
        g_pos,
        g_out,
        out_ln2_gain,
        out_ln2_bias,
        g_ff1,
        out_ff1_b,
        g_ff2,
        out_ff2_b,
        g_up,
        out_up_b,
    )


def solution(mesh):
    links = Links(mesh.shape["dp"], mesh.shape["fsdp"])
    rows = P(AXES, None)
    flat = P(AXES)
    ranks = (2, 1, 1, 2, 1, 1, 1, 2, 1, 1, 2, 2, 1, 1, 2, 1, 2, 1, 2, 1, 2)
    out_ranks = (2, 2, 2, 1, 1, 1, 2, 1, 1, 2, 2, 1, 1, 2, 1, 2, 1, 2, 1)
    return jax.shard_map(
        lambda *args: per_device(links, *args),
        mesh=mesh,
        in_specs=tuple(rows if k == 2 else flat for k in ranks),
        out_specs=tuple(rows if k == 2 else flat for k in out_ranks),
        check_vma=False,
    )
```

```python
import jax
import jax.numpy as jnp
from jax import lax
from jax.experimental import pallas as pl
from jax.experimental.pallas import tpu as pltpu
from jax.sharding import PartitionSpec as P

H = 8
DH = 64
QBLK = 256
AXES = ("dp", "fsdp")


eps_norm = 1e-05
big_negative = -1e30

F32 = jnp.float32
BF16 = jnp.bfloat16
BLOCKS = 32
PAIRS = 4
CH = 64
VMEM = pl.BlockSpec(memory_space=pltpu.VMEM)
SMEM = pl.BlockSpec(memory_space=pltpu.SMEM)
ANY = pl.BlockSpec(memory_space=pl.ANY)
GELU_C = 0.7978845608028654
ROWS_A = 128
ROWS_B = 192
ROWS_C = 48
VEC = slice(48, 64)


def mm(left, right, cl=1, cr=0):
    return lax.dot_general(left, right, (((cl,), (cr,)), ((), ())), preferred_element_type=F32)


def weight(ref, start, rows):
    block = ref[:, start : start + rows, :]
    return block.reshape(block.shape[0] * rows, block.shape[2])


def weight_ff2(ref, start, j):
    block = ref[8 * j : 8 * j + 8, start : start + 64, :]
    return block.reshape(512, block.shape[2])


def start_copy(source, dest, sem):
    copy = pltpu.make_async_copy(source, dest, sem)
    copy.start()
    return copy


def load_rows(me, plan, refs, dest, first, stop, sem):
    for (start, blocks), ref in zip(plan, refs):
        low, high = max(first, start), min(stop, start + ref.shape[1])
        if low < high:
            for k, (base, mask) in enumerate(blocks):
                pltpu.make_async_copy(
                    ref.at[k, pl.ds(low - start, high - low)],
                    dest.at[base + (me ^ mask), pl.ds(low, high - low)],
                    sem,
                ).start()


def wait_rows(dest, first, stop, sem):
    rows = dest.at[:, pl.ds(first, stop - first)]
    pltpu.make_async_copy(rows, rows, sem).wait()


def lane_half(shape, s):
    return (lax.broadcasted_iota(jnp.int32, shape, len(shape) - 1) // DH) == s


def norm_stats(x):
    width = x.shape[-1]
    mean = jnp.sum(x, axis=-1, keepdims=True) * (1.0 / width)
    centre = x - mean
    var = jnp.sum(centre * centre, axis=-1, keepdims=True) * (1.0 / width)
    rstd = lax.rsqrt(var + eps_norm)
    return centre * rstd, rstd


def norm_back(dy, xhat, rstd, gain):
    width = dy.shape[-1]
    d = dy * gain
    m1 = jnp.sum(d, axis=-1, keepdims=True) * (1.0 / width)
    m2 = jnp.sum(d * xhat, axis=-1, keepdims=True) * (1.0 / width)
    return rstd * (d - m1 - xhat * m2)


def forward_kernel(plan, n_pieces, me_ref, *refs):
    pieces = refs[:n_pieces]
    (grouped_hbm, item_col, item_row, sine_hbm, cosine_hbm, key_pos_hbm) = refs[
        n_pieces : n_pieces + 6
    ]
    hbm = refs[n_pieces + 6 : n_pieces + 14]
    vecs, w_out_hbm = refs[n_pieces + 14 : n_pieces + 16]
    (grouped, sine, cosine, pooled, normed, qu, qv, keys, vals, prob, ctx) = refs[
        n_pieces + 16 : n_pieces + 27
    ]
    (w, w_pos, bias, proj, qcat, kcat, tmp, scores, sem, sem2) = refs[n_pieces + 27 :]
    (pooled_hbm, normed_hbm, qu_hbm, qv_hbm, keys_hbm, vals_hbm, prob_hbm, ctx_hbm) = hbm
    me = me_ref[0]
    rows = grouped.shape[0]
    load_rows(me, plan, pieces, w, 0, 64, sem.at[0])
    get_grouped = start_copy(grouped_hbm, grouped, sem2.at[0])
    load_rows(me, plan, pieces, w, 64, ROWS_A, sem.at[1])
    get_sine = start_copy(sine_hbm, sine, sem2.at[1])
    get_cosine = start_copy(cosine_hbm, cosine, sem2.at[2])
    get_key_pos = start_copy(key_pos_hbm, kcat.at[:, 0:rows], sem2.at[3])
    for r in range(0, rows, CH):
        row = r + lax.broadcasted_iota(jnp.int32, (CH, rows), 0)
        col = lax.broadcasted_iota(jnp.int32, (CH, rows), 1)
        allowed = (item_col[r : r + CH, :] == item_row[...]) & (row >= col)
        bias[r : r + CH, :] = jnp.where(allowed, 0.0, big_negative)
    wait_rows(w, 0, 64, sem.at[0])
    get_grouped.wait()
    vec = jnp.sum(w[:, VEC, :].astype(F32), axis=0)
    vecs[...] = vec
    tmp[...] = mm(grouped[...], weight(w, 0, 48))
    for r in range(0, rows, CH):
        x = tmp[r : r + CH, :] + vec[0:1]
        pooled[r : r + CH, :] = x
        xhat, rstd = norm_stats(x)
        normed[r : r + CH, :] = (xhat * vec[1:2] + vec[2:3]).astype(BF16)
    wait_rows(w, 64, ROWS_A, sem.at[1])
    puts = [
        start_copy(w, w_out_hbm, sem2.at[4]),
        start_copy(pooled, pooled_hbm, sem2.at[5]),
        start_copy(normed, normed_hbm, sem2.at[6]),
    ]
    tmp[...] = mm(normed[...], weight(w, 64, 16))
    for r in range(0, rows, CH):
        x = tmp[r : r + CH, :]
        u = (x + vec[3:4]).astype(BF16)
        v = (x + vec[4:5]).astype(BF16)
        for p in range(PAIRS):
            qu[p, r : r + CH, :] = u[:, 128 * p : 128 * p + 128]
            qv[p, r : r + CH, :] = v[:, 128 * p : 128 * p + 128]
    x = mm(normed[...], weight(w, 80, 16)).astype(BF16)
    for p in range(PAIRS):
        keys[p] = x[:, 128 * p : 128 * p + 128]
    x = mm(normed[...], weight(w, 96, 16)).astype(BF16)
    for p in range(PAIRS):
        vals[p] = x[:, 128 * p : 128 * p + 128]
    x = weight(w, 112, 16)
    for p in range(PAIRS):
        w_pos[p] = x[:, 128 * p : 128 * p + 128]

    puts += [
        start_copy(x, y, sem2.at[7 + j])
        for j, (x, y) in enumerate(((qu, qu_hbm), (qv, qv_hbm), (keys, keys_hbm), (vals, vals_hbm)))
    ]
    get_sine.wait()
    get_cosine.wait()
    get_key_pos.wait()

    def put_prob(p):
        pair = pl.ds(2 * p, 2)
        return pltpu.make_async_copy(prob.at[pair], prob_hbm.at[pair], sem2.at[11])

    @pl.loop(0, PAIRS)
    def _(p):
        kcat[:, rows : rows + 128] = keys[p]
        zero = jnp.zeros((rows, 128), BF16)
        halves = [lane_half((rows, 128), s) for s in range(2)]

        def project(s):
            proj[s] = mm(jnp.where(halves[s], qv[p], zero), w_pos[p], 1, 1)

        def rotate(s):
            for r in range(0, rows, CH):
                a = proj[s, r : r + CH, 0:256]
                b = proj[s, r : r + CH, 256:512]
                si = sine[r : r + CH, :]
                co = cosine[r : r + CH, :]
                qcat[s, r : r + CH, 0:256] = (a * si + b * co).astype(BF16)
                qcat[s, r : r + CH, 256:512] = (b * si - a * co).astype(BF16)
            qcat[s, :, 512:640] = jnp.where(halves[s], qu[p], zero)

        def score(s, q):
            first, stop = q * QBLK, (q + 1) * QBLK
            scores[s, first:stop, 0:stop] = mm(qcat[s, first:stop, :], kcat[0:stop, :], 1, 1)

        def softmax(s, q):
            first, stop = q * QBLK, (q + 1) * QBLK
            for r in range(first, stop, CH):
                x = scores[s, r : r + CH, 0:stop] * (DH ** (-0.5)) + bias[r : r + CH, 0:stop]
                e = jnp.exp(x - jnp.max(x, axis=-1, keepdims=True))
                inv = 1.0 / jnp.sum(e, axis=-1, keepdims=True)
                prob[2 * p + s, r : r + CH, 0:stop] = (e * inv).astype(BF16)

        def context(s, q):
            first, stop = q * QBLK, (q + 1) * QBLK
            out = mm(prob[2 * p + s, first:stop, 0:stop], vals[p, 0:stop, :]).astype(BF16)
            if s == 1:
                out = jnp.where(lane_half((QBLK, 128), 1), out, ctx[p, first:stop, :])
            ctx[p, first:stop, :] = out

        project(0)
        project(1)
        rotate(0)
        score(0, 0)
        score(0, 1)
        rotate(1)
        softmax(0, 0)
        score(1, 0)
        score(1, 1)
        softmax(0, 1)
        context(0, 0)
        softmax(1, 0)
        context(0, 1)
        softmax(1, 1)
        context(1, 0)
        context(1, 1)
        put_prob(p).start()

    puts.append(start_copy(ctx, ctx_hbm, sem2.at[12]))
    pltpu.make_async_copy(prob, prob_hbm, sem2.at[11]).wait()
    for c in puts:
        c.wait()


def join(ref):
    return jnp.concatenate([ref[p] for p in range(PAIRS)], axis=1)


def store_blocks(grads, place_ref, line, grad, first, rows=16, start=0):
    for k in range(grad.shape[0] // rows):
        grads[place_ref[line, start + k], first : first + rows, :] = grad[k * rows : (k + 1) * rows].astype(BF16)


def put_blocks(grads, keep_hbm, send_hbm, first, stop, sem):
    rows = pl.ds(first, stop - first)
    half = BLOCKS // 2
    copies = []
    start = half
    for j, ref in enumerate(send_hbm):
        n = ref.shape[0]
        copies.append(start_copy(grads.at[pl.ds(start, n), rows], ref.at[:, rows], sem.at[1 + j]))
        start += n
    copies.append(start_copy(grads.at[pl.ds(0, half), rows], keep_hbm.at[:, rows], sem.at[0]))
    return copies


def middle_kernel(plan, n_pieces, me_ref, place_ref, *refs):
    pieces = refs[:n_pieces]
    (pooled_hbm, ctx_hbm, up_grad_hbm, vecs) = refs[n_pieces : n_pieces + 4]
    (res_grad_hbm, cg, short_out_hbm, vec_grads, w_up_hbm, keep_hbm, send_hbm) = refs[
        n_pieces + 4 : n_pieces + 11
    ]
    (pooled, ctx, up_grad, res_grad, short_out) = refs[n_pieces + 11 : n_pieces + 16]
    (w, grads, xhat, rstd, n2, hidden, pre, slope, acc, tmp, sgrad, bg, attn, sem, sem2, sem3) = refs[
        n_pieces + 16 :
    ]
    me = me_ref[0]
    rows = pooled.shape[0]
    load_rows(me, plan, pieces, w, 0, 80, sem.at[0])
    get_ctx = start_copy(ctx_hbm, ctx, sem2.at[0])
    get_pooled = start_copy(pooled_hbm, pooled, sem2.at[1])
    load_rows(me, plan, pieces, w, 80, 144, sem.at[1])
    load_rows(me, plan, pieces, w, 144, ROWS_B, sem.at[2])
    get_up_grad = start_copy(up_grad_hbm, up_grad, sem2.at[2])
    get_ctx.wait()
    get_pooled.wait()
    wait_rows(w, 0, 80, sem.at[0])
    gain2, bias2 = vecs[5:6, :], vecs[6:7, :]
    acc[...] = pooled[...] + mm(join(ctx), weight(w, 0, 16))
    for r in range(0, rows, CH):
        xh, rs = norm_stats(acc[r : r + CH, :])
        xhat[r : r + CH, :] = xh
        rstd[r : r + CH, :] = jnp.broadcast_to(rs, (CH, 128))
        n2[r : r + CH, :] = (xh * gain2 + bias2).astype(BF16)

    def first_layer(j):
        tmp[j] = mm(n2[...], weight(w, 16 + 16 * j, 16))

    def activate(j):
        b1 = vecs[8 + j : 9 + j, :]
        for r in range(0, rows, CH):
            x = tmp[j, r : r + CH, :] + b1
            x2 = x * x
            t = jnp.tanh(GELU_C * (x + 0.044715 * (x * x2)))
            hidden[r : r + CH, 512 * j : 512 * j + 512] = (0.5 * x * (1.0 + t)).astype(BF16)
            slope[j, r : r + CH, :] = 0.5 * (1.0 + t) + (0.5 * GELU_C) * x * (1.0 - t * t) * (
                1.0 + (3.0 * 0.044715) * x2
            )

    def up_back(j):
        return mm(up_grad[:, 512 * j : 512 * j + 512], weight(w, 144 + 16 * j, 16), 1, 1)

    def second_layer(j):
        return mm(hidden[:, 512 * j : 512 * j + 512], weight_ff2(w, 80, j))

    first_layer(0)
    first_layer(1)
    activate(0)
    wait_rows(w, 80, 144, sem.at[1])
    first_layer(2)
    activate(1)
    acc[...] += second_layer(0)
    first_layer(3)
    activate(2)
    acc[...] += second_layer(1)
    wait_rows(w, 144, ROWS_B, sem.at[2])
    get_up_grad.wait()
    sgrad[...] = up_back(0) + up_back(1)
    activate(3)
    acc[...] += second_layer(2)
    sgrad[...] += up_back(2)
    acc[...] += second_layer(3)
    bg[...] = sgrad[...].astype(BF16)
    short_out[...] = (acc[...] + vecs[7:8, :]).astype(BF16)
    puts = [
        start_copy(w.at[:, pl.ds(144, 48)], w_up_hbm, sem2.at[3]),
        start_copy(short_out, short_out_hbm, sem2.at[4]),
    ]

    def hidden_back(j):
        tmp[j] = mm(bg[...], weight_ff2(w, 80, j), 1, 1)

    def activate_back(j):
        total = jnp.zeros((1, 512), F32)
        for r in range(0, rows, CH):
            x = (tmp[j, r : r + CH, :] * slope[j, r : r + CH, :]).astype(BF16)
            pre[r : r + CH, 512 * j : 512 * j + 512] = x
            total = total + jnp.sum(x.astype(F32), axis=0, keepdims=True)
        vec_grads[8 + j : 9 + j, :] = total

    def up_weights(j):
        g = mm(short_out[...], up_grad[:, 512 * j : 512 * j + 512], 0, 0)
        store_blocks(grads, place_ref, 0, g, 144 + 16 * j)

    def second_weights(j):
        g = mm(hidden[:, 512 * j : 512 * j + 512], bg[...], 0, 0)
        store_blocks(grads, place_ref, 0, g, 80, 64, 8 * j)

    def first_weights(j):
        g = mm(n2[...], pre[:, 512 * j : 512 * j + 512], 0, 0)
        store_blocks(grads, place_ref, 0, g, 16 + 16 * j)

    def first_back(j):
        return mm(pre[:, 512 * j : 512 * j + 512], weight(w, 16 + 16 * j, 16), 1, 1)

    vec_grads[...] = jnp.zeros(vec_grads.shape, F32)
    hidden_back(0)
    hidden_back(1)
    activate_back(0)
    hidden_back(2)
    activate_back(1)
    acc[...] = first_back(0)
    hidden_back(3)
    activate_back(2)
    acc[...] += first_back(1)
    second_weights(0)
    activate_back(3)
    acc[...] += first_back(2)
    second_weights(1)
    acc[...] += first_back(3)
    second_weights(2)
    second_weights(3)
    dgain = jnp.zeros((1, 512), F32)
    dbias = jnp.zeros((1, 512), F32)
    for r in range(0, rows, CH):
        dy = acc[r : r + CH, :]
        xh = xhat[r : r + CH, :]
        dgain = dgain + jnp.sum(dy * xh, axis=0, keepdims=True)
        dbias = dbias + jnp.sum(dy, axis=0, keepdims=True)
        x = sgrad[r : r + CH, :] + norm_back(dy, xh, rstd[r : r + CH, 0:1], gain2)
        res_grad[r : r + CH, :] = x
        attn[r : r + CH, :] = x.astype(BF16)
    vec_grads[5:6, :] = dgain
    vec_grads[6:7, :] = dbias
    up_weights(0)
    up_weights(1)
    up_weights(2)
    puts += put_blocks(grads, keep_hbm, (send_hbm,), 80, ROWS_B, sem3.at[0])
    first_weights(0)
    first_weights(1)
    first_weights(2)
    first_weights(3)
    puts += put_blocks(grads, keep_hbm, (send_hbm,), 16, 80, sem3.at[1])
    for j in range(3):
        vec_grads[12 + j : 13 + j, :] = jnp.sum(
            up_grad[:, 512 * j : 512 * j + 512].astype(F32), axis=0, keepdims=True
        )
    vec_grads[7:8, :] = jnp.sum(bg[...].astype(F32), axis=0, keepdims=True)
    store_blocks(grads, place_ref, 0, mm(join(ctx), attn[...], 0, 0), 0)
    puts += put_blocks(grads, keep_hbm, (send_hbm,), 0, 16, sem3.at[2])
    puts.append(start_copy(res_grad, res_grad_hbm, sem2.at[5]))
    x = mm(attn[...], weight(w, 0, 16), 1, 1).astype(BF16)
    for p in range(PAIRS):
        cg[p] = x[:, 128 * p : 128 * p + 128]
    for c in puts:
        c.wait()


def tail_kernel(
    place_ref, prob, cg_hbm, vals_hbm, keys_hbm, qu_hbm, qv_hbm, key_pos_hbm, sine_hbm, cosine_hbm,
    normed_hbm, grouped_hbm, pooled_hbm, res_grad_hbm, vecs, vec_in, w_hbm,
    pg, w_pool_out, keep_hbm, send0, send1, send2, send3,
    cg, vals, keys, qu, qv, key_pos, sine, cosine, normed, grouped, pooled, res_grad,
    w_pos, pgrad, sg, posg, qg, qkvg, pos_w_grad, w, grads, acc, vec, prob_v, sem, prob_sem, get_sem,
):
    rows = key_pos.shape[0]
    n_q = rows // QBLK
    pairs = ((cg_hbm, cg), (vals_hbm, vals), (keys_hbm, keys), (qu_hbm, qu), (qv_hbm, qv))
    first_gets = [start_copy(x, y, get_sem.at[j]) for j, (x, y) in enumerate(pairs)]

    def fetch(p):
        return pltpu.make_async_copy(prob.at[pl.ds(2 * p, 2)], prob_v.at[p % 2], prob_sem.at[p % 2])

    fetch(0).start()
    tables = ((key_pos_hbm, key_pos), (sine_hbm, sine), (cosine_hbm, cosine))
    first_gets += [start_copy(x, y, get_sem.at[5 + j]) for j, (x, y) in enumerate(tables)]
    load = start_copy(w_hbm.at[:, pl.ds(112, 16)], w.at[:, pl.ds(112, 16)], sem.at[0])
    late = ((normed_hbm, normed), (grouped_hbm, grouped), (pooled_hbm, pooled), (res_grad_hbm, res_grad))
    late_gets = [start_copy(x, y, get_sem.at[8 + j]) for j, (x, y) in enumerate(late)]
    late_gets.append(start_copy(w_hbm.at[:, pl.ds(0, 112)], w.at[:, pl.ds(0, 112)], get_sem.at[12]))
    vec[...] = vec_in[...]
    load.wait()
    for c in first_gets:
        c.wait()
    x = weight(w, 112, 16)
    for p in range(PAIRS):
        w_pos[p] = x[:, 128 * p : 128 * p + 128]

    @pl.loop(0, PAIRS)
    def _(p):
        @pl.when(p + 1 < PAIRS)
        def _():
            fetch(p + 1).start()

        fetch(p).wait()
        slot = p % 2
        u_sums = []
        v_sums = []
        for s in range(2):
            half = lane_half((rows, 128), s)
            zero = jnp.zeros((rows, 128), BF16)
            cgm = jnp.where(half, cg[p], zero)
            qum = jnp.where(half, qu[p], zero)
            qvm = jnp.where(half, qv[p], zero)
            for q in range(n_q):
                first, stop = q * QBLK, (q + 1) * QBLK
                pgrad[first:stop, 0:stop] = mm(cgm[first:stop], vals[p, 0:stop, :], 1, 1)
                for r in range(first, stop, CH):
                    pr = prob_v[slot, s, r : r + CH, 0:stop].astype(F32)
                    t = pr * pgrad[r : r + CH, 0:stop]
                    inner = jnp.sum(t, axis=-1, keepdims=True)
                    sg[r : r + CH, 0:stop] = ((t - pr * inner) * (DH ** (-0.5))).astype(BF16)
                posg[first:stop, :] = mm(sg[first:stop, 0:stop], key_pos[0:stop, :])
                part = mm(sg[first:stop, 0:stop], keys[p, 0:stop, :])
                if s == 0:
                    qg[p, first:stop, :] = part
                else:
                    qg[p, first:stop, :] = jnp.where(
                        lane_half((QBLK, 128), 1), part, qg[p, first:stop, :]
                    )
                kg = mm(sg[first:stop, 0:stop], qum[first:stop], 0, 0)
                vg = mm(prob_v[slot, s, first:stop, 0:stop], cgm[first:stop], 0, 0)
                if s == 0 and q == 0:
                    qg[PAIRS + p] = jnp.zeros((rows, 128), F32)
                    qg[2 * PAIRS + p] = jnp.zeros((rows, 128), F32)
                qg[PAIRS + p, 0:stop, :] += kg
                qg[2 * PAIRS + p, 0:stop, :] += vg
            for r in range(0, rows, CH):
                a = posg[r : r + CH, 0:256]
                b = posg[r : r + CH, 256:512]
                si = sine[r : r + CH, :]
                co = cosine[r : r + CH, :]
                sg[r : r + CH, 0:256] = (a * si - b * co).astype(BF16)
                sg[r : r + CH, 256:512] = (a * co + b * si).astype(BF16)
            gw = mm(sg[...], qvm, 0, 0)
            if s == 0:
                pos_w_grad[p] = gw
            else:
                pos_w_grad[p] += gw
            qvg = jnp.where(half, mm(sg[...], w_pos[p]), 0.0)
            v_sums.append(jnp.sum(qvg, axis=0, keepdims=True))
            u_sums.append(jnp.sum(jnp.where(half, qg[p], 0.0), axis=0, keepdims=True))
            qg[p] += qvg
        u_row = u_sums[0] + u_sums[1]
        v_row = v_sums[0] + v_sums[1]
        for k in range(PAIRS):

            @pl.when(p == k)
            def _():
                vec[3:4, 128 * k : 128 * k + 128] = u_row
                vec[4:5, 128 * k : 128 * k + 128] = v_row

    for c in late_gets:
        c.wait()
    for j in range(3):
        for p in range(PAIRS):
            qkvg[j, :, 128 * p : 128 * p + 128] = qg[PAIRS * j + p].astype(BF16)
    for j in range(3):
        store_blocks(grads, place_ref, 1, mm(normed[...], qkvg[j], 0, 0), 64 + 16 * j)
    store_blocks(grads, place_ref, 1, join(pos_w_grad), 112)
    sends = (send0, send1, send2, send3)
    puts = put_blocks(grads, keep_hbm, sends, 64, ROWS_A, sem.at[pl.ds(2, 5)])
    keep_pool = pltpu.make_async_copy(w.at[:, 0:48], w_pool_out, sem.at[1])
    keep_pool.start()
    acc[...] = (
        mm(qkvg[0], weight(w, 64, 16), 1, 1)
        + mm(qkvg[1], weight(w, 80, 16), 1, 1)
        + mm(qkvg[2], weight(w, 96, 16), 1, 1)
    )
    gain1 = vecs[1:2, :]
    dgain = jnp.zeros((1, 512), F32)
    dbias = jnp.zeros((1, 512), F32)
    dpool = jnp.zeros((1, 512), F32)
    for r in range(0, rows, CH):
        dy = acc[r : r + CH, :]
        xh, rs = norm_stats(pooled[r : r + CH, :])
        dgain = dgain + jnp.sum(dy * xh, axis=0, keepdims=True)
        dbias = dbias + jnp.sum(dy, axis=0, keepdims=True)
        x = (res_grad[r : r + CH, :] + norm_back(dy, xh, rs, gain1)).astype(BF16)
        pg[r : r + CH, :] = x
        dpool = dpool + jnp.sum(x.astype(F32), axis=0, keepdims=True)
    vec[0:1, :] = dpool
    vec[1:2, :] = dgain
    vec[2:3, :] = dbias
    table = vec[...].astype(BF16)
    for d in range(BLOCKS):
        grads[place_ref[1, d], VEC, :] = table
    for j in range(3):
        g = mm(grouped[:, 512 * j : 512 * j + 512], pg[...], 0, 0)
        for k in range(32):
            granule = 32 * j + k
            d, sub = granule // 3, granule % 3
            grads[place_ref[1, d], 16 * sub : 16 * sub + 16, :] = g[16 * k : 16 * k + 16].astype(BF16)
    puts += put_blocks(grads, keep_hbm, sends, 0, 64, sem.at[pl.ds(7, 5)])
    keep_pool.wait()
    for c in puts:
        c.wait()


def bytes_kernel(emb, cot, cols, short_out, w_up, vecs, pg, w_pool, out, grad, tmp):
    rows = emb.shape[0]
    for j in range(3):
        tmp[...] = mm(short_out[...], weight(w_up, 16 * j, 16))
        up_bias = vecs[12 + j : 13 + j, :]
        for r in range(0, rows, CH):
            x = emb[r : r + CH, 512 * j : 512 * j + 512].astype(F32) + tmp[r : r + CH, :] + up_bias
            out[r : r + CH, 512 * j : 512 * j + 512] = jnp.where(
                cols[r : r + CH, j : j + 1] > 0, x, 0.0
            ).astype(BF16)
    pool = weight(w_pool, 0, 48)
    for j in range(3):
        src = (j + 2) % 3
        tmp[...] = mm(pg[...], pool[512 * src : 512 * src + 512, :], 1, 1)
        if j > 0:
            tmp[...] = pltpu.roll(tmp[...], rows - 1, 0)
        for r in range(0, rows, CH):
            x = tmp[r : r + CH, :]
            if j > 0:
                x = jnp.where(cols[r : r + CH, 3:4] > 0, x, 0.0)
            x = cot[r : r + CH, 512 * j : 512 * j + 512].astype(F32) + x
            grad[r : r + CH, 512 * j : 512 * j + 512] = jnp.where(
                cols[r : r + CH, j : j + 1] > 0, x, 0.0
            ).astype(BF16)


def pack_kernel(me_ref, *refs):
    (w_pool, w_qkv, w_pos, w_out, w_ff1, w_ff2, w_up) = refs[:7]
    vectors = refs[7:17]
    all_a, all_b, out_c, out_a, out_b, sem = refs[17:]
    me = me_ref[0]
    out_a[0:48, :] = w_pool[...]
    for j in range(3):
        out_a[64 + 16 * j : 80 + 16 * j, :] = w_qkv[:, 512 * j : 512 * j + 512]
        out_c[0, 16 * j : 16 + 16 * j, :] = w_up[:, 512 * j : 512 * j + 512]
    out_a[112:128, :] = w_pos[...]
    out_b[0:16, :] = w_out[...]
    for j in range(4):
        out_b[16 + 16 * j : 32 + 16 * j, :] = w_ff1[:, 512 * j : 512 * j + 512]
    out_b[80:144, :] = w_ff2[...]

    def spread(x, first):
        k = x.shape[1]
        lane = first + lax.broadcasted_iota(jnp.int32, (k, 512), 1)
        row = lax.broadcasted_iota(jnp.int32, (k, 512), 0)
        pick = jnp.where(lane % k == row, 1.0, 0.0).astype(BF16)
        own = (first + lax.broadcasted_iota(jnp.int32, (x.shape[0], 512), 1)) // k == me
        return jnp.where(own, mm(x, pick), 0.0)

    lines = [spread(v[...], 0) for v in vectors[:8]]
    lines += [spread(vectors[8][...], 512 * j) for j in range(4)]
    lines += [spread(vectors[9][...], 512 * j) for j in range(3)]
    lines.append(jnp.zeros((1, 512), F32))
    out_a[VEC, :] = jnp.concatenate(lines, axis=0).astype(BF16)
    copies = []
    for j in range(all_a.shape[0]):
        copies.append(pltpu.make_async_copy(out_a, all_a.at[j], sem.at[j]))
    for j in range(all_b.shape[0]):
        copies.append(pltpu.make_async_copy(out_b, all_b.at[j], sem.at[all_a.shape[0] + j]))
    for c in copies:
        c.start()
    for c in copies:
        c.wait()


def finish_b_kernel(parts, out, ff1, up, ff2):
    total = parts[0].astype(F32)
    for j in range(1, parts.shape[0]):
        total = total + parts[j].astype(F32)
    out[...] = total[0:16]
    for j in range(4):
        ff1[:, 512 * j : 512 * j + 512] = total[16 + 16 * j : 32 + 16 * j]
    for j in range(3):
        up[:, 512 * j : 512 * j + 512] = total[144 + 16 * j : 160 + 16 * j]
    ff2[...] = total[80:144]


def finish_a_kernel(me_ref, parts, pool, qkv, pos, *vectors):
    me = me_ref[0]
    total = parts[0].astype(F32)
    for j in range(1, parts.shape[0]):
        total = total + parts[j].astype(F32)
    pool[...] = total[0:48]
    for j in range(3):
        qkv[:, 512 * j : 512 * j + 512] = total[64 + 16 * j : 80 + 16 * j]
    pos[...] = total[112:128]
    table = total[VEC]
    lines = pltpu.roll(table[0:8], 512 - 16 * me, 1)
    for j in range(8):
        vectors[j][...] = lines[j : j + 1, 0:16]
    row = lax.broadcasted_iota(jnp.int32, (16, 512), 0)

    def line(j):
        return jnp.sum(jnp.where(row == j, table, 0.0), axis=0, keepdims=True)

    def part(first, length):
        j, off = first // 512, first % 512
        here = pltpu.roll(jnp.broadcast_to(line(j), (8, 512)), 512 - off, 1)
        there = pltpu.roll(jnp.broadcast_to(line(j + 1), (8, 512)), 512 - off, 1)
        lane = lax.broadcasted_iota(jnp.int32, (8, 512), 1)
        return jnp.where(lane < 512 - off, here, there)[0:1, 0:length]

    vectors[8][...] = part(8 * 512 + 64 * me, 64)
    vectors[9][...] = part(12 * 512 + 48 * me, 48)


class Links:
    def __init__(self, dp, fsdp):
        self.dp = dp
        self.fsdp = fsdp
        self.count = dp * fsdp
        self.near = [2 * m for m in range(fsdp // 2)]

    def send(self, values, mask):
        return lax.ppermute(values, AXES, [(i, i ^ mask) for i in range(self.count)])

    def deep(self, blocks):
        return lax.all_to_all(blocks, "dp", 0, 0, tiled=True)

    def gather_near(self, held):
        return [held] + [self.send(held, m) for m in self.near[1:]]

    def gather_core(self, pieces):
        return pieces + [
            (first, [(z, m ^ 1) for z, m in blocks], self.send(array, 1)) for first, blocks, array in pieces
        ]

    def near_pieces(self, first, near):
        return [(first, [(z, m) for z in range(self.dp)], x) for m, x in zip(self.near, near)]

    def places(self, me, relative):
        owner = jnp.arange(self.count, dtype=jnp.int32)
        differ = (owner ^ me) % self.fsdp
        place = differ // 2 if relative else owner % self.fsdp // 2
        return (differ % 2 * (self.fsdp // 2) + place) * self.dp + owner // self.fsdp

    def split_core(self, keep, got):
        n = self.dp
        return [
            add(keep[k * n : k * n + n], got[k]).astype(BF16)
            for k in range(len(self.near))
        ]

    def start_near(self, totals):
        return totals[:1] + [self.send(t, m) for t, m in zip(totals[1:], self.near[1:])]

    def swap_near(self, blocks):
        groups = [list(range(c, self.fsdp, 2)) for c in range(2)]
        return lax.all_to_all(blocks, "fsdp", 0, 0, axis_index_groups=groups, tiled=True)

    def total_core(self, keep, got):
        outs = []
        first = 0
        for x in got:
            outs.append(add(keep[first : first + x.shape[0]], x).astype(BF16))
            first += x.shape[0]
        return jnp.concatenate(outs, axis=0) if len(outs) > 1 else outs[0]

    def total_near(self, parts):
        if not isinstance(parts, list):
            parts = [parts[k : k + self.dp] for k in range(0, parts.shape[0], self.dp)]
        total = parts[0].astype(F32)
        for x in parts[1:]:
            total = total + x.astype(F32)
        return total.astype(BF16)

    def total_deep(self, parts):
        return jnp.sum(parts.astype(F32), axis=0)

    def reduce(self, keep, send):
        near = self.swap_near(self.total_core(keep, [self.send(send, 1)]))
        return self.total_deep(self.deep(self.total_near(near)))


def add(left, right):
    return left.astype(F32) + right.astype(F32)


def cost(us):
    return pl.CostEstimate(flops=us * 10**9, transcendentals=0, bytes_accessed=us * 10**6)


def add(left, right):
    return left.astype(F32) + right.astype(F32)


def fold(shard, width):
    return jnp.concatenate(
        [shard[..., j : j + width] for j in range(0, shard.shape[-1], width)], axis=-2
    )


def unfold(block, count):
    rows = block.shape[-2] // count
    return jnp.concatenate(
        [block[..., j * rows : (j + 1) * rows, :] for j in range(count)], axis=-1
    )


def reblock(blocks, layout, count):
    m = blocks.shape[0]
    outs = []
    for first, rows, k in layout:
        x = unfold(blocks[:, first : first + rows], k)
        x = x.reshape(m * x.shape[1], x.shape[2]).reshape(count, -1, x.shape[2])
        outs.append(fold(x, blocks.shape[2]))
    return jnp.concatenate(outs, axis=1)


def layout_of(parts):
    out = []
    first = 0
    for rows, k in parts:
        out.append((first, rows, k))
        first += rows
    return out


def per_device(links, *args):
    (
        byte_embeddings,
        byte_item,
        byte_mask,
        w_pool,
        b_pool,
        ln1_gain,
        ln1_bias,
        w_qkv,
        pos_u,
        pos_v,
        w_pos,
        w_out,
        ln2_gain,
        ln2_bias,
        w_ff1,
        b_ff1,
        w_ff2,
        b_ff2,
        w_up,
        b_up,
        cotangent,
    ) = args
    n_dev = links.count
    me = lax.axis_index(AXES).astype(jnp.int32)
    width = w_pos.shape[1]
    r_pool, r, r_ff2 = w_pool.shape[0], w_pos.shape[0], w_ff2.shape[0]
    direct = n_dev == BLOCKS
    vectors = [b_pool, ln1_gain, ln1_bias, pos_u, pos_v, ln2_gain, ln2_bias, b_ff2, b_ff1, b_up]
    lengths = [v.shape[0] for v in vectors]
    vec_rows = [v * n_dev // width for v in lengths]
    vec_first = [sum(vec_rows[:i]) for i in range(len(vec_rows))]

    params = pltpu.CompilerParams(vmem_limit_bytes=60 << 20)
    sds = jax.ShapeDtypeStruct
    if direct:
        shard_a, shard_b, shard_c = pl.pallas_call(
            pack_kernel,
            out_shape=(
                sds((links.dp, ROWS_A, width), BF16),
                sds((links.dp, ROWS_B - ROWS_C, width), BF16),
                sds((1, ROWS_C, width), BF16),
            ),
            in_specs=[SMEM] + [VMEM] * 17,
            out_specs=[ANY] * 2 + [VMEM],
            scratch_shapes=[
                pltpu.VMEM((ROWS_A, width), BF16),
                pltpu.VMEM((ROWS_B - ROWS_C, width), BF16),
                pltpu.SemaphoreType.DMA((2 * links.dp,)),
            ],
            compiler_params=params,
            cost_estimate=cost(3),
        name="pack",
        )(me[None], w_pool, w_qkv, w_pos, w_out, w_ff1, w_ff2, w_up, *[v[None] for v in vectors])
    else:
        flat = jnp.arange(n_dev * lengths[8])
        table = []
        for v in vectors:
            k = v.shape[0]
            spread = jnp.where(flat[: n_dev * k] // k == me, jnp.tile(v, n_dev), jnp.zeros((), v.dtype))
            table.append(spread.reshape(-1, width))
        table.append(jnp.zeros((16 - sum(vec_rows), width), BF16))
        shard_a = jnp.concatenate([w_pool] + table + [fold(w_qkv, width), w_pos], axis=0)
        shard_b = jnp.concatenate([w_out, fold(w_ff1, width), w_ff2], axis=0)
        shard_c = fold(w_up, width)[None]
        shard_a, shard_b = [
            jnp.broadcast_to(x[None], (links.dp,) + x.shape) for x in (shard_a, shard_b)
        ]
    split_a = r_pool + 16
    byte_total = byte_embeddings.shape[0]
    rows = byte_total // 3
    emb = byte_embeddings.reshape(rows, 3 * width)
    cot = cotangent.reshape(rows, 3 * width)
    mask3 = byte_mask.reshape(rows, 3)
    item = byte_item.reshape(rows, 3)[:, 0]
    same = item[1:] == item[:-1]
    no = jnp.zeros((1,), jnp.bool_)
    same_before = jnp.concatenate([no, same])[:, None]
    same_after = jnp.concatenate([same, no])[:, None]
    cols = jnp.concatenate([mask3, same_after.astype(jnp.int32)], axis=1)
    item_f = item.astype(F32)
    live = [mask3[:, j : j + 1] > 0 for j in range(3)]
    zero = jnp.zeros((), jnp.bfloat16)
    masked = [jnp.where(live[j], emb[:, j * width : (j + 1) * width], zero) for j in range(3)]
    up_grad = jnp.concatenate(
        [jnp.where(live[j], cot[:, j * width : (j + 1) * width], zero) for j in range(3)], axis=1
    )

    def down(x):
        moved = jnp.concatenate([jnp.zeros((1, width), x.dtype), x[:-1]], axis=0)
        return jnp.where(same_before, moved, zero)

    grouped = jnp.concatenate([down(masked[1]), down(masked[2]), masked[0]], axis=1)
    places = jnp.arange(rows).astype(F32)
    frequency = 10000.0 ** (-(2.0 * jnp.arange(width // 2).astype(F32)) / width)
    angles = places[:, None] * frequency[None, :]
    sine, cosine = jnp.sin(angles), jnp.cos(angles)
    key_pos = jnp.concatenate([cosine, sine], axis=1).astype(BF16)

    held_a = links.deep(shard_a)
    held_c = jnp.concatenate(links.gather_near(shard_c), axis=0)
    item_col, item_row = item_f[:, None], item_f[None, :]
    if direct:
        place = jnp.stack([links.places(me, False), links.places(me, True)])
    else:
        place = jnp.tile(jnp.arange(BLOCKS, dtype=jnp.int32)[None], (2, 1))
    held_a, held_c, shard_b = lax.optimization_barrier((held_a, held_c, shard_b))
    near_a = links.gather_near(held_a)
    given = (emb, cot, cols, up_grad, grouped, sine, cosine, key_pos, item_col, item_row, place)
    near_a, given = lax.optimization_barrier((near_a, given))
    emb, cot, cols, up_grad, grouped, sine, cosine, key_pos, item_col, item_row, place = given
    pieces_a = links.gather_core(links.near_pieces(0, near_a))
    held_b = links.deep(shard_b)
    grouped, held_b = lax.optimization_barrier((grouped, held_b))
    near_b = links.gather_near(held_b)
    copies_c = jnp.concatenate([held_c] * links.dp, axis=0)
    last = pieces_a[-1]
    copies_c, array = lax.optimization_barrier((copies_c, last[2]))
    pieces_a[-1] = last[:2] + (array,)
    deep_c = links.deep(copies_c)
    layout_a = layout_of([(r_pool, 1), (16, 0), (3 * r, 3), (r, 1)])
    layout_b = layout_of([(r, 1), (4 * r, 4), (r_ff2, 1), (3 * r, 3)])
    layout_a32 = layout_of([(48, 1), (16, 0), (48, 3), (16, 1)])
    layout_b32 = layout_of([(16, 1), (64, 4), (64, 1), (48, 3)])

    if direct:
        base = (me % links.fsdp)[None]
    else:

        def canonical(pieces, layout):
            lines = {}
            for first, blocks, array in pieces:
                for j, (z, m) in enumerate(blocks):
                    lines.setdefault(first, {})[m, z] = array[j]
            parts = []
            for first in sorted(lines):
                arr = jnp.stack(
                    [jnp.stack([lines[first][m, z] for m in range(links.fsdp)]) for z in range(links.dp)]
                )
                arr = jnp.take(arr, jnp.arange(links.fsdp) ^ (me % links.fsdp), axis=1)
                parts.append(arr.reshape((n_dev,) + arr.shape[2:]))
            blocks = jnp.concatenate(parts, axis=1)
            outs = []
            for first, rows_, k in layout:
                if k == 0:
                    total = jnp.sum(blocks[:, first : first + rows_].astype(F32), axis=0)
                    outs.append(
                        jnp.concatenate(
                            [total[None], jnp.zeros((BLOCKS - 1,) + total.shape, F32)], axis=0
                        ).astype(BF16)
                    )
                else:
                    outs.append(reblock(blocks, [(first, rows_, k)], BLOCKS))
            return [(0, [(d, 0) for d in range(BLOCKS)], jnp.concatenate(outs, axis=1))]

        pieces_a = canonical(pieces_a, layout_a)
        base = jnp.zeros((1,), jnp.int32)

    pair_bf = sds((PAIRS, rows, 128), BF16)
    pair_f = sds((PAIRS, rows, 128), F32)
    square = sds((rows, width), F32)
    table_f = sds((16, width), F32)

    step = links.fsdp if direct else 1
    plan_a = [(first, [(z * step, m) for z, m in blocks]) for first, blocks, _ in pieces_a]
    n_a = len(plan_a)
    forward = pl.pallas_call(
        lambda *refs: forward_kernel(plan_a, n_a, *refs),
        out_shape=(
            square,
            sds((rows, width), BF16),
            pair_bf,
            pair_bf,
            pair_bf,
            pair_bf,
            sds((H, rows, rows), BF16),
            pair_bf,
            table_f,
            sds((BLOCKS, ROWS_A, width), BF16),
        ),
        in_specs=[SMEM] + [ANY] * n_a + [ANY, VMEM, VMEM, ANY, ANY, ANY],
        out_specs=[ANY] * 8 + [VMEM, ANY],
        scratch_shapes=[
            pltpu.VMEM((rows, 3 * width), BF16),
            pltpu.VMEM((rows, width // 2), F32),
            pltpu.VMEM((rows, width // 2), F32),
            pltpu.VMEM((rows, width), F32),
            pltpu.VMEM((rows, width), BF16),
        ]
        + [pltpu.VMEM((PAIRS, rows, 128), BF16)] * 4
        + [
            pltpu.VMEM((H, rows, rows), BF16),
            pltpu.VMEM((PAIRS, rows, 128), BF16),
            pltpu.VMEM((BLOCKS, ROWS_A, width), BF16),
            pltpu.VMEM((PAIRS, width, 128), BF16),
            pltpu.VMEM((rows, rows), F32),
            pltpu.VMEM((2, rows, width), F32),
            pltpu.VMEM((2, rows, width + 128), BF16),
            pltpu.VMEM((rows, width + 128), BF16),
            pltpu.VMEM((rows, width), F32),
            pltpu.VMEM((2, rows, rows), F32),
            pltpu.SemaphoreType.DMA((2,)),
            pltpu.SemaphoreType.DMA((13,)),
        ],
        compiler_params=params,
        cost_estimate=cost(20),
        name="forward",
    )
    pooled, normed, qu, qv, keys, vals, prob, ctx, vecs, wa = forward(base, *[a for _, _, a in pieces_a], grouped, item_col, item_row, sine, cosine, key_pos)
    pooled, near_b, deep_c = lax.optimization_barrier((pooled, near_b, deep_c))
    blocks_c = [(z, m) for z in range(links.dp) for m in links.near]
    pieces_b = links.gather_core(links.near_pieces(0, near_b) + [(shard_b.shape[1], blocks_c, deep_c)])
    if not direct:
        pieces_b = canonical(pieces_b, layout_b)

    plan_b = [(first, [(z * step, m) for z, m in blocks]) for first, blocks, _ in pieces_b]
    n_b = len(plan_b)
    half = BLOCKS // 2
    res_grad, cg, short_out, vec_grads, w_up_abs, keep_b, *send_b = pl.pallas_call(
        lambda *refs: middle_kernel(plan_b, n_b, *refs),
        out_shape=(
            square,
            pair_bf,
            sds((rows, width), BF16),
            table_f,
            sds((BLOCKS, 48, width), BF16),
            sds((half, ROWS_B, width), BF16),
        )
        + (sds((half, ROWS_B, width), BF16),),
        in_specs=[SMEM, SMEM] + [ANY] * n_b + [ANY, ANY, ANY, VMEM],
        out_specs=[ANY, VMEM, ANY, VMEM] + [ANY] * 3,
        scratch_shapes=[
            pltpu.VMEM((rows, width), F32),
            pltpu.VMEM((PAIRS, rows, 128), BF16),
            pltpu.VMEM((rows, 3 * width), BF16),
            pltpu.VMEM((rows, width), F32),
            pltpu.VMEM((rows, width), BF16),
            pltpu.VMEM((BLOCKS, ROWS_B, width), BF16),
            pltpu.VMEM((BLOCKS, ROWS_B, width), BF16),
            pltpu.VMEM((rows, width), F32),
            pltpu.VMEM((rows, 128), F32),
            pltpu.VMEM((rows, width), BF16),
            pltpu.VMEM((rows, 4 * 512), BF16),
            pltpu.VMEM((rows, 4 * 512), BF16),
            pltpu.VMEM((4, rows, 512), F32),
            pltpu.VMEM((rows, width), F32),
            pltpu.VMEM((4, rows, width), F32),
            pltpu.VMEM((rows, width), F32),
            pltpu.VMEM((rows, width), BF16),
            pltpu.VMEM((rows, width), BF16),
            pltpu.SemaphoreType.DMA((3,)),
            pltpu.SemaphoreType.DMA((6,)),
            pltpu.SemaphoreType.DMA((3, 2)),
        ],
        compiler_params=params,
        cost_estimate=cost(20),
        name="middle",
    )(base, place, *[a for _, _, a in pieces_b], pooled, ctx, up_grad, vecs)

    if direct:
        total_b = links.total_core(keep_b, [links.send(x, 1) for x in send_b])
        cg, total_b = lax.optimization_barrier((cg, total_b))
        near_b = links.swap_near(total_b)

    pooled_grad, w_pool_abs, keep_a, *send_a = pl.pallas_call(
        tail_kernel,
        out_shape=(
            sds((rows, width), BF16),
            sds((BLOCKS, 48, width), BF16),
            sds((half, ROWS_A, width), BF16),
        )
        + (sds((half // 4, ROWS_A, width), BF16),) * 4,
        in_specs=[SMEM] + [ANY] * 13 + [VMEM] * 2 + [ANY],
        out_specs=[VMEM] + [ANY] * 6,
        scratch_shapes=[pltpu.VMEM((PAIRS, rows, 128), BF16)] * 5
        + [
            pltpu.VMEM((rows, width), BF16),
            pltpu.VMEM((rows, width // 2), F32),
            pltpu.VMEM((rows, width // 2), F32),
            pltpu.VMEM((rows, width), BF16),
            pltpu.VMEM((rows, 3 * width), BF16),
            pltpu.VMEM((rows, width), F32),
            pltpu.VMEM((rows, width), F32),
            pltpu.VMEM((PAIRS, width, 128), BF16),
            pltpu.VMEM((rows, width), F32),
            pltpu.VMEM((rows, rows), BF16),
            pltpu.VMEM((rows, width), F32),
            pltpu.VMEM((3 * PAIRS, rows, 128), F32),
            pltpu.VMEM((3, rows, width), BF16),
            pltpu.VMEM((PAIRS, width, 128), F32),
            pltpu.VMEM((BLOCKS, ROWS_A, width), BF16),
            pltpu.VMEM((BLOCKS, ROWS_A, width), BF16),
            pltpu.VMEM((rows, width), F32),
            pltpu.VMEM((16, width), F32),
            pltpu.VMEM((2, 2, rows, rows), BF16),
            pltpu.SemaphoreType.DMA((12,)),
            pltpu.SemaphoreType.DMA((2,)),
            pltpu.SemaphoreType.DMA((13,)),
        ],
        compiler_params=params,
        cost_estimate=cost(27),
        name="tail",
    )(
        place, prob, cg, vals, keys, qu, qv, key_pos, sine, cosine, normed, grouped, pooled, res_grad, vecs,
        vec_grads, wa,
    )
    if direct:
        got_a = [links.send(x, 1) for x in send_a]
        totals_a = links.split_core(keep_a, got_a)
    out3, grad3 = pl.pallas_call(
        bytes_kernel,
        out_shape=(sds((rows, 3 * width), BF16), sds((rows, 3 * width), BF16)),
        in_specs=[VMEM] * 8,
        out_specs=[VMEM] * 2,
        scratch_shapes=[pltpu.VMEM((rows, width), F32)],
        compiler_params=params,
        cost_estimate=cost(1),
        name="bytes",
    )(emb, cot, cols, short_out, w_up_abs, vecs, pooled_grad, w_pool_abs)
    if direct:
        totals_a, near_b, out3, grad3 = lax.optimization_barrier((totals_a, near_b, out3, grad3))
        near_a = links.start_near(totals_a)
        deep_b = links.deep(links.total_near(near_b))
    block_output = out3.reshape(byte_total, width)
    input_grad = grad3.reshape(byte_total, width)

    if direct:
        deep_a = links.deep(links.total_near(near_a))
        g_out, g_ff1, g_up, g_ff2 = pl.pallas_call(
            finish_b_kernel,
            out_shape=tuple(sds(w.shape, F32) for w in (w_out, w_ff1, w_up, w_ff2)),
            in_specs=[VMEM],
            out_specs=[VMEM] * 4,
            compiler_params=params,
            name="finish_b",
        )(deep_b)
        g_pool, g_qkv, g_pos, *vec_out = pl.pallas_call(
            finish_a_kernel,
            out_shape=tuple(sds(w.shape, F32) for w in (w_pool, w_qkv, w_pos))
            + tuple(sds((1, n), F32) for n in lengths),
            in_specs=[SMEM, VMEM],
            out_specs=[VMEM] * 13,
            compiler_params=params,
            name="finish_a",
        )(me[None], deep_a)
        vec_out = [v.reshape(-1) for v in vec_out]
    else:

        def owned(keep, send, layout):
            blocks = jnp.concatenate([keep, *send], axis=0)
            outs = []
            for first, rows_, k in layout:
                if k == 0:
                    outs.append(jnp.tile(blocks[:1, first : first + rows_], (n_dev, 1, 1)))
                else:
                    outs.append(reblock(blocks, [(first, rows_, k)], n_dev))
            full = jnp.concatenate(outs, axis=1)
            full = jnp.zeros_like(full).at[links.places(me, False)].set(full)
            return links.reduce(full[: n_dev // 2], full[n_dev // 2 :])

        sum_b = owned(keep_b, send_b, layout_b32)
        sum_a = owned(keep_a, send_a, layout_a32)
        vec_sum = sum_a[r_pool : r_pool + 16]
        vec_out = []
        for first, k, n in zip(vec_first, lengths, vec_rows):
            line = vec_sum[first : first + n].reshape(-1)
            vec_out.append(lax.dynamic_slice(line, (me * k,), (k,)))
        g_pool, g_pos, g_out, g_ff2 = sum_a[:r_pool], sum_a[split_a + 3 * r :], sum_b[:r], sum_b[5 * r : 5 * r + r_ff2]
        g_qkv = unfold(sum_a[split_a : split_a + 3 * r], 3)
        g_ff1 = unfold(sum_b[r : 5 * r], 4)
        g_up = unfold(sum_b[5 * r + r_ff2 :], 3)
    (
        out_pool_b,
        out_ln1_gain,
        out_ln1_bias,
        out_u,
        out_v,
        out_ln2_gain,
        out_ln2_bias,
        out_ff2_b,
        out_ff1_b,
        out_up_b,
    ) = vec_out
    return (
        block_output,
        input_grad,
        g_pool,
        out_pool_b,
        out_ln1_gain,
        out_ln1_bias,
        g_qkv,
        out_u,
        out_v,
        g_pos,
        g_out,
        out_ln2_gain,
        out_ln2_bias,
        g_ff1,
        out_ff1_b,
        g_ff2,
        out_ff2_b,
        g_up,
        out_up_b,
    )


def solution(mesh):
    links = Links(mesh.shape["dp"], mesh.shape["fsdp"])
    rows = P(AXES, None)
    flat = P(AXES)
    ranks = (2, 1, 1, 2, 1, 1, 1, 2, 1, 1, 2, 2, 1, 1, 2, 1, 2, 1, 2, 1, 2)
    out_ranks = (2, 2, 2, 1, 1, 1, 2, 1, 1, 2, 2, 1, 1, 2, 1, 2, 1, 2, 1)
    return jax.shard_map(
        lambda *args: per_device(links, *args),
        mesh=mesh,
        in_specs=tuple(rows if k == 2 else flat for k in ranks),
        out_specs=tuple(rows if k == 2 else flat for k in out_ranks),
        check_vma=False,
    )
```

```python
import jax
import jax.numpy as jnp
from jax import lax
from jax.experimental import pallas as pl
from jax.experimental.pallas import tpu as pltpu
from jax.sharding import PartitionSpec as P

H = 8
DH = 64
QBLK = 256
AXES = ("dp", "fsdp")


eps_norm = 1e-05
big_negative = -1e30

F32 = jnp.float32
BF16 = jnp.bfloat16
BLOCKS = 32
PAIRS = 4
CH = 64
VMEM = pl.BlockSpec(memory_space=pltpu.VMEM)
SMEM = pl.BlockSpec(memory_space=pltpu.SMEM)
ANY = pl.BlockSpec(memory_space=pl.ANY)
GELU_C = 0.7978845608028654
ROWS_A = 128
ROWS_B = 192
ROWS_C = 48
VEC = slice(48, 64)


def mm(left, right, cl=1, cr=0):
    return lax.dot_general(left, right, (((cl,), (cr,)), ((), ())), preferred_element_type=F32)


def weight(ref, start, rows):
    block = ref[:, start : start + rows, :]
    return block.reshape(block.shape[0] * rows, block.shape[2])


def weight_ff2(ref, start, j):
    block = ref[8 * j : 8 * j + 8, start : start + 64, :]
    return block.reshape(512, block.shape[2])


def start_copy(source, dest, sem):
    copy = pltpu.make_async_copy(source, dest, sem)
    copy.start()
    return copy


def load_rows(me, plan, refs, dest, first, stop, sem):
    for (start, blocks), ref in zip(plan, refs):
        low, high = max(first, start), min(stop, start + ref.shape[1])
        if low < high:
            for k, (base, mask) in enumerate(blocks):
                pltpu.make_async_copy(
                    ref.at[k, pl.ds(low - start, high - low)],
                    dest.at[base + (me ^ mask), pl.ds(low, high - low)],
                    sem,
                ).start()


def wait_rows(dest, first, stop, sem):
    rows = dest.at[:, pl.ds(first, stop - first)]
    pltpu.make_async_copy(rows, rows, sem).wait()


def lane_half(shape, s):
    return (lax.broadcasted_iota(jnp.int32, shape, len(shape) - 1) // DH) == s


def norm_stats(x):
    width = x.shape[-1]
    mean = jnp.sum(x, axis=-1, keepdims=True) * (1.0 / width)
    centre = x - mean
    var = jnp.sum(centre * centre, axis=-1, keepdims=True) * (1.0 / width)
    rstd = lax.rsqrt(var + eps_norm)
    return centre * rstd, rstd


def norm_back(dy, xhat, rstd, gain):
    width = dy.shape[-1]
    d = dy * gain
    m1 = jnp.sum(d, axis=-1, keepdims=True) * (1.0 / width)
    m2 = jnp.sum(d * xhat, axis=-1, keepdims=True) * (1.0 / width)
    return rstd * (d - m1 - xhat * m2)


def forward_kernel(plan, n_pieces, me_ref, *refs):
    pieces = refs[:n_pieces]
    (grouped_hbm, item_col, item_row, sine_hbm, cosine_hbm, key_pos_hbm) = refs[
        n_pieces : n_pieces + 6
    ]
    hbm = refs[n_pieces + 6 : n_pieces + 14]
    vecs, w_out_hbm = refs[n_pieces + 14 : n_pieces + 16]
    (grouped, sine, cosine, pooled, normed, qu, qv, keys, vals, prob, ctx) = refs[
        n_pieces + 16 : n_pieces + 27
    ]
    (w, w_pos, bias, proj, qcat, kcat, tmp, scores, sem, sem2) = refs[n_pieces + 27 :]
    (pooled_hbm, normed_hbm, qu_hbm, qv_hbm, keys_hbm, vals_hbm, prob_hbm, ctx_hbm) = hbm
    me = me_ref[0]
    rows = grouped.shape[0]
    load_rows(me, plan, pieces, w, 0, 64, sem.at[0])
    get_grouped = start_copy(grouped_hbm, grouped, sem2.at[0])
    load_rows(me, plan, pieces, w, 64, ROWS_A, sem.at[1])
    get_sine = start_copy(sine_hbm, sine, sem2.at[1])
    get_cosine = start_copy(cosine_hbm, cosine, sem2.at[2])
    get_key_pos = start_copy(key_pos_hbm, kcat.at[:, 0:rows], sem2.at[3])
    for r in range(0, rows, CH):
        row = r + lax.broadcasted_iota(jnp.int32, (CH, rows), 0)
        col = lax.broadcasted_iota(jnp.int32, (CH, rows), 1)
        allowed = (item_col[r : r + CH, :] == item_row[...]) & (row >= col)
        bias[r : r + CH, :] = jnp.where(allowed, 0.0, big_negative)
    wait_rows(w, 0, 64, sem.at[0])
    get_grouped.wait()
    vec = jnp.sum(w[:, VEC, :].astype(F32), axis=0)
    vecs[...] = vec
    tmp[...] = mm(grouped[...], weight(w, 0, 48))
    for r in range(0, rows, CH):
        x = tmp[r : r + CH, :] + vec[0:1]
        pooled[r : r + CH, :] = x
        xhat, rstd = norm_stats(x)
        normed[r : r + CH, :] = (xhat * vec[1:2] + vec[2:3]).astype(BF16)
    wait_rows(w, 64, ROWS_A, sem.at[1])
    puts = [
        start_copy(w, w_out_hbm, sem2.at[4]),
        start_copy(pooled, pooled_hbm, sem2.at[5]),
        start_copy(normed, normed_hbm, sem2.at[6]),
    ]
    tmp[...] = mm(normed[...], weight(w, 64, 16))
    for r in range(0, rows, CH):
        x = tmp[r : r + CH, :]
        u = (x + vec[3:4]).astype(BF16)
        v = (x + vec[4:5]).astype(BF16)
        for p in range(PAIRS):
            qu[p, r : r + CH, :] = u[:, 128 * p : 128 * p + 128]
            qv[p, r : r + CH, :] = v[:, 128 * p : 128 * p + 128]
    x = mm(normed[...], weight(w, 80, 16)).astype(BF16)
    for p in range(PAIRS):
        keys[p] = x[:, 128 * p : 128 * p + 128]
    x = mm(normed[...], weight(w, 96, 16)).astype(BF16)
    for p in range(PAIRS):
        vals[p] = x[:, 128 * p : 128 * p + 128]
    x = weight(w, 112, 16)
    for p in range(PAIRS):
        w_pos[p] = x[:, 128 * p : 128 * p + 128]

    puts += [
        start_copy(x, y, sem2.at[7 + j])
        for j, (x, y) in enumerate(((qu, qu_hbm), (qv, qv_hbm), (keys, keys_hbm), (vals, vals_hbm)))
    ]
    get_sine.wait()
    get_cosine.wait()
    get_key_pos.wait()

    def put_prob(p):
        pair = pl.ds(2 * p, 2)
        return pltpu.make_async_copy(prob.at[pair], prob_hbm.at[pair], sem2.at[11])

    @pl.loop(0, PAIRS)
    def _(p):
        kcat[:, rows : rows + 128] = keys[p]
        zero = jnp.zeros((rows, 128), BF16)
        halves = [lane_half((rows, 128), s) for s in range(2)]

        def project(s):
            proj[s] = mm(jnp.where(halves[s], qv[p], zero), w_pos[p], 1, 1)

        def rotate(s):
            for r in range(0, rows, CH):
                a = proj[s, r : r + CH, 0:256]
                b = proj[s, r : r + CH, 256:512]
                si = sine[r : r + CH, :]
                co = cosine[r : r + CH, :]
                qcat[s, r : r + CH, 0:256] = (a * si + b * co).astype(BF16)
                qcat[s, r : r + CH, 256:512] = (b * si - a * co).astype(BF16)
            qcat[s, :, 512:640] = jnp.where(halves[s], qu[p], zero)

        def score(s, q):
            first, stop = q * QBLK, (q + 1) * QBLK
            scores[s, first:stop, 0:stop] = mm(qcat[s, first:stop, :], kcat[0:stop, :], 1, 1)

        def softmax(s, q):
            first, stop = q * QBLK, (q + 1) * QBLK
            for r in range(first, stop, CH):
                x = scores[s, r : r + CH, 0:stop] * (DH ** (-0.5)) + bias[r : r + CH, 0:stop]
                e = jnp.exp(x - jnp.max(x, axis=-1, keepdims=True))
                inv = 1.0 / jnp.sum(e, axis=-1, keepdims=True)
                prob[2 * p + s, r : r + CH, 0:stop] = (e * inv).astype(BF16)

        def context(s, q):
            first, stop = q * QBLK, (q + 1) * QBLK
            out = mm(prob[2 * p + s, first:stop, 0:stop], vals[p, 0:stop, :]).astype(BF16)
            if s == 1:
                out = jnp.where(lane_half((QBLK, 128), 1), out, ctx[p, first:stop, :])
            ctx[p, first:stop, :] = out

        project(0)
        project(1)
        rotate(0)
        score(0, 0)
        score(0, 1)
        rotate(1)
        softmax(0, 0)
        score(1, 0)
        score(1, 1)
        softmax(0, 1)
        context(0, 0)
        softmax(1, 0)
        context(0, 1)
        softmax(1, 1)
        context(1, 0)
        context(1, 1)
        put_prob(p).start()

    puts.append(start_copy(ctx, ctx_hbm, sem2.at[12]))
    pltpu.make_async_copy(prob, prob_hbm, sem2.at[11]).wait()
    for c in puts:
        c.wait()


def join(ref):
    return jnp.concatenate([ref[p] for p in range(PAIRS)], axis=1)


def store_blocks(grads, place_ref, line, grad, first, rows=16, start=0):
    for k in range(grad.shape[0] // rows):
        grads[place_ref[line, start + k], first : first + rows, :] = grad[k * rows : (k + 1) * rows].astype(BF16)


def put_blocks(grads, keep_hbm, send_hbm, first, stop, sem):
    rows = pl.ds(first, stop - first)
    half = BLOCKS // 2
    copies = []
    start = half
    for j, ref in enumerate(send_hbm):
        n = ref.shape[0]
        copies.append(start_copy(grads.at[pl.ds(start, n), rows], ref.at[:, rows], sem.at[1 + j]))
        start += n
    copies.append(start_copy(grads.at[pl.ds(0, half), rows], keep_hbm.at[:, rows], sem.at[0]))
    return copies


def middle_kernel(plan, n_pieces, me_ref, place_ref, *refs):
    pieces = refs[:n_pieces]
    (pooled_hbm, ctx_hbm, up_grad_hbm, vecs) = refs[n_pieces : n_pieces + 4]
    (res_grad_hbm, cg, short_out_hbm, vec_grads, w_up_hbm, keep_hbm, send_hbm) = refs[
        n_pieces + 4 : n_pieces + 11
    ]
    (pooled, ctx, up_grad, res_grad, short_out) = refs[n_pieces + 11 : n_pieces + 16]
    (w, grads, xhat, rstd, n2, hidden, pre, slope, acc, tmp, sgrad, bg, attn, sem, sem2, sem3) = refs[
        n_pieces + 16 :
    ]
    me = me_ref[0]
    rows = pooled.shape[0]
    load_rows(me, plan, pieces, w, 0, 80, sem.at[0])
    get_ctx = start_copy(ctx_hbm, ctx, sem2.at[0])
    get_pooled = start_copy(pooled_hbm, pooled, sem2.at[1])
    load_rows(me, plan, pieces, w, 80, 144, sem.at[1])
    load_rows(me, plan, pieces, w, 144, ROWS_B, sem.at[2])
    get_up_grad = start_copy(up_grad_hbm, up_grad, sem2.at[2])
    get_ctx.wait()
    get_pooled.wait()
    wait_rows(w, 0, 80, sem.at[0])
    gain2, bias2 = vecs[5:6, :], vecs[6:7, :]
    acc[...] = pooled[...] + mm(join(ctx), weight(w, 0, 16))
    for r in range(0, rows, CH):
        xh, rs = norm_stats(acc[r : r + CH, :])
        xhat[r : r + CH, :] = xh
        rstd[r : r + CH, :] = jnp.broadcast_to(rs, (CH, 128))
        n2[r : r + CH, :] = (xh * gain2 + bias2).astype(BF16)

    def first_layer(j):
        tmp[j] = mm(n2[...], weight(w, 16 + 16 * j, 16))

    def activate(j):
        b1 = vecs[8 + j : 9 + j, :]
        for r in range(0, rows, CH):
            x = tmp[j, r : r + CH, :] + b1
            x2 = x * x
            t = jnp.tanh(GELU_C * (x + 0.044715 * (x * x2)))
            hidden[r : r + CH, 512 * j : 512 * j + 512] = (0.5 * x * (1.0 + t)).astype(BF16)
            slope[j, r : r + CH, :] = 0.5 * (1.0 + t) + (0.5 * GELU_C) * x * (1.0 - t * t) * (
                1.0 + (3.0 * 0.044715) * x2
            )

    def up_back(j):
        return mm(up_grad[:, 512 * j : 512 * j + 512], weight(w, 144 + 16 * j, 16), 1, 1)

    def second_layer(j):
        return mm(hidden[:, 512 * j : 512 * j + 512], weight_ff2(w, 80, j))

    first_layer(0)
    first_layer(1)
    activate(0)
    wait_rows(w, 80, 144, sem.at[1])
    first_layer(2)
    activate(1)
    acc[...] += second_layer(0)
    first_layer(3)
    activate(2)
    acc[...] += second_layer(1)
    wait_rows(w, 144, ROWS_B, sem.at[2])
    get_up_grad.wait()
    sgrad[...] = up_back(0) + up_back(1)
    activate(3)
    acc[...] += second_layer(2)
    sgrad[...] += up_back(2)
    acc[...] += second_layer(3)
    bg[...] = sgrad[...].astype(BF16)
    short_out[...] = (acc[...] + vecs[7:8, :]).astype(BF16)
    puts = [
        start_copy(w.at[:, pl.ds(144, 48)], w_up_hbm, sem2.at[3]),
        start_copy(short_out, short_out_hbm, sem2.at[4]),
    ]

    def hidden_back(j):
        tmp[j] = mm(bg[...], weight_ff2(w, 80, j), 1, 1)

    def activate_back(j):
        total = jnp.zeros((1, 512), F32)
        for r in range(0, rows, CH):
            x = (tmp[j, r : r + CH, :] * slope[j, r : r + CH, :]).astype(BF16)
            pre[r : r + CH, 512 * j : 512 * j + 512] = x
            total = total + jnp.sum(x.astype(F32), axis=0, keepdims=True)
        vec_grads[8 + j : 9 + j, :] = total

    def up_weights(j):
        g = mm(short_out[...], up_grad[:, 512 * j : 512 * j + 512], 0, 0)
        store_blocks(grads, place_ref, 0, g, 144 + 16 * j)

    def second_weights(j):
        g = mm(hidden[:, 512 * j : 512 * j + 512], bg[...], 0, 0)
        store_blocks(grads, place_ref, 0, g, 80, 64, 8 * j)

    def first_weights(j):
        g = mm(n2[...], pre[:, 512 * j : 512 * j + 512], 0, 0)
        store_blocks(grads, place_ref, 0, g, 16 + 16 * j)

    def first_back(j):
        return mm(pre[:, 512 * j : 512 * j + 512], weight(w, 16 + 16 * j, 16), 1, 1)

    vec_grads[...] = jnp.zeros(vec_grads.shape, F32)
    hidden_back(0)
    hidden_back(1)
    activate_back(0)
    hidden_back(2)
    activate_back(1)
    acc[...] = first_back(0)
    hidden_back(3)
    activate_back(2)
    acc[...] += first_back(1)
    second_weights(0)
    activate_back(3)
    acc[...] += first_back(2)
    second_weights(1)
    acc[...] += first_back(3)
    second_weights(2)
    second_weights(3)
    dgain = jnp.zeros((1, 512), F32)
    dbias = jnp.zeros((1, 512), F32)
    for r in range(0, rows, CH):
        dy = acc[r : r + CH, :]
        xh = xhat[r : r + CH, :]
        dgain = dgain + jnp.sum(dy * xh, axis=0, keepdims=True)
        dbias = dbias + jnp.sum(dy, axis=0, keepdims=True)
        x = sgrad[r : r + CH, :] + norm_back(dy, xh, rstd[r : r + CH, 0:1], gain2)
        res_grad[r : r + CH, :] = x
        attn[r : r + CH, :] = x.astype(BF16)
    vec_grads[5:6, :] = dgain
    vec_grads[6:7, :] = dbias
    up_weights(0)
    up_weights(1)
    up_weights(2)
    puts += put_blocks(grads, keep_hbm, (send_hbm,), 80, ROWS_B, sem3.at[0])
    first_weights(0)
    first_weights(1)
    first_weights(2)
    first_weights(3)
    puts += put_blocks(grads, keep_hbm, (send_hbm,), 16, 80, sem3.at[1])
    for j in range(3):
        vec_grads[12 + j : 13 + j, :] = jnp.sum(
            up_grad[:, 512 * j : 512 * j + 512].astype(F32), axis=0, keepdims=True
        )
    vec_grads[7:8, :] = jnp.sum(bg[...].astype(F32), axis=0, keepdims=True)
    store_blocks(grads, place_ref, 0, mm(join(ctx), attn[...], 0, 0), 0)
    puts += put_blocks(grads, keep_hbm, (send_hbm,), 0, 16, sem3.at[2])
    puts.append(start_copy(res_grad, res_grad_hbm, sem2.at[5]))
    x = mm(attn[...], weight(w, 0, 16), 1, 1).astype(BF16)
    for p in range(PAIRS):
        cg[p] = x[:, 128 * p : 128 * p + 128]
    for c in puts:
        c.wait()


def tail_kernel(
    place_ref, prob, cg_hbm, vals_hbm, keys_hbm, qu_hbm, qv_hbm, key_pos_hbm, sine_hbm, cosine_hbm,
    normed_hbm, grouped_hbm, pooled_hbm, res_grad_hbm, vecs, vec_in, w_hbm,
    pg, w_pool_out, keep_hbm, send0, send1, send2, send3,
    cg, vals, keys, qu, qv, key_pos, sine, cosine, normed, grouped, pooled, res_grad,
    w_pos, pgrad, sg, posg, qg, qkvg, pos_w_grad, w, grads, acc, vec, prob_v, sem, prob_sem, get_sem,
):
    rows = key_pos.shape[0]
    n_q = rows // QBLK
    pairs = ((cg_hbm, cg), (vals_hbm, vals), (keys_hbm, keys), (qu_hbm, qu), (qv_hbm, qv))
    first_gets = [start_copy(x, y, get_sem.at[j]) for j, (x, y) in enumerate(pairs)]

    def fetch(p):
        return pltpu.make_async_copy(prob.at[pl.ds(2 * p, 2)], prob_v.at[p % 2], prob_sem.at[p % 2])

    fetch(0).start()
    tables = ((key_pos_hbm, key_pos), (sine_hbm, sine), (cosine_hbm, cosine))
    first_gets += [start_copy(x, y, get_sem.at[5 + j]) for j, (x, y) in enumerate(tables)]
    load = start_copy(w_hbm.at[:, pl.ds(112, 16)], w.at[:, pl.ds(112, 16)], sem.at[0])
    late = ((normed_hbm, normed), (grouped_hbm, grouped), (pooled_hbm, pooled), (res_grad_hbm, res_grad))
    late_gets = [start_copy(x, y, get_sem.at[8 + j]) for j, (x, y) in enumerate(late)]
    late_gets.append(start_copy(w_hbm.at[:, pl.ds(0, 112)], w.at[:, pl.ds(0, 112)], get_sem.at[12]))
    vec[...] = vec_in[...]
    load.wait()
    for c in first_gets:
        c.wait()
    x = weight(w, 112, 16)
    for p in range(PAIRS):
        w_pos[p] = x[:, 128 * p : 128 * p + 128]

    @pl.loop(0, PAIRS)
    def _(p):
        @pl.when(p + 1 < PAIRS)
        def _():
            fetch(p + 1).start()

        fetch(p).wait()
        slot = p % 2
        u_sums = []
        v_sums = []
        for s in range(2):
            half = lane_half((rows, 128), s)
            zero = jnp.zeros((rows, 128), BF16)
            cgm = jnp.where(half, cg[p], zero)
            qum = jnp.where(half, qu[p], zero)
            qvm = jnp.where(half, qv[p], zero)
            for q in range(n_q):
                first, stop = q * QBLK, (q + 1) * QBLK
                pgrad[first:stop, 0:stop] = mm(cgm[first:stop], vals[p, 0:stop, :], 1, 1)
                for r in range(first, stop, CH):
                    pr = prob_v[slot, s, r : r + CH, 0:stop].astype(F32)
                    t = pr * pgrad[r : r + CH, 0:stop]
                    inner = jnp.sum(t, axis=-1, keepdims=True)
                    sg[r : r + CH, 0:stop] = ((t - pr * inner) * (DH ** (-0.5))).astype(BF16)
                posg[first:stop, :] = mm(sg[first:stop, 0:stop], key_pos[0:stop, :])
                part = mm(sg[first:stop, 0:stop], keys[p, 0:stop, :])
                if s == 0:
                    qg[p, first:stop, :] = part
                else:
                    qg[p, first:stop, :] = jnp.where(
                        lane_half((QBLK, 128), 1), part, qg[p, first:stop, :]
                    )
                kg = mm(sg[first:stop, 0:stop], qum[first:stop], 0, 0)
                vg = mm(prob_v[slot, s, first:stop, 0:stop], cgm[first:stop], 0, 0)
                if s == 0 and q == 0:
                    qg[PAIRS + p] = jnp.zeros((rows, 128), F32)
                    qg[2 * PAIRS + p] = jnp.zeros((rows, 128), F32)
                qg[PAIRS + p, 0:stop, :] += kg
                qg[2 * PAIRS + p, 0:stop, :] += vg
            for r in range(0, rows, CH):
                a = posg[r : r + CH, 0:256]
                b = posg[r : r + CH, 256:512]
                si = sine[r : r + CH, :]
                co = cosine[r : r + CH, :]
                sg[r : r + CH, 0:256] = (a * si - b * co).astype(BF16)
                sg[r : r + CH, 256:512] = (a * co + b * si).astype(BF16)
            gw = mm(sg[...], qvm, 0, 0)
            if s == 0:
                pos_w_grad[p] = gw
            else:
                pos_w_grad[p] += gw
            qvg = jnp.where(half, mm(sg[...], w_pos[p]), 0.0)
            v_sums.append(jnp.sum(qvg, axis=0, keepdims=True))
            u_sums.append(jnp.sum(jnp.where(half, qg[p], 0.0), axis=0, keepdims=True))
            qg[p] += qvg
        u_row = u_sums[0] + u_sums[1]
        v_row = v_sums[0] + v_sums[1]
        for k in range(PAIRS):

            @pl.when(p == k)
            def _():
                vec[3:4, 128 * k : 128 * k + 128] = u_row
                vec[4:5, 128 * k : 128 * k + 128] = v_row

    for c in late_gets:
        c.wait()
    for j in range(3):
        for p in range(PAIRS):
            qkvg[j, :, 128 * p : 128 * p + 128] = qg[PAIRS * j + p].astype(BF16)
    for j in range(3):
        store_blocks(grads, place_ref, 1, mm(normed[...], qkvg[j], 0, 0), 64 + 16 * j)
    store_blocks(grads, place_ref, 1, join(pos_w_grad), 112)
    sends = (send0, send1, send2, send3)
    puts = put_blocks(grads, keep_hbm, sends, 64, ROWS_A, sem.at[pl.ds(2, 5)])
    keep_pool = pltpu.make_async_copy(w.at[:, 0:48], w_pool_out, sem.at[1])
    keep_pool.start()
    acc[...] = (
        mm(qkvg[0], weight(w, 64, 16), 1, 1)
        + mm(qkvg[1], weight(w, 80, 16), 1, 1)
        + mm(qkvg[2], weight(w, 96, 16), 1, 1)
    )
    gain1 = vecs[1:2, :]
    dgain = jnp.zeros((1, 512), F32)
    dbias = jnp.zeros((1, 512), F32)
    dpool = jnp.zeros((1, 512), F32)
    for r in range(0, rows, CH):
        dy = acc[r : r + CH, :]
        xh, rs = norm_stats(pooled[r : r + CH, :])
        dgain = dgain + jnp.sum(dy * xh, axis=0, keepdims=True)
        dbias = dbias + jnp.sum(dy, axis=0, keepdims=True)
        x = (res_grad[r : r + CH, :] + norm_back(dy, xh, rs, gain1)).astype(BF16)
        pg[r : r + CH, :] = x
        dpool = dpool + jnp.sum(x.astype(F32), axis=0, keepdims=True)
    vec[0:1, :] = dpool
    vec[1:2, :] = dgain
    vec[2:3, :] = dbias
    table = vec[...].astype(BF16)
    for d in range(BLOCKS):
        grads[place_ref[1, d], VEC, :] = table
    for j in range(3):
        g = mm(grouped[:, 512 * j : 512 * j + 512], pg[...], 0, 0)
        for k in range(32):
            granule = 32 * j + k
            d, sub = granule // 3, granule % 3
            grads[place_ref[1, d], 16 * sub : 16 * sub + 16, :] = g[16 * k : 16 * k + 16].astype(BF16)
    puts += put_blocks(grads, keep_hbm, sends, 0, 64, sem.at[pl.ds(7, 5)])
    keep_pool.wait()
    for c in puts:
        c.wait()


def bytes_kernel(emb, cot, cols, short_out, w_up, vecs, pg, w_pool, out, grad, tmp):
    rows = emb.shape[0]
    for j in range(3):
        tmp[...] = mm(short_out[...], weight(w_up, 16 * j, 16))
        up_bias = vecs[12 + j : 13 + j, :]
        for r in range(0, rows, CH):
            x = emb[r : r + CH, 512 * j : 512 * j + 512].astype(F32) + tmp[r : r + CH, :] + up_bias
            out[r : r + CH, 512 * j : 512 * j + 512] = jnp.where(
                cols[r : r + CH, j : j + 1] > 0, x, 0.0
            ).astype(BF16)
    pool = weight(w_pool, 0, 48)
    for j in range(3):
        src = (j + 2) % 3
        tmp[...] = mm(pg[...], pool[512 * src : 512 * src + 512, :], 1, 1)
        if j > 0:
            tmp[...] = pltpu.roll(tmp[...], rows - 1, 0)
        for r in range(0, rows, CH):
            x = tmp[r : r + CH, :]
            if j > 0:
                x = jnp.where(cols[r : r + CH, 3:4] > 0, x, 0.0)
            x = cot[r : r + CH, 512 * j : 512 * j + 512].astype(F32) + x
            grad[r : r + CH, 512 * j : 512 * j + 512] = jnp.where(
                cols[r : r + CH, j : j + 1] > 0, x, 0.0
            ).astype(BF16)


def pack_kernel(me_ref, *refs):
    (w_pool, w_qkv, w_pos, w_out, w_ff1, w_ff2, w_up) = refs[:7]
    vectors = refs[7:17]
    all_a, all_b, out_c, out_a, out_b, sem = refs[17:]
    me = me_ref[0]
    out_a[0:48, :] = w_pool[...]
    for j in range(3):
        out_a[64 + 16 * j : 80 + 16 * j, :] = w_qkv[:, 512 * j : 512 * j + 512]
        out_c[0, 16 * j : 16 + 16 * j, :] = w_up[:, 512 * j : 512 * j + 512]
    out_a[112:128, :] = w_pos[...]
    out_b[0:16, :] = w_out[...]
    for j in range(4):
        out_b[16 + 16 * j : 32 + 16 * j, :] = w_ff1[:, 512 * j : 512 * j + 512]
    out_b[80:144, :] = w_ff2[...]

    def spread(x, first):
        k = x.shape[1]
        lane = first + lax.broadcasted_iota(jnp.int32, (k, 512), 1)
        row = lax.broadcasted_iota(jnp.int32, (k, 512), 0)
        pick = jnp.where(lane % k == row, 1.0, 0.0).astype(BF16)
        own = (first + lax.broadcasted_iota(jnp.int32, (x.shape[0], 512), 1)) // k == me
        return jnp.where(own, mm(x, pick), 0.0)

    lines = [spread(v[...], 0) for v in vectors[:8]]
    lines += [spread(vectors[8][...], 512 * j) for j in range(4)]
    lines += [spread(vectors[9][...], 512 * j) for j in range(3)]
    lines.append(jnp.zeros((1, 512), F32))
    out_a[VEC, :] = jnp.concatenate(lines, axis=0).astype(BF16)
    copies = []
    for j in range(all_a.shape[0]):
        copies.append(pltpu.make_async_copy(out_a, all_a.at[j], sem.at[j]))
    for j in range(all_b.shape[0]):
        copies.append(pltpu.make_async_copy(out_b, all_b.at[j], sem.at[all_a.shape[0] + j]))
    for c in copies:
        c.start()
    for c in copies:
        c.wait()


def finish_b_kernel(*refs):
    out, ff1, up, ff2 = refs[-4:]
    total = refs[0][0].astype(F32)
    for ref in refs[1:-4]:
        total = total + ref[0].astype(F32)
    out[...] = total[0:16]
    for j in range(4):
        ff1[:, 512 * j : 512 * j + 512] = total[16 + 16 * j : 32 + 16 * j]
    for j in range(3):
        up[:, 512 * j : 512 * j + 512] = total[144 + 16 * j : 160 + 16 * j]
    ff2[...] = total[80:144]


def finish_a_kernel(me_ref, *refs):
    me = me_ref[0]
    parts, (pool, qkv, pos), vectors = refs[:-13], refs[-13:-10], refs[-10:]
    total = parts[0][0].astype(F32)
    for ref in parts[1:]:
        total = total + ref[0].astype(F32)
    pool[...] = total[0:48]
    for j in range(3):
        qkv[:, 512 * j : 512 * j + 512] = total[64 + 16 * j : 80 + 16 * j]
    pos[...] = total[112:128]
    table = total[VEC]
    lines = pltpu.roll(table[0:8], 512 - 16 * me, 1)
    for j in range(8):
        vectors[j][...] = lines[j : j + 1, 0:16]
    row = lax.broadcasted_iota(jnp.int32, (16, 512), 0)

    def line(j):
        return jnp.sum(jnp.where(row == j, table, 0.0), axis=0, keepdims=True)

    def part(first, length):
        j, off = first // 512, first % 512
        here = pltpu.roll(jnp.broadcast_to(line(j), (8, 512)), 512 - off, 1)
        there = pltpu.roll(jnp.broadcast_to(line(j + 1), (8, 512)), 512 - off, 1)
        lane = lax.broadcasted_iota(jnp.int32, (8, 512), 1)
        return jnp.where(lane < 512 - off, here, there)[0:1, 0:length]

    vectors[8][...] = part(8 * 512 + 64 * me, 64)
    vectors[9][...] = part(12 * 512 + 48 * me, 48)


class Links:
    def __init__(self, dp, fsdp):
        self.dp = dp
        self.fsdp = fsdp
        self.count = dp * fsdp
        self.near = [2 * m for m in range(fsdp // 2)]

    def send(self, values, mask):
        return lax.ppermute(values, AXES, [(i, i ^ mask) for i in range(self.count)])

    def deep(self, blocks):
        return lax.all_to_all(blocks, "dp", 0, 0, tiled=True)

    def gather_near(self, held):
        return [held] + [self.send(held, m) for m in self.near[1:]]

    def gather_core(self, pieces):
        return pieces + [
            (first, [(z, m ^ 1) for z, m in blocks], self.send(array, 1)) for first, blocks, array in pieces
        ]

    def near_pieces(self, first, near):
        return [(first, [(z, m) for z in range(self.dp)], x) for m, x in zip(self.near, near)]

    def places(self, me, by_place, by_plane):
        owner = jnp.arange(self.count, dtype=jnp.int32)
        place = (owner if by_place else owner ^ me) % self.fsdp // 2
        plane = (owner if by_plane else owner ^ me) // self.fsdp
        return ((owner ^ me) % 2 * (self.fsdp // 2) + place) * self.dp + plane

    def start_deep(self, blocks):
        return [blocks[:1]] + [
            self.send(blocks[m : m + 1], self.fsdp * m) for m in range(1, self.dp)
        ]

    def split_core(self, keep, got):
        n = self.dp
        return [
            add(keep[k * n : k * n + n], got[k]).astype(BF16)
            for k in range(len(self.near))
        ]

    def start_near(self, totals):
        return totals[:1] + [self.send(t, m) for t, m in zip(totals[1:], self.near[1:])]

    def swap_near(self, blocks):
        groups = [list(range(c, self.fsdp, 2)) for c in range(2)]
        return lax.all_to_all(blocks, "fsdp", 0, 0, axis_index_groups=groups, tiled=True)

    def total_core(self, keep, got):
        outs = []
        first = 0
        for x in got:
            outs.append(add(keep[first : first + x.shape[0]], x).astype(BF16))
            first += x.shape[0]
        return jnp.concatenate(outs, axis=0) if len(outs) > 1 else outs[0]

    def total_near(self, parts):
        if not isinstance(parts, list):
            parts = [parts[k : k + self.dp] for k in range(0, parts.shape[0], self.dp)]
        total = parts[0].astype(F32)
        for x in parts[1:]:
            total = total + x.astype(F32)
        return total.astype(BF16)

    def total_deep(self, parts):
        return jnp.sum(parts.astype(F32), axis=0)

    def reduce(self, keep, send):
        near = self.swap_near(self.total_core(keep, [self.send(send, 1)]))
        return self.total_deep(self.deep(self.total_near(near)))


def add(left, right):
    return left.astype(F32) + right.astype(F32)


def cost(us):
    return pl.CostEstimate(flops=us * 10**9, transcendentals=0, bytes_accessed=us * 10**6)


def add(left, right):
    return left.astype(F32) + right.astype(F32)


def fold(shard, width):
    return jnp.concatenate(
        [shard[..., j : j + width] for j in range(0, shard.shape[-1], width)], axis=-2
    )


def unfold(block, count):
    rows = block.shape[-2] // count
    return jnp.concatenate(
        [block[..., j * rows : (j + 1) * rows, :] for j in range(count)], axis=-1
    )


def reblock(blocks, layout, count):
    m = blocks.shape[0]
    outs = []
    for first, rows, k in layout:
        x = unfold(blocks[:, first : first + rows], k)
        x = x.reshape(m * x.shape[1], x.shape[2]).reshape(count, -1, x.shape[2])
        outs.append(fold(x, blocks.shape[2]))
    return jnp.concatenate(outs, axis=1)


def layout_of(parts):
    out = []
    first = 0
    for rows, k in parts:
        out.append((first, rows, k))
        first += rows
    return out


def per_device(links, *args):
    (
        byte_embeddings,
        byte_item,
        byte_mask,
        w_pool,
        b_pool,
        ln1_gain,
        ln1_bias,
        w_qkv,
        pos_u,
        pos_v,
        w_pos,
        w_out,
        ln2_gain,
        ln2_bias,
        w_ff1,
        b_ff1,
        w_ff2,
        b_ff2,
        w_up,
        b_up,
        cotangent,
    ) = args
    n_dev = links.count
    me = lax.axis_index(AXES).astype(jnp.int32)
    width = w_pos.shape[1]
    r_pool, r, r_ff2 = w_pool.shape[0], w_pos.shape[0], w_ff2.shape[0]
    direct = n_dev == BLOCKS
    vectors = [b_pool, ln1_gain, ln1_bias, pos_u, pos_v, ln2_gain, ln2_bias, b_ff2, b_ff1, b_up]
    lengths = [v.shape[0] for v in vectors]
    vec_rows = [v * n_dev // width for v in lengths]
    vec_first = [sum(vec_rows[:i]) for i in range(len(vec_rows))]

    params = pltpu.CompilerParams(vmem_limit_bytes=60 << 20)
    sds = jax.ShapeDtypeStruct
    if direct:
        shard_a, shard_b, shard_c = pl.pallas_call(
            pack_kernel,
            out_shape=(
                sds((links.dp, ROWS_A, width), BF16),
                sds((links.dp, ROWS_B - ROWS_C, width), BF16),
                sds((1, ROWS_C, width), BF16),
            ),
            in_specs=[SMEM] + [VMEM] * 17,
            out_specs=[ANY] * 2 + [VMEM],
            scratch_shapes=[
                pltpu.VMEM((ROWS_A, width), BF16),
                pltpu.VMEM((ROWS_B - ROWS_C, width), BF16),
                pltpu.SemaphoreType.DMA((2 * links.dp,)),
            ],
            compiler_params=params,
            cost_estimate=cost(3),
        name="pack",
        )(me[None], w_pool, w_qkv, w_pos, w_out, w_ff1, w_ff2, w_up, *[v[None] for v in vectors])
    else:
        flat = jnp.arange(n_dev * lengths[8])
        table = []
        for v in vectors:
            k = v.shape[0]
            spread = jnp.where(flat[: n_dev * k] // k == me, jnp.tile(v, n_dev), jnp.zeros((), v.dtype))
            table.append(spread.reshape(-1, width))
        table.append(jnp.zeros((16 - sum(vec_rows), width), BF16))
        shard_a = jnp.concatenate([w_pool] + table + [fold(w_qkv, width), w_pos], axis=0)
        shard_b = jnp.concatenate([w_out, fold(w_ff1, width), w_ff2], axis=0)
        shard_c = fold(w_up, width)[None]
        shard_a, shard_b = [
            jnp.broadcast_to(x[None], (links.dp,) + x.shape) for x in (shard_a, shard_b)
        ]
    split_a = r_pool + 16
    byte_total = byte_embeddings.shape[0]
    rows = byte_total // 3
    emb = byte_embeddings.reshape(rows, 3 * width)
    cot = cotangent.reshape(rows, 3 * width)
    mask3 = byte_mask.reshape(rows, 3)
    item = byte_item.reshape(rows, 3)[:, 0]
    same = item[1:] == item[:-1]
    no = jnp.zeros((1,), jnp.bool_)
    same_before = jnp.concatenate([no, same])[:, None]
    same_after = jnp.concatenate([same, no])[:, None]
    cols = jnp.concatenate([mask3, same_after.astype(jnp.int32)], axis=1)
    item_f = item.astype(F32)
    live = [mask3[:, j : j + 1] > 0 for j in range(3)]
    zero = jnp.zeros((), jnp.bfloat16)
    masked = [jnp.where(live[j], emb[:, j * width : (j + 1) * width], zero) for j in range(3)]
    up_grad = jnp.concatenate(
        [jnp.where(live[j], cot[:, j * width : (j + 1) * width], zero) for j in range(3)], axis=1
    )

    def down(x):
        moved = jnp.concatenate([jnp.zeros((1, width), x.dtype), x[:-1]], axis=0)
        return jnp.where(same_before, moved, zero)

    grouped = jnp.concatenate([down(masked[1]), down(masked[2]), masked[0]], axis=1)
    places = jnp.arange(rows).astype(F32)
    frequency = 10000.0 ** (-(2.0 * jnp.arange(width // 2).astype(F32)) / width)
    angles = places[:, None] * frequency[None, :]
    sine, cosine = jnp.sin(angles), jnp.cos(angles)
    key_pos = jnp.concatenate([cosine, sine], axis=1).astype(BF16)

    held_a = links.deep(shard_a)
    held_c = jnp.concatenate(links.gather_near(shard_c), axis=0)
    item_col, item_row = item_f[:, None], item_f[None, :]
    if direct:
        place = jnp.stack([links.places(me, True, False), links.places(me, False, False)])
    else:
        place = jnp.tile(jnp.arange(BLOCKS, dtype=jnp.int32)[None], (2, 1))
    held_a, held_c, shard_b = lax.optimization_barrier((held_a, held_c, shard_b))
    near_a = links.gather_near(held_a)
    given = (emb, cot, cols, up_grad, grouped, sine, cosine, key_pos, item_col, item_row, place)
    near_a, given = lax.optimization_barrier((near_a, given))
    emb, cot, cols, up_grad, grouped, sine, cosine, key_pos, item_col, item_row, place = given
    pieces_a = links.gather_core(links.near_pieces(0, near_a))
    held_b = links.deep(shard_b)
    grouped, held_b = lax.optimization_barrier((grouped, held_b))
    near_b = links.gather_near(held_b)
    copies_c = jnp.concatenate([held_c] * links.dp, axis=0)
    last = pieces_a[-1]
    copies_c, array = lax.optimization_barrier((copies_c, last[2]))
    pieces_a[-1] = last[:2] + (array,)
    deep_c = links.deep(copies_c)
    layout_a = layout_of([(r_pool, 1), (16, 0), (3 * r, 3), (r, 1)])
    layout_b = layout_of([(r, 1), (4 * r, 4), (r_ff2, 1), (3 * r, 3)])
    layout_a32 = layout_of([(48, 1), (16, 0), (48, 3), (16, 1)])
    layout_b32 = layout_of([(16, 1), (64, 4), (64, 1), (48, 3)])

    if direct:
        base = (me % links.fsdp)[None]
    else:

        def canonical(pieces, layout):
            lines = {}
            for first, blocks, array in pieces:
                for j, (z, m) in enumerate(blocks):
                    lines.setdefault(first, {})[m, z] = array[j]
            parts = []
            for first in sorted(lines):
                arr = jnp.stack(
                    [jnp.stack([lines[first][m, z] for m in range(links.fsdp)]) for z in range(links.dp)]
                )
                arr = jnp.take(arr, jnp.arange(links.fsdp) ^ (me % links.fsdp), axis=1)
                parts.append(arr.reshape((n_dev,) + arr.shape[2:]))
            blocks = jnp.concatenate(parts, axis=1)
            outs = []
            for first, rows_, k in layout:
                if k == 0:
                    total = jnp.sum(blocks[:, first : first + rows_].astype(F32), axis=0)
                    outs.append(
                        jnp.concatenate(
                            [total[None], jnp.zeros((BLOCKS - 1,) + total.shape, F32)], axis=0
                        ).astype(BF16)
                    )
                else:
                    outs.append(reblock(blocks, [(first, rows_, k)], BLOCKS))
            return [(0, [(d, 0) for d in range(BLOCKS)], jnp.concatenate(outs, axis=1))]

        pieces_a = canonical(pieces_a, layout_a)
        base = jnp.zeros((1,), jnp.int32)

    pair_bf = sds((PAIRS, rows, 128), BF16)
    pair_f = sds((PAIRS, rows, 128), F32)
    square = sds((rows, width), F32)
    table_f = sds((16, width), F32)

    step = links.fsdp if direct else 1
    plan_a = [(first, [(z * step, m) for z, m in blocks]) for first, blocks, _ in pieces_a]
    n_a = len(plan_a)
    forward = pl.pallas_call(
        lambda *refs: forward_kernel(plan_a, n_a, *refs),
        out_shape=(
            square,
            sds((rows, width), BF16),
            pair_bf,
            pair_bf,
            pair_bf,
            pair_bf,
            sds((H, rows, rows), BF16),
            pair_bf,
            table_f,
            sds((BLOCKS, ROWS_A, width), BF16),
        ),
        in_specs=[SMEM] + [ANY] * n_a + [ANY, VMEM, VMEM, ANY, ANY, ANY],
        out_specs=[ANY] * 8 + [VMEM, ANY],
        scratch_shapes=[
            pltpu.VMEM((rows, 3 * width), BF16),
            pltpu.VMEM((rows, width // 2), F32),
            pltpu.VMEM((rows, width // 2), F32),
            pltpu.VMEM((rows, width), F32),
            pltpu.VMEM((rows, width), BF16),
        ]
        + [pltpu.VMEM((PAIRS, rows, 128), BF16)] * 4
        + [
            pltpu.VMEM((H, rows, rows), BF16),
            pltpu.VMEM((PAIRS, rows, 128), BF16),
            pltpu.VMEM((BLOCKS, ROWS_A, width), BF16),
            pltpu.VMEM((PAIRS, width, 128), BF16),
            pltpu.VMEM((rows, rows), F32),
            pltpu.VMEM((2, rows, width), F32),
            pltpu.VMEM((2, rows, width + 128), BF16),
            pltpu.VMEM((rows, width + 128), BF16),
            pltpu.VMEM((rows, width), F32),
            pltpu.VMEM((2, rows, rows), F32),
            pltpu.SemaphoreType.DMA((2,)),
            pltpu.SemaphoreType.DMA((13,)),
        ],
        compiler_params=params,
        cost_estimate=cost(20),
        name="forward",
    )
    pooled, normed, qu, qv, keys, vals, prob, ctx, vecs, wa = forward(base, *[a for _, _, a in pieces_a], grouped, item_col, item_row, sine, cosine, key_pos)
    pooled, near_b, deep_c = lax.optimization_barrier((pooled, near_b, deep_c))
    blocks_c = [(z, m) for z in range(links.dp) for m in links.near]
    pieces_b = links.gather_core(links.near_pieces(0, near_b) + [(shard_b.shape[1], blocks_c, deep_c)])
    if not direct:
        pieces_b = canonical(pieces_b, layout_b)

    plan_b = [(first, [(z * step, m) for z, m in blocks]) for first, blocks, _ in pieces_b]
    n_b = len(plan_b)
    half = BLOCKS // 2
    res_grad, cg, short_out, vec_grads, w_up_abs, keep_b, *send_b = pl.pallas_call(
        lambda *refs: middle_kernel(plan_b, n_b, *refs),
        out_shape=(
            square,
            pair_bf,
            sds((rows, width), BF16),
            table_f,
            sds((BLOCKS, 48, width), BF16),
            sds((half, ROWS_B, width), BF16),
        )
        + (sds((half, ROWS_B, width), BF16),),
        in_specs=[SMEM, SMEM] + [ANY] * n_b + [ANY, ANY, ANY, VMEM],
        out_specs=[ANY, VMEM, ANY, VMEM] + [ANY] * 3,
        scratch_shapes=[
            pltpu.VMEM((rows, width), F32),
            pltpu.VMEM((PAIRS, rows, 128), BF16),
            pltpu.VMEM((rows, 3 * width), BF16),
            pltpu.VMEM((rows, width), F32),
            pltpu.VMEM((rows, width), BF16),
            pltpu.VMEM((BLOCKS, ROWS_B, width), BF16),
            pltpu.VMEM((BLOCKS, ROWS_B, width), BF16),
            pltpu.VMEM((rows, width), F32),
            pltpu.VMEM((rows, 128), F32),
            pltpu.VMEM((rows, width), BF16),
            pltpu.VMEM((rows, 4 * 512), BF16),
            pltpu.VMEM((rows, 4 * 512), BF16),
            pltpu.VMEM((4, rows, 512), F32),
            pltpu.VMEM((rows, width), F32),
            pltpu.VMEM((4, rows, width), F32),
            pltpu.VMEM((rows, width), F32),
            pltpu.VMEM((rows, width), BF16),
            pltpu.VMEM((rows, width), BF16),
            pltpu.SemaphoreType.DMA((3,)),
            pltpu.SemaphoreType.DMA((6,)),
            pltpu.SemaphoreType.DMA((3, 2)),
        ],
        compiler_params=params,
        cost_estimate=cost(20),
        name="middle",
    )(base, place, *[a for _, _, a in pieces_b], pooled, ctx, up_grad, vecs)

    if direct:
        total_b = links.total_core(keep_b, [links.send(x, 1) for x in send_b])
        cg, total_b = lax.optimization_barrier((cg, total_b))
        near_b = links.swap_near(total_b)

    pooled_grad, w_pool_abs, keep_a, *send_a = pl.pallas_call(
        tail_kernel,
        out_shape=(
            sds((rows, width), BF16),
            sds((BLOCKS, 48, width), BF16),
            sds((half, ROWS_A, width), BF16),
        )
        + (sds((half // 4, ROWS_A, width), BF16),) * 4,
        in_specs=[SMEM] + [ANY] * 13 + [VMEM] * 2 + [ANY],
        out_specs=[VMEM] + [ANY] * 6,
        scratch_shapes=[pltpu.VMEM((PAIRS, rows, 128), BF16)] * 5
        + [
            pltpu.VMEM((rows, width), BF16),
            pltpu.VMEM((rows, width // 2), F32),
            pltpu.VMEM((rows, width // 2), F32),
            pltpu.VMEM((rows, width), BF16),
            pltpu.VMEM((rows, 3 * width), BF16),
            pltpu.VMEM((rows, width), F32),
            pltpu.VMEM((rows, width), F32),
            pltpu.VMEM((PAIRS, width, 128), BF16),
            pltpu.VMEM((rows, width), F32),
            pltpu.VMEM((rows, rows), BF16),
            pltpu.VMEM((rows, width), F32),
            pltpu.VMEM((3 * PAIRS, rows, 128), F32),
            pltpu.VMEM((3, rows, width), BF16),
            pltpu.VMEM((PAIRS, width, 128), F32),
            pltpu.VMEM((BLOCKS, ROWS_A, width), BF16),
            pltpu.VMEM((BLOCKS, ROWS_A, width), BF16),
            pltpu.VMEM((rows, width), F32),
            pltpu.VMEM((16, width), F32),
            pltpu.VMEM((2, 2, rows, rows), BF16),
            pltpu.SemaphoreType.DMA((12,)),
            pltpu.SemaphoreType.DMA((2,)),
            pltpu.SemaphoreType.DMA((13,)),
        ],
        compiler_params=params,
        cost_estimate=cost(27),
        name="tail",
    )(
        place, prob, cg, vals, keys, qu, qv, key_pos, sine, cosine, normed, grouped, pooled, res_grad, vecs,
        vec_grads, wa,
    )
    if direct:
        got_a = [links.send(x, 1) for x in send_a]
        totals_a = links.split_core(keep_a, got_a)
    out3, grad3 = pl.pallas_call(
        bytes_kernel,
        out_shape=(sds((rows, 3 * width), BF16), sds((rows, 3 * width), BF16)),
        in_specs=[VMEM] * 8,
        out_specs=[VMEM] * 2,
        scratch_shapes=[pltpu.VMEM((rows, width), F32)],
        compiler_params=params,
        cost_estimate=cost(1),
        name="bytes",
    )(emb, cot, cols, short_out, w_up_abs, vecs, pooled_grad, w_pool_abs)
    if direct:
        totals_a, near_b, out3, grad3 = lax.optimization_barrier((totals_a, near_b, out3, grad3))
        near_a = links.start_near(totals_a)
        deep_b = links.start_deep(links.total_near(near_b))
    block_output = out3.reshape(byte_total, width)
    input_grad = grad3.reshape(byte_total, width)

    if direct:
        near_a, deep_b = lax.optimization_barrier((near_a, deep_b))
        deep_a = links.start_deep(links.total_near(near_a))
        g_out, g_ff1, g_up, g_ff2 = pl.pallas_call(
            finish_b_kernel,
            out_shape=tuple(sds(w.shape, F32) for w in (w_out, w_ff1, w_up, w_ff2)),
            in_specs=[VMEM] * links.dp,
            out_specs=[VMEM] * 4,
            compiler_params=params,
            name="finish_b",
        )(*deep_b)
        g_pool, g_qkv, g_pos, *vec_out = pl.pallas_call(
            finish_a_kernel,
            out_shape=tuple(sds(w.shape, F32) for w in (w_pool, w_qkv, w_pos))
            + tuple(sds((1, n), F32) for n in lengths),
            in_specs=[SMEM] + [VMEM] * links.dp,
            out_specs=[VMEM] * 13,
            compiler_params=params,
            name="finish_a",
        )(me[None], *deep_a)
        vec_out = [v.reshape(-1) for v in vec_out]
    else:

        def owned(keep, send, layout):
            blocks = jnp.concatenate([keep, *send], axis=0)
            outs = []
            for first, rows_, k in layout:
                if k == 0:
                    outs.append(jnp.tile(blocks[:1, first : first + rows_], (n_dev, 1, 1)))
                else:
                    outs.append(reblock(blocks, [(first, rows_, k)], n_dev))
            full = jnp.concatenate(outs, axis=1)
            full = jnp.zeros_like(full).at[links.places(me, True, True)].set(full)
            return links.reduce(full[: n_dev // 2], full[n_dev // 2 :])

        sum_b = owned(keep_b, send_b, layout_b32)
        sum_a = owned(keep_a, send_a, layout_a32)
        vec_sum = sum_a[r_pool : r_pool + 16]
        vec_out = []
        for first, k, n in zip(vec_first, lengths, vec_rows):
            line = vec_sum[first : first + n].reshape(-1)
            vec_out.append(lax.dynamic_slice(line, (me * k,), (k,)))
        g_pool, g_pos, g_out, g_ff2 = sum_a[:r_pool], sum_a[split_a + 3 * r :], sum_b[:r], sum_b[5 * r : 5 * r + r_ff2]
        g_qkv = unfold(sum_a[split_a : split_a + 3 * r], 3)
        g_ff1 = unfold(sum_b[r : 5 * r], 4)
        g_up = unfold(sum_b[5 * r + r_ff2 :], 3)
    (
        out_pool_b,
        out_ln1_gain,
        out_ln1_bias,
        out_u,
        out_v,
        out_ln2_gain,
        out_ln2_bias,
        out_ff2_b,
        out_ff1_b,
        out_up_b,
    ) = vec_out
    return (
        block_output,
        input_grad,
        g_pool,
        out_pool_b,
        out_ln1_gain,
        out_ln1_bias,
        g_qkv,
        out_u,
        out_v,
        g_pos,
        g_out,
        out_ln2_gain,
        out_ln2_bias,
        g_ff1,
        out_ff1_b,
        g_ff2,
        out_ff2_b,
        g_up,
        out_up_b,
    )


def solution(mesh):
    links = Links(mesh.shape["dp"], mesh.shape["fsdp"])
    rows = P(AXES, None)
    flat = P(AXES)
    ranks = (2, 1, 1, 2, 1, 1, 1, 2, 1, 1, 2, 2, 1, 1, 2, 1, 2, 1, 2, 1, 2)
    out_ranks = (2, 2, 2, 1, 1, 1, 2, 1, 1, 2, 2, 1, 1, 2, 1, 2, 1, 2, 1)
    return jax.shard_map(
        lambda *args: per_device(links, *args),
        mesh=mesh,
        in_specs=tuple(rows if k == 2 else flat for k in ranks),
        out_specs=tuple(rows if k == 2 else flat for k in out_ranks),
        check_vma=False,
    )
```

```python
import jax
import jax.numpy as jnp
from jax import lax
from jax.experimental import pallas as pl
from jax.experimental.pallas import tpu as pltpu
from jax.sharding import PartitionSpec as P

H = 8
DH = 64
QBLK = 256
AXES = ("dp", "fsdp")


eps_norm = 1e-05
big_negative = -1e30

F32 = jnp.float32
BF16 = jnp.bfloat16
BLOCKS = 32
PAIRS = 4
CH = 64
VMEM = pl.BlockSpec(memory_space=pltpu.VMEM)
SMEM = pl.BlockSpec(memory_space=pltpu.SMEM)
ANY = pl.BlockSpec(memory_space=pl.ANY)
GELU_C = 0.7978845608028654
ROWS_A = 128
ROWS_B = 192
ROWS_C = 48
VEC = slice(48, 64)


def mm(left, right, cl=1, cr=0):
    return lax.dot_general(left, right, (((cl,), (cr,)), ((), ())), preferred_element_type=F32)


def weight(ref, start, rows):
    block = ref[:, start : start + rows, :]
    return block.reshape(block.shape[0] * rows, block.shape[2])


def weight_ff2(ref, start, j):
    block = ref[8 * j : 8 * j + 8, start : start + 64, :]
    return block.reshape(512, block.shape[2])


def start_copy(source, dest, sem):
    copy = pltpu.make_async_copy(source, dest, sem)
    copy.start()
    return copy


def load_rows(me, plan, refs, dest, first, stop, sem):
    for (start, blocks), ref in zip(plan, refs):
        low, high = max(first, start), min(stop, start + ref.shape[1])
        if low < high:
            for k, (base, mask) in enumerate(blocks):
                pltpu.make_async_copy(
                    ref.at[k, pl.ds(low - start, high - low)],
                    dest.at[base + (me ^ mask), pl.ds(low, high - low)],
                    sem,
                ).start()


def wait_rows(dest, first, stop, sem):
    rows = dest.at[:, pl.ds(first, stop - first)]
    pltpu.make_async_copy(rows, rows, sem).wait()


def lane_half(shape, s):
    return (lax.broadcasted_iota(jnp.int32, shape, len(shape) - 1) // DH) == s


def norm_stats(x):
    width = x.shape[-1]
    mean = jnp.sum(x, axis=-1, keepdims=True) * (1.0 / width)
    centre = x - mean
    var = jnp.sum(centre * centre, axis=-1, keepdims=True) * (1.0 / width)
    rstd = lax.rsqrt(var + eps_norm)
    return centre * rstd, rstd


def norm_back(dy, xhat, rstd, gain):
    width = dy.shape[-1]
    d = dy * gain
    m1 = jnp.sum(d, axis=-1, keepdims=True) * (1.0 / width)
    m2 = jnp.sum(d * xhat, axis=-1, keepdims=True) * (1.0 / width)
    return rstd * (d - m1 - xhat * m2)


def forward_kernel(plan, n_pieces, me_ref, *refs):
    pieces = refs[:n_pieces]
    (grouped_hbm, item_col, item_row, sine_hbm, cosine_hbm, key_pos_hbm) = refs[
        n_pieces : n_pieces + 6
    ]
    hbm = refs[n_pieces + 6 : n_pieces + 14]
    vecs, w_out_hbm = refs[n_pieces + 14 : n_pieces + 16]
    (grouped, sine, cosine, pooled, normed, qu, qv, keys, vals, prob, ctx) = refs[
        n_pieces + 16 : n_pieces + 27
    ]
    (w, w_pos, bias, proj, qcat, kcat, tmp, scores, sem, sem2) = refs[n_pieces + 27 :]
    (pooled_hbm, normed_hbm, qu_hbm, qv_hbm, keys_hbm, vals_hbm, prob_hbm, ctx_hbm) = hbm
    me = me_ref[0]
    rows = grouped.shape[0]
    load_rows(me, plan, pieces, w, 0, 64, sem.at[0])
    get_grouped = start_copy(grouped_hbm, grouped, sem2.at[0])
    load_rows(me, plan, pieces, w, 64, ROWS_A, sem.at[1])
    get_sine = start_copy(sine_hbm, sine, sem2.at[1])
    get_cosine = start_copy(cosine_hbm, cosine, sem2.at[2])
    get_key_pos = start_copy(key_pos_hbm, kcat.at[:, 0:rows], sem2.at[3])
    for r in range(0, rows, CH):
        row = r + lax.broadcasted_iota(jnp.int32, (CH, rows), 0)
        col = lax.broadcasted_iota(jnp.int32, (CH, rows), 1)
        allowed = (item_col[r : r + CH, :] == item_row[...]) & (row >= col)
        bias[r : r + CH, :] = jnp.where(allowed, 0.0, big_negative)
    wait_rows(w, 0, 64, sem.at[0])
    get_grouped.wait()
    vec = jnp.sum(w[:, VEC, :].astype(F32), axis=0)
    vecs[...] = vec
    tmp[...] = mm(grouped[...], weight(w, 0, 48))
    for r in range(0, rows, CH):
        x = tmp[r : r + CH, :] + vec[0:1]
        pooled[r : r + CH, :] = x
        xhat, rstd = norm_stats(x)
        normed[r : r + CH, :] = (xhat * vec[1:2] + vec[2:3]).astype(BF16)
    wait_rows(w, 64, ROWS_A, sem.at[1])
    puts = [
        start_copy(w, w_out_hbm, sem2.at[4]),
        start_copy(pooled, pooled_hbm, sem2.at[5]),
        start_copy(normed, normed_hbm, sem2.at[6]),
    ]
    tmp[...] = mm(normed[...], weight(w, 64, 16))
    for r in range(0, rows, CH):
        x = tmp[r : r + CH, :]
        u = (x + vec[3:4]).astype(BF16)
        v = (x + vec[4:5]).astype(BF16)
        for p in range(PAIRS):
            qu[p, r : r + CH, :] = u[:, 128 * p : 128 * p + 128]
            qv[p, r : r + CH, :] = v[:, 128 * p : 128 * p + 128]
    x = mm(normed[...], weight(w, 80, 16)).astype(BF16)
    for p in range(PAIRS):
        keys[p] = x[:, 128 * p : 128 * p + 128]
    x = mm(normed[...], weight(w, 96, 16)).astype(BF16)
    for p in range(PAIRS):
        vals[p] = x[:, 128 * p : 128 * p + 128]
    x = weight(w, 112, 16)
    for p in range(PAIRS):
        w_pos[p] = x[:, 128 * p : 128 * p + 128]

    puts += [
        start_copy(x, y, sem2.at[7 + j])
        for j, (x, y) in enumerate(((qu, qu_hbm), (qv, qv_hbm), (keys, keys_hbm), (vals, vals_hbm)))
    ]
    get_sine.wait()
    get_cosine.wait()
    get_key_pos.wait()

    def put_prob(p):
        pair = pl.ds(2 * p, 2)
        return pltpu.make_async_copy(prob.at[pair], prob_hbm.at[pair], sem2.at[11])

    @pl.loop(0, PAIRS)
    def _(p):
        kcat[:, rows : rows + 128] = keys[p]
        zero = jnp.zeros((rows, 128), BF16)
        halves = [lane_half((rows, 128), s) for s in range(2)]

        def project(s):
            proj[s] = mm(jnp.where(halves[s], qv[p], zero), w_pos[p], 1, 1)

        def rotate(s):
            for r in range(0, rows, CH):
                a = proj[s, r : r + CH, 0:256]
                b = proj[s, r : r + CH, 256:512]
                si = sine[r : r + CH, :]
                co = cosine[r : r + CH, :]
                qcat[s, r : r + CH, 0:256] = (a * si + b * co).astype(BF16)
                qcat[s, r : r + CH, 256:512] = (b * si - a * co).astype(BF16)
            qcat[s, :, 512:640] = jnp.where(halves[s], qu[p], zero)

        def score(s, q):
            first, stop = q * QBLK, (q + 1) * QBLK
            scores[s, first:stop, 0:stop] = mm(qcat[s, first:stop, :], kcat[0:stop, :], 1, 1)

        def softmax(s, q):
            first, stop = q * QBLK, (q + 1) * QBLK
            for r in range(first, stop, CH):
                x = scores[s, r : r + CH, 0:stop] * (DH ** (-0.5)) + bias[r : r + CH, 0:stop]
                e = jnp.exp(x - jnp.max(x, axis=-1, keepdims=True))
                inv = 1.0 / jnp.sum(e, axis=-1, keepdims=True)
                prob[2 * p + s, r : r + CH, 0:stop] = (e * inv).astype(BF16)

        def context(s, q):
            first, stop = q * QBLK, (q + 1) * QBLK
            out = mm(prob[2 * p + s, first:stop, 0:stop], vals[p, 0:stop, :]).astype(BF16)
            if s == 1:
                out = jnp.where(lane_half((QBLK, 128), 1), out, ctx[p, first:stop, :])
            ctx[p, first:stop, :] = out

        project(0)
        project(1)
        rotate(0)
        score(0, 0)
        score(0, 1)
        rotate(1)
        softmax(0, 0)
        score(1, 0)
        score(1, 1)
        softmax(0, 1)
        context(0, 0)
        softmax(1, 0)
        context(0, 1)
        softmax(1, 1)
        context(1, 0)
        context(1, 1)
        put_prob(p).start()

    puts.append(start_copy(ctx, ctx_hbm, sem2.at[12]))
    pltpu.make_async_copy(prob, prob_hbm, sem2.at[11]).wait()
    for c in puts:
        c.wait()


def join(ref):
    return jnp.concatenate([ref[p] for p in range(PAIRS)], axis=1)


def store_blocks(grads, place_ref, line, grad, first, rows=16, start=0):
    for k in range(grad.shape[0] // rows):
        grads[place_ref[line, start + k], first : first + rows, :] = grad[k * rows : (k + 1) * rows].astype(BF16)


def put_blocks(grads, keep_hbm, send_hbm, first, stop, sem):
    rows = pl.ds(first, stop - first)
    half = BLOCKS // 2
    copies = []
    start = half
    for j, ref in enumerate(send_hbm):
        n = ref.shape[0]
        copies.append(start_copy(grads.at[pl.ds(start, n), rows], ref.at[:, rows], sem.at[1 + j]))
        start += n
    copies.append(start_copy(grads.at[pl.ds(0, half), rows], keep_hbm.at[:, rows], sem.at[0]))
    return copies


def middle_kernel(plan, n_pieces, me_ref, place_ref, *refs):
    pieces = refs[:n_pieces]
    (pooled_hbm, ctx_hbm, up_grad_hbm, vecs) = refs[n_pieces : n_pieces + 4]
    (res_grad_hbm, cg, short_out_hbm, vec_grads, w_up_hbm, keep_hbm, send_hbm) = refs[
        n_pieces + 4 : n_pieces + 11
    ]
    (pooled, ctx, up_grad, res_grad, short_out) = refs[n_pieces + 11 : n_pieces + 16]
    (w, grads, xhat, rstd, n2, hidden, pre, slope, acc, tmp, sgrad, bg, attn, sem, sem2, sem3) = refs[
        n_pieces + 16 :
    ]
    me = me_ref[0]
    rows = pooled.shape[0]
    load_rows(me, plan, pieces, w, 0, 80, sem.at[0])
    get_ctx = start_copy(ctx_hbm, ctx, sem2.at[0])
    get_pooled = start_copy(pooled_hbm, pooled, sem2.at[1])
    load_rows(me, plan, pieces, w, 80, 144, sem.at[1])
    load_rows(me, plan, pieces, w, 144, ROWS_B, sem.at[2])
    get_up_grad = start_copy(up_grad_hbm, up_grad, sem2.at[2])
    get_ctx.wait()
    get_pooled.wait()
    wait_rows(w, 0, 80, sem.at[0])
    gain2, bias2 = vecs[5:6, :], vecs[6:7, :]
    acc[...] = pooled[...] + mm(join(ctx), weight(w, 0, 16))
    for r in range(0, rows, CH):
        xh, rs = norm_stats(acc[r : r + CH, :])
        xhat[r : r + CH, :] = xh
        rstd[r : r + CH, :] = jnp.broadcast_to(rs, (CH, 128))
        n2[r : r + CH, :] = (xh * gain2 + bias2).astype(BF16)

    def first_layer(j):
        tmp[j] = mm(n2[...], weight(w, 16 + 16 * j, 16))

    def activate(j):
        b1 = vecs[8 + j : 9 + j, :]
        for r in range(0, rows, CH):
            x = tmp[j, r : r + CH, :] + b1
            x2 = x * x
            t = jnp.tanh(GELU_C * (x + 0.044715 * (x * x2)))
            hidden[r : r + CH, 512 * j : 512 * j + 512] = (0.5 * x * (1.0 + t)).astype(BF16)
            slope[j, r : r + CH, :] = 0.5 * (1.0 + t) + (0.5 * GELU_C) * x * (1.0 - t * t) * (
                1.0 + (3.0 * 0.044715) * x2
            )

    def up_back(j):
        return mm(up_grad[:, 512 * j : 512 * j + 512], weight(w, 144 + 16 * j, 16), 1, 1)

    def second_layer(j):
        return mm(hidden[:, 512 * j : 512 * j + 512], weight_ff2(w, 80, j))

    first_layer(0)
    first_layer(1)
    activate(0)
    wait_rows(w, 80, 144, sem.at[1])
    first_layer(2)
    activate(1)
    acc[...] += second_layer(0)
    first_layer(3)
    activate(2)
    acc[...] += second_layer(1)
    wait_rows(w, 144, ROWS_B, sem.at[2])
    get_up_grad.wait()
    sgrad[...] = up_back(0) + up_back(1)
    activate(3)
    acc[...] += second_layer(2)
    sgrad[...] += up_back(2)
    acc[...] += second_layer(3)
    bg[...] = sgrad[...].astype(BF16)
    short_out[...] = (acc[...] + vecs[7:8, :]).astype(BF16)
    puts = [
        start_copy(w.at[:, pl.ds(144, 48)], w_up_hbm, sem2.at[3]),
        start_copy(short_out, short_out_hbm, sem2.at[4]),
    ]

    def hidden_back(j):
        tmp[j] = mm(bg[...], weight_ff2(w, 80, j), 1, 1)

    def activate_back(j):
        total = jnp.zeros((1, 512), F32)
        for r in range(0, rows, CH):
            x = (tmp[j, r : r + CH, :] * slope[j, r : r + CH, :]).astype(BF16)
            pre[r : r + CH, 512 * j : 512 * j + 512] = x
            total = total + jnp.sum(x.astype(F32), axis=0, keepdims=True)
        vec_grads[8 + j : 9 + j, :] = total

    def up_weights(j):
        g = mm(short_out[...], up_grad[:, 512 * j : 512 * j + 512], 0, 0)
        store_blocks(grads, place_ref, 0, g, 144 + 16 * j)

    def second_weights(j):
        g = mm(hidden[:, 512 * j : 512 * j + 512], bg[...], 0, 0)
        store_blocks(grads, place_ref, 0, g, 80, 64, 8 * j)

    def first_weights(j):
        g = mm(n2[...], pre[:, 512 * j : 512 * j + 512], 0, 0)
        store_blocks(grads, place_ref, 0, g, 16 + 16 * j)

    def first_back(j):
        return mm(pre[:, 512 * j : 512 * j + 512], weight(w, 16 + 16 * j, 16), 1, 1)

    vec_grads[...] = jnp.zeros(vec_grads.shape, F32)
    hidden_back(0)
    hidden_back(1)
    activate_back(0)
    hidden_back(2)
    activate_back(1)
    acc[...] = first_back(0)
    hidden_back(3)
    activate_back(2)
    acc[...] += first_back(1)
    second_weights(0)
    activate_back(3)
    acc[...] += first_back(2)
    second_weights(1)
    acc[...] += first_back(3)
    second_weights(2)
    second_weights(3)
    dgain = jnp.zeros((1, 512), F32)
    dbias = jnp.zeros((1, 512), F32)
    for r in range(0, rows, CH):
        dy = acc[r : r + CH, :]
        xh = xhat[r : r + CH, :]
        dgain = dgain + jnp.sum(dy * xh, axis=0, keepdims=True)
        dbias = dbias + jnp.sum(dy, axis=0, keepdims=True)
        x = sgrad[r : r + CH, :] + norm_back(dy, xh, rstd[r : r + CH, 0:1], gain2)
        res_grad[r : r + CH, :] = x
        attn[r : r + CH, :] = x.astype(BF16)
    vec_grads[5:6, :] = dgain
    vec_grads[6:7, :] = dbias
    up_weights(0)
    up_weights(1)
    up_weights(2)
    puts += put_blocks(grads, keep_hbm, (send_hbm,), 80, ROWS_B, sem3.at[0])
    first_weights(0)
    first_weights(1)
    first_weights(2)
    first_weights(3)
    puts += put_blocks(grads, keep_hbm, (send_hbm,), 16, 80, sem3.at[1])
    for j in range(3):
        vec_grads[12 + j : 13 + j, :] = jnp.sum(
            up_grad[:, 512 * j : 512 * j + 512].astype(F32), axis=0, keepdims=True
        )
    vec_grads[7:8, :] = jnp.sum(bg[...].astype(F32), axis=0, keepdims=True)
    store_blocks(grads, place_ref, 0, mm(join(ctx), attn[...], 0, 0), 0)
    puts += put_blocks(grads, keep_hbm, (send_hbm,), 0, 16, sem3.at[2])
    puts.append(start_copy(res_grad, res_grad_hbm, sem2.at[5]))
    x = mm(attn[...], weight(w, 0, 16), 1, 1).astype(BF16)
    for p in range(PAIRS):
        cg[p] = x[:, 128 * p : 128 * p + 128]
    for c in puts:
        c.wait()


def tail_kernel(
    place_ref, prob, cg_hbm, vals_hbm, keys_hbm, qu_hbm, qv_hbm, key_pos_hbm, sine_hbm, cosine_hbm,
    normed_hbm, grouped_hbm, pooled_hbm, res_grad_hbm, vecs, vec_in, w_hbm,
    pg, w_pool_out, keep_hbm, send0, send1, send2, send3,
    cg, vals, keys, qu, qv, key_pos, sine, cosine, normed, grouped, pooled, res_grad,
    w_pos, pgrad, sg, posg, qg, qkvg, pos_w_grad, w, grads, acc, vec, prob_v, sem, prob_sem, get_sem,
):
    rows = key_pos.shape[0]
    n_q = rows // QBLK
    pairs = ((cg_hbm, cg), (vals_hbm, vals), (keys_hbm, keys), (qu_hbm, qu), (qv_hbm, qv))
    first_gets = [start_copy(x, y, get_sem.at[j]) for j, (x, y) in enumerate(pairs)]

    def fetch(p):
        return pltpu.make_async_copy(prob.at[pl.ds(2 * p, 2)], prob_v.at[p % 2], prob_sem.at[p % 2])

    fetch(0).start()
    tables = ((key_pos_hbm, key_pos), (sine_hbm, sine), (cosine_hbm, cosine))
    first_gets += [start_copy(x, y, get_sem.at[5 + j]) for j, (x, y) in enumerate(tables)]
    load = start_copy(w_hbm.at[:, pl.ds(112, 16)], w.at[:, pl.ds(112, 16)], sem.at[0])
    late = ((normed_hbm, normed), (grouped_hbm, grouped), (pooled_hbm, pooled), (res_grad_hbm, res_grad))
    late_gets = [start_copy(x, y, get_sem.at[8 + j]) for j, (x, y) in enumerate(late)]
    late_gets.append(start_copy(w_hbm.at[:, pl.ds(0, 112)], w.at[:, pl.ds(0, 112)], get_sem.at[12]))
    vec[...] = vec_in[...]
    load.wait()
    for c in first_gets:
        c.wait()
    x = weight(w, 112, 16)
    for p in range(PAIRS):
        w_pos[p] = x[:, 128 * p : 128 * p + 128]

    @pl.loop(0, PAIRS)
    def _(p):
        @pl.when(p + 1 < PAIRS)
        def _():
            fetch(p + 1).start()

        fetch(p).wait()
        slot = p % 2
        u_sums = []
        v_sums = []
        for s in range(2):
            half = lane_half((rows, 128), s)
            zero = jnp.zeros((rows, 128), BF16)
            cgm = jnp.where(half, cg[p], zero)
            qum = jnp.where(half, qu[p], zero)
            qvm = jnp.where(half, qv[p], zero)
            for q in range(n_q):
                first, stop = q * QBLK, (q + 1) * QBLK
                pgrad[first:stop, 0:stop] = mm(cgm[first:stop], vals[p, 0:stop, :], 1, 1)
                for r in range(first, stop, CH):
                    pr = prob_v[slot, s, r : r + CH, 0:stop].astype(F32)
                    t = pr * pgrad[r : r + CH, 0:stop]
                    inner = jnp.sum(t, axis=-1, keepdims=True)
                    sg[r : r + CH, 0:stop] = ((t - pr * inner) * (DH ** (-0.5))).astype(BF16)
                posg[first:stop, :] = mm(sg[first:stop, 0:stop], key_pos[0:stop, :])
                part = mm(sg[first:stop, 0:stop], keys[p, 0:stop, :])
                if s == 0:
                    qg[p, first:stop, :] = part
                else:
                    qg[p, first:stop, :] = jnp.where(
                        lane_half((QBLK, 128), 1), part, qg[p, first:stop, :]
                    )
                kg = mm(sg[first:stop, 0:stop], qum[first:stop], 0, 0)
                vg = mm(prob_v[slot, s, first:stop, 0:stop], cgm[first:stop], 0, 0)
                if s == 0 and q == 0:
                    qg[PAIRS + p] = jnp.zeros((rows, 128), F32)
                    qg[2 * PAIRS + p] = jnp.zeros((rows, 128), F32)
                qg[PAIRS + p, 0:stop, :] += kg
                qg[2 * PAIRS + p, 0:stop, :] += vg
            for r in range(0, rows, CH):
                a = posg[r : r + CH, 0:256]
                b = posg[r : r + CH, 256:512]
                si = sine[r : r + CH, :]
                co = cosine[r : r + CH, :]
                sg[r : r + CH, 0:256] = (a * si - b * co).astype(BF16)
                sg[r : r + CH, 256:512] = (a * co + b * si).astype(BF16)
            gw = mm(sg[...], qvm, 0, 0)
            if s == 0:
                pos_w_grad[p] = gw
            else:
                pos_w_grad[p] += gw
            qvg = jnp.where(half, mm(sg[...], w_pos[p]), 0.0)
            v_sums.append(jnp.sum(qvg, axis=0, keepdims=True))
            u_sums.append(jnp.sum(jnp.where(half, qg[p], 0.0), axis=0, keepdims=True))
            qg[p] += qvg
        u_row = u_sums[0] + u_sums[1]
        v_row = v_sums[0] + v_sums[1]
        for k in range(PAIRS):

            @pl.when(p == k)
            def _():
                vec[3:4, 128 * k : 128 * k + 128] = u_row
                vec[4:5, 128 * k : 128 * k + 128] = v_row

    for c in late_gets:
        c.wait()
    for j in range(3):
        for p in range(PAIRS):
            qkvg[j, :, 128 * p : 128 * p + 128] = qg[PAIRS * j + p].astype(BF16)
    for j in range(3):
        store_blocks(grads, place_ref, 1, mm(normed[...], qkvg[j], 0, 0), 64 + 16 * j)
    store_blocks(grads, place_ref, 1, join(pos_w_grad), 112)
    sends = (send0, send1, send2, send3)
    puts = put_blocks(grads, keep_hbm, sends, 64, ROWS_A, sem.at[pl.ds(2, 5)])
    keep_pool = pltpu.make_async_copy(w.at[:, 0:48], w_pool_out, sem.at[1])
    keep_pool.start()
    acc[...] = (
        mm(qkvg[0], weight(w, 64, 16), 1, 1)
        + mm(qkvg[1], weight(w, 80, 16), 1, 1)
        + mm(qkvg[2], weight(w, 96, 16), 1, 1)
    )
    gain1 = vecs[1:2, :]
    dgain = jnp.zeros((1, 512), F32)
    dbias = jnp.zeros((1, 512), F32)
    dpool = jnp.zeros((1, 512), F32)
    for r in range(0, rows, CH):
        dy = acc[r : r + CH, :]
        xh, rs = norm_stats(pooled[r : r + CH, :])
        dgain = dgain + jnp.sum(dy * xh, axis=0, keepdims=True)
        dbias = dbias + jnp.sum(dy, axis=0, keepdims=True)
        x = (res_grad[r : r + CH, :] + norm_back(dy, xh, rs, gain1)).astype(BF16)
        pg[r : r + CH, :] = x
        dpool = dpool + jnp.sum(x.astype(F32), axis=0, keepdims=True)
    vec[0:1, :] = dpool
    vec[1:2, :] = dgain
    vec[2:3, :] = dbias
    table = vec[...].astype(BF16)
    for d in range(BLOCKS):
        grads[place_ref[1, d], VEC, :] = table
    for j in range(3):
        g = mm(grouped[:, 512 * j : 512 * j + 512], pg[...], 0, 0)
        for k in range(32):
            granule = 32 * j + k
            d, sub = granule // 3, granule % 3
            grads[place_ref[1, d], 16 * sub : 16 * sub + 16, :] = g[16 * k : 16 * k + 16].astype(BF16)
    puts += put_blocks(grads, keep_hbm, sends, 0, 64, sem.at[pl.ds(7, 5)])
    keep_pool.wait()
    for c in puts:
        c.wait()


def bytes_kernel(emb, cot, cols, short_out, w_up, vecs, pg, w_pool, out, grad, tmp):
    rows = emb.shape[0]
    for j in range(3):
        tmp[...] = mm(short_out[...], weight(w_up, 16 * j, 16))
        up_bias = vecs[12 + j : 13 + j, :]
        for r in range(0, rows, CH):
            x = emb[r : r + CH, 512 * j : 512 * j + 512].astype(F32) + tmp[r : r + CH, :] + up_bias
            out[r : r + CH, 512 * j : 512 * j + 512] = jnp.where(
                cols[r : r + CH, j : j + 1] > 0, x, 0.0
            ).astype(BF16)
    pool = weight(w_pool, 0, 48)
    for j in range(3):
        src = (j + 2) % 3
        tmp[...] = mm(pg[...], pool[512 * src : 512 * src + 512, :], 1, 1)
        if j > 0:
            tmp[...] = pltpu.roll(tmp[...], rows - 1, 0)
        for r in range(0, rows, CH):
            x = tmp[r : r + CH, :]
            if j > 0:
                x = jnp.where(cols[r : r + CH, 3:4] > 0, x, 0.0)
            x = cot[r : r + CH, 512 * j : 512 * j + 512].astype(F32) + x
            grad[r : r + CH, 512 * j : 512 * j + 512] = jnp.where(
                cols[r : r + CH, j : j + 1] > 0, x, 0.0
            ).astype(BF16)


def pack_kernel(me_ref, *refs):
    (w_pool, w_qkv, w_pos, w_out, w_ff1, w_ff2, w_up) = refs[:7]
    vectors = refs[7:17]
    all_a, all_b, out_c, out_a, out_b, sem = refs[17:]
    me = me_ref[0]
    out_a[0:48, :] = w_pool[...]
    for j in range(3):
        out_a[64 + 16 * j : 80 + 16 * j, :] = w_qkv[:, 512 * j : 512 * j + 512]
        out_c[0, 16 * j : 16 + 16 * j, :] = w_up[:, 512 * j : 512 * j + 512]
    out_a[112:128, :] = w_pos[...]
    out_b[0:16, :] = w_out[...]
    for j in range(4):
        out_b[16 + 16 * j : 32 + 16 * j, :] = w_ff1[:, 512 * j : 512 * j + 512]
    out_b[80:144, :] = w_ff2[...]

    def spread(x, first):
        k = x.shape[1]
        lane = first + lax.broadcasted_iota(jnp.int32, (k, 512), 1)
        row = lax.broadcasted_iota(jnp.int32, (k, 512), 0)
        pick = jnp.where(lane % k == row, 1.0, 0.0).astype(BF16)
        own = (first + lax.broadcasted_iota(jnp.int32, (x.shape[0], 512), 1)) // k == me
        return jnp.where(own, mm(x, pick), 0.0)

    lines = [spread(v[...], 0) for v in vectors[:8]]
    lines += [spread(vectors[8][...], 512 * j) for j in range(4)]
    lines += [spread(vectors[9][...], 512 * j) for j in range(3)]
    lines.append(jnp.zeros((1, 512), F32))
    out_a[VEC, :] = jnp.concatenate(lines, axis=0).astype(BF16)
    copies = []
    for j in range(all_a.shape[0]):
        copies.append(pltpu.make_async_copy(out_a, all_a.at[j], sem.at[j]))
    for j in range(all_b.shape[0]):
        copies.append(pltpu.make_async_copy(out_b, all_b.at[j], sem.at[all_a.shape[0] + j]))
    for c in copies:
        c.start()
    for c in copies:
        c.wait()


def finish_b_kernel(*refs):
    out, ff1, up, ff2 = refs[-4:]
    total = refs[0][0].astype(F32)
    for ref in refs[1:-4]:
        total = total + ref[0].astype(F32)
    out[...] = total[0:16]
    for j in range(4):
        ff1[:, 512 * j : 512 * j + 512] = total[16 + 16 * j : 32 + 16 * j]
    for j in range(3):
        up[:, 512 * j : 512 * j + 512] = total[144 + 16 * j : 160 + 16 * j]
    ff2[...] = total[80:144]


def finish_a_kernel(me_ref, *refs):
    me = me_ref[0]
    parts, (pool, qkv, pos), vectors = refs[:-13], refs[-13:-10], refs[-10:]
    total = parts[0][0].astype(F32)
    for ref in parts[1:]:
        total = total + ref[0].astype(F32)
    pool[...] = total[0:48]
    for j in range(3):
        qkv[:, 512 * j : 512 * j + 512] = total[64 + 16 * j : 80 + 16 * j]
    pos[...] = total[112:128]
    table = total[VEC]
    lines = pltpu.roll(table[0:8], 512 - 16 * me, 1)
    for j in range(8):
        vectors[j][...] = lines[j : j + 1, 0:16]
    row = lax.broadcasted_iota(jnp.int32, (16, 512), 0)

    def line(j):
        return jnp.sum(jnp.where(row == j, table, 0.0), axis=0, keepdims=True)

    def part(first, length):
        j, off = first // 512, first % 512
        here = pltpu.roll(jnp.broadcast_to(line(j), (8, 512)), 512 - off, 1)
        there = pltpu.roll(jnp.broadcast_to(line(j + 1), (8, 512)), 512 - off, 1)
        lane = lax.broadcasted_iota(jnp.int32, (8, 512), 1)
        return jnp.where(lane < 512 - off, here, there)[0:1, 0:length]

    vectors[8][...] = part(8 * 512 + 64 * me, 64)
    vectors[9][...] = part(12 * 512 + 48 * me, 48)


class Links:
    def __init__(self, dp, fsdp):
        self.dp = dp
        self.fsdp = fsdp
        self.count = dp * fsdp
        self.near = [2 * m for m in range(fsdp // 2)]

    def send(self, values, mask):
        return lax.ppermute(values, AXES, [(i, i ^ mask) for i in range(self.count)])

    def deep(self, blocks):
        return lax.all_to_all(blocks, "dp", 0, 0, tiled=True)

    def gather_near(self, held):
        return [held] + [self.send(held, m) for m in self.near[1:]]

    def gather_core(self, pieces):
        return pieces + [
            (first, [(z, m ^ 1) for z, m in blocks], self.send(array, 1)) for first, blocks, array in pieces
        ]

    def near_pieces(self, first, near):
        return [(first, [(z, m) for z in range(self.dp)], x) for m, x in zip(self.near, near)]

    def places(self, me, by_place, by_plane):
        owner = jnp.arange(self.count, dtype=jnp.int32)
        place = (owner if by_place else owner ^ me) % self.fsdp // 2
        plane = (owner if by_plane else owner ^ me) // self.fsdp
        return ((owner ^ me) % 2 * (self.fsdp // 2) + place) * self.dp + plane

    def start_deep(self, blocks):
        return [blocks[:1]] + [
            self.send(blocks[m : m + 1], self.fsdp * m) for m in range(1, self.dp)
        ]

    def split_core(self, keep, got):
        n = self.dp
        return [
            add(keep[k * n : k * n + n], got[k]).astype(BF16)
            for k in range(len(self.near))
        ]

    def start_near(self, totals):
        return totals[:1] + [self.send(t, m) for t, m in zip(totals[1:], self.near[1:])]

    def swap_near(self, blocks):
        groups = [list(range(c, self.fsdp, 2)) for c in range(2)]
        return lax.all_to_all(blocks, "fsdp", 0, 0, axis_index_groups=groups, tiled=True)

    def total_core(self, keep, got):
        outs = []
        first = 0
        for x in got:
            outs.append(add(keep[first : first + x.shape[0]], x).astype(BF16))
            first += x.shape[0]
        return jnp.concatenate(outs, axis=0) if len(outs) > 1 else outs[0]

    def total_near(self, parts):
        if not isinstance(parts, list):
            parts = [parts[k : k + self.dp] for k in range(0, parts.shape[0], self.dp)]
        total = parts[0].astype(F32)
        for x in parts[1:]:
            total = total + x.astype(F32)
        return total.astype(BF16)

    def total_deep(self, parts):
        return jnp.sum(parts.astype(F32), axis=0)

    def reduce(self, keep, send):
        near = self.swap_near(self.total_core(keep, [self.send(send, 1)]))
        return self.total_deep(self.deep(self.total_near(near)))


def in_vmem(x):
    return pltpu.with_memory_space_constraint(x, pltpu.VMEM)


def add(left, right):
    return left.astype(F32) + right.astype(F32)


def cost(us):
    return pl.CostEstimate(flops=us * 10**9, transcendentals=0, bytes_accessed=us * 10**6)


def in_vmem(x):
    return pltpu.with_memory_space_constraint(x, pltpu.VMEM)


def add(left, right):
    return left.astype(F32) + right.astype(F32)


def fold(shard, width):
    return jnp.concatenate(
        [shard[..., j : j + width] for j in range(0, shard.shape[-1], width)], axis=-2
    )


def unfold(block, count):
    rows = block.shape[-2] // count
    return jnp.concatenate(
        [block[..., j * rows : (j + 1) * rows, :] for j in range(count)], axis=-1
    )


def reblock(blocks, layout, count):
    m = blocks.shape[0]
    outs = []
    for first, rows, k in layout:
        x = unfold(blocks[:, first : first + rows], k)
        x = x.reshape(m * x.shape[1], x.shape[2]).reshape(count, -1, x.shape[2])
        outs.append(fold(x, blocks.shape[2]))
    return jnp.concatenate(outs, axis=1)


def layout_of(parts):
    out = []
    first = 0
    for rows, k in parts:
        out.append((first, rows, k))
        first += rows
    return out


def per_device(links, *args):
    (
        byte_embeddings,
        byte_item,
        byte_mask,
        w_pool,
        b_pool,
        ln1_gain,
        ln1_bias,
        w_qkv,
        pos_u,
        pos_v,
        w_pos,
        w_out,
        ln2_gain,
        ln2_bias,
        w_ff1,
        b_ff1,
        w_ff2,
        b_ff2,
        w_up,
        b_up,
        cotangent,
    ) = args
    n_dev = links.count
    me = lax.axis_index(AXES).astype(jnp.int32)
    width = w_pos.shape[1]
    r_pool, r, r_ff2 = w_pool.shape[0], w_pos.shape[0], w_ff2.shape[0]
    direct = n_dev == BLOCKS
    vectors = [b_pool, ln1_gain, ln1_bias, pos_u, pos_v, ln2_gain, ln2_bias, b_ff2, b_ff1, b_up]
    lengths = [v.shape[0] for v in vectors]
    vec_rows = [v * n_dev // width for v in lengths]
    vec_first = [sum(vec_rows[:i]) for i in range(len(vec_rows))]

    params = pltpu.CompilerParams(vmem_limit_bytes=60 << 20)
    sds = jax.ShapeDtypeStruct
    if direct:
        shard_a, shard_b, shard_c = pl.pallas_call(
            pack_kernel,
            out_shape=(
                sds((links.dp, ROWS_A, width), BF16),
                sds((links.dp, ROWS_B - ROWS_C, width), BF16),
                sds((1, ROWS_C, width), BF16),
            ),
            in_specs=[SMEM] + [VMEM] * 17,
            out_specs=[ANY] * 2 + [VMEM],
            scratch_shapes=[
                pltpu.VMEM((ROWS_A, width), BF16),
                pltpu.VMEM((ROWS_B - ROWS_C, width), BF16),
                pltpu.SemaphoreType.DMA((2 * links.dp,)),
            ],
            compiler_params=params,
            cost_estimate=cost(3),
        name="pack",
        )(me[None], w_pool, w_qkv, w_pos, w_out, w_ff1, w_ff2, w_up, *[v[None] for v in vectors])
    else:
        flat = jnp.arange(n_dev * lengths[8])
        table = []
        for v in vectors:
            k = v.shape[0]
            spread = jnp.where(flat[: n_dev * k] // k == me, jnp.tile(v, n_dev), jnp.zeros((), v.dtype))
            table.append(spread.reshape(-1, width))
        table.append(jnp.zeros((16 - sum(vec_rows), width), BF16))
        shard_a = jnp.concatenate([w_pool] + table + [fold(w_qkv, width), w_pos], axis=0)
        shard_b = jnp.concatenate([w_out, fold(w_ff1, width), w_ff2], axis=0)
        shard_c = fold(w_up, width)[None]
        shard_a, shard_b = [
            jnp.broadcast_to(x[None], (links.dp,) + x.shape) for x in (shard_a, shard_b)
        ]
    split_a = r_pool + 16
    byte_total = byte_embeddings.shape[0]
    rows = byte_total // 3
    emb = byte_embeddings.reshape(rows, 3 * width)
    cot = cotangent.reshape(rows, 3 * width)
    mask3 = byte_mask.reshape(rows, 3)
    item = byte_item.reshape(rows, 3)[:, 0]
    same = item[1:] == item[:-1]
    no = jnp.zeros((1,), jnp.bool_)
    same_before = jnp.concatenate([no, same])[:, None]
    same_after = jnp.concatenate([same, no])[:, None]
    cols = jnp.concatenate([mask3, same_after.astype(jnp.int32)], axis=1)
    item_f = item.astype(F32)
    live = [mask3[:, j : j + 1] > 0 for j in range(3)]
    zero = jnp.zeros((), jnp.bfloat16)
    masked = [jnp.where(live[j], emb[:, j * width : (j + 1) * width], zero) for j in range(3)]
    up_grad = jnp.concatenate(
        [jnp.where(live[j], cot[:, j * width : (j + 1) * width], zero) for j in range(3)], axis=1
    )

    def down(x):
        moved = jnp.concatenate([jnp.zeros((1, width), x.dtype), x[:-1]], axis=0)
        return jnp.where(same_before, moved, zero)

    grouped = jnp.concatenate([down(masked[1]), down(masked[2]), masked[0]], axis=1)
    places = jnp.arange(rows).astype(F32)
    frequency = 10000.0 ** (-(2.0 * jnp.arange(width // 2).astype(F32)) / width)
    angles = places[:, None] * frequency[None, :]
    sine, cosine = jnp.sin(angles), jnp.cos(angles)
    key_pos = jnp.concatenate([cosine, sine], axis=1).astype(BF16)

    held_a = links.deep(shard_a)
    held_c = jnp.concatenate(links.gather_near(shard_c), axis=0)
    item_col, item_row = item_f[:, None], item_f[None, :]
    if direct:
        place = jnp.stack([links.places(me, True, False), links.places(me, False, False)])
    else:
        place = jnp.tile(jnp.arange(BLOCKS, dtype=jnp.int32)[None], (2, 1))
    held_a, held_c, shard_b = lax.optimization_barrier((held_a, held_c, shard_b))
    near_a = links.gather_near(held_a)
    given = (emb, cot, cols, up_grad, grouped, sine, cosine, key_pos, item_col, item_row, place)
    near_a, given = lax.optimization_barrier((near_a, given))
    emb, cot, cols, up_grad, grouped, sine, cosine, key_pos, item_col, item_row, place = given
    pieces_a = links.gather_core(links.near_pieces(0, near_a))
    held_b = links.deep(shard_b)
    grouped, held_b = lax.optimization_barrier((grouped, held_b))
    near_b = links.gather_near(held_b)
    copies_c = jnp.concatenate([held_c] * links.dp, axis=0)
    copies_c, arrays = lax.optimization_barrier((copies_c, [x for _, _, x in pieces_a]))
    pieces_a = [(first, blocks, x) for (first, blocks, _), x in zip(pieces_a, arrays)]
    deep_c = links.deep(copies_c)
    layout_a = layout_of([(r_pool, 1), (16, 0), (3 * r, 3), (r, 1)])
    layout_b = layout_of([(r, 1), (4 * r, 4), (r_ff2, 1), (3 * r, 3)])
    layout_a32 = layout_of([(48, 1), (16, 0), (48, 3), (16, 1)])
    layout_b32 = layout_of([(16, 1), (64, 4), (64, 1), (48, 3)])

    if direct:
        base = (me % links.fsdp)[None]
    else:

        def canonical(pieces, layout):
            lines = {}
            for first, blocks, array in pieces:
                for j, (z, m) in enumerate(blocks):
                    lines.setdefault(first, {})[m, z] = array[j]
            parts = []
            for first in sorted(lines):
                arr = jnp.stack(
                    [jnp.stack([lines[first][m, z] for m in range(links.fsdp)]) for z in range(links.dp)]
                )
                arr = jnp.take(arr, jnp.arange(links.fsdp) ^ (me % links.fsdp), axis=1)
                parts.append(arr.reshape((n_dev,) + arr.shape[2:]))
            blocks = jnp.concatenate(parts, axis=1)
            outs = []
            for first, rows_, k in layout:
                if k == 0:
                    total = jnp.sum(blocks[:, first : first + rows_].astype(F32), axis=0)
                    outs.append(
                        jnp.concatenate(
                            [total[None], jnp.zeros((BLOCKS - 1,) + total.shape, F32)], axis=0
                        ).astype(BF16)
                    )
                else:
                    outs.append(reblock(blocks, [(first, rows_, k)], BLOCKS))
            return [(0, [(d, 0) for d in range(BLOCKS)], jnp.concatenate(outs, axis=1))]

        pieces_a = canonical(pieces_a, layout_a)
        base = jnp.zeros((1,), jnp.int32)

    pair_bf = sds((PAIRS, rows, 128), BF16)
    pair_f = sds((PAIRS, rows, 128), F32)
    square = sds((rows, width), F32)
    table_f = sds((16, width), F32)

    step = links.fsdp if direct else 1
    plan_a = [(first, [(z * step, m) for z, m in blocks]) for first, blocks, _ in pieces_a]
    n_a = len(plan_a)
    forward = pl.pallas_call(
        lambda *refs: forward_kernel(plan_a, n_a, *refs),
        out_shape=(
            square,
            sds((rows, width), BF16),
            pair_bf,
            pair_bf,
            pair_bf,
            pair_bf,
            sds((H, rows, rows), BF16),
            pair_bf,
            table_f,
            sds((BLOCKS, ROWS_A, width), BF16),
        ),
        in_specs=[SMEM] + [ANY] * n_a + [ANY, VMEM, VMEM, ANY, ANY, ANY],
        out_specs=[ANY] * 8 + [VMEM, ANY],
        scratch_shapes=[
            pltpu.VMEM((rows, 3 * width), BF16),
            pltpu.VMEM((rows, width // 2), F32),
            pltpu.VMEM((rows, width // 2), F32),
            pltpu.VMEM((rows, width), F32),
            pltpu.VMEM((rows, width), BF16),
        ]
        + [pltpu.VMEM((PAIRS, rows, 128), BF16)] * 4
        + [
            pltpu.VMEM((H, rows, rows), BF16),
            pltpu.VMEM((PAIRS, rows, 128), BF16),
            pltpu.VMEM((BLOCKS, ROWS_A, width), BF16),
            pltpu.VMEM((PAIRS, width, 128), BF16),
            pltpu.VMEM((rows, rows), F32),
            pltpu.VMEM((2, rows, width), F32),
            pltpu.VMEM((2, rows, width + 128), BF16),
            pltpu.VMEM((rows, width + 128), BF16),
            pltpu.VMEM((rows, width), F32),
            pltpu.VMEM((2, rows, rows), F32),
            pltpu.SemaphoreType.DMA((2,)),
            pltpu.SemaphoreType.DMA((13,)),
        ],
        compiler_params=params,
        cost_estimate=cost(20),
        name="forward",
    )
    pooled, normed, qu, qv, keys, vals, prob, ctx, vecs, wa = forward(base, *[a for _, _, a in pieces_a], grouped, item_col, item_row, sine, cosine, key_pos)
    pooled, far_b, deep_c = lax.optimization_barrier((pooled, near_b[1:], deep_c))
    near_b = near_b[:1] + far_b
    blocks_c = [(z, m) for z in range(links.dp) for m in links.near]
    pieces_b = links.gather_core(links.near_pieces(0, near_b) + [(shard_b.shape[1], blocks_c, deep_c)])
    if not direct:
        pieces_b = canonical(pieces_b, layout_b)

    plan_b = [(first, [(z * step, m) for z, m in blocks]) for first, blocks, _ in pieces_b]
    n_b = len(plan_b)
    half = BLOCKS // 2
    res_grad, cg, short_out, vec_grads, w_up_abs, keep_b, *send_b = pl.pallas_call(
        lambda *refs: middle_kernel(plan_b, n_b, *refs),
        out_shape=(
            square,
            pair_bf,
            sds((rows, width), BF16),
            table_f,
            sds((BLOCKS, 48, width), BF16),
            sds((half, ROWS_B, width), BF16),
        )
        + (sds((half, ROWS_B, width), BF16),),
        in_specs=[SMEM, SMEM] + [ANY] * n_b + [ANY, ANY, ANY, VMEM],
        out_specs=[ANY, VMEM, ANY, VMEM] + [ANY] * 3,
        scratch_shapes=[
            pltpu.VMEM((rows, width), F32),
            pltpu.VMEM((PAIRS, rows, 128), BF16),
            pltpu.VMEM((rows, 3 * width), BF16),
            pltpu.VMEM((rows, width), F32),
            pltpu.VMEM((rows, width), BF16),
            pltpu.VMEM((BLOCKS, ROWS_B, width), BF16),
            pltpu.VMEM((BLOCKS, ROWS_B, width), BF16),
            pltpu.VMEM((rows, width), F32),
            pltpu.VMEM((rows, 128), F32),
            pltpu.VMEM((rows, width), BF16),
            pltpu.VMEM((rows, 4 * 512), BF16),
            pltpu.VMEM((rows, 4 * 512), BF16),
            pltpu.VMEM((4, rows, 512), F32),
            pltpu.VMEM((rows, width), F32),
            pltpu.VMEM((4, rows, width), F32),
            pltpu.VMEM((rows, width), F32),
            pltpu.VMEM((rows, width), BF16),
            pltpu.VMEM((rows, width), BF16),
            pltpu.SemaphoreType.DMA((3,)),
            pltpu.SemaphoreType.DMA((6,)),
            pltpu.SemaphoreType.DMA((3, 2)),
        ],
        compiler_params=params,
        cost_estimate=cost(20),
        name="middle",
    )(base, place, *[a for _, _, a in pieces_b], pooled, ctx, up_grad, vecs)

    if direct:
        total_b = links.total_core(keep_b, [links.send(x, 1) for x in send_b])
        cg, total_b = lax.optimization_barrier((cg, total_b))
        near_b = links.swap_near(total_b)

    pooled_grad, w_pool_abs, keep_a, *send_a = pl.pallas_call(
        tail_kernel,
        out_shape=(
            sds((rows, width), BF16),
            sds((BLOCKS, 48, width), BF16),
            sds((half, ROWS_A, width), BF16),
        )
        + (sds((half // 4, ROWS_A, width), BF16),) * 4,
        in_specs=[SMEM] + [ANY] * 13 + [VMEM] * 2 + [ANY],
        out_specs=[VMEM] + [ANY] * 6,
        scratch_shapes=[pltpu.VMEM((PAIRS, rows, 128), BF16)] * 5
        + [
            pltpu.VMEM((rows, width), BF16),
            pltpu.VMEM((rows, width // 2), F32),
            pltpu.VMEM((rows, width // 2), F32),
            pltpu.VMEM((rows, width), BF16),
            pltpu.VMEM((rows, 3 * width), BF16),
            pltpu.VMEM((rows, width), F32),
            pltpu.VMEM((rows, width), F32),
            pltpu.VMEM((PAIRS, width, 128), BF16),
            pltpu.VMEM((rows, width), F32),
            pltpu.VMEM((rows, rows), BF16),
            pltpu.VMEM((rows, width), F32),
            pltpu.VMEM((3 * PAIRS, rows, 128), F32),
            pltpu.VMEM((3, rows, width), BF16),
            pltpu.VMEM((PAIRS, width, 128), F32),
            pltpu.VMEM((BLOCKS, ROWS_A, width), BF16),
            pltpu.VMEM((BLOCKS, ROWS_A, width), BF16),
            pltpu.VMEM((rows, width), F32),
            pltpu.VMEM((16, width), F32),
            pltpu.VMEM((2, 2, rows, rows), BF16),
            pltpu.SemaphoreType.DMA((12,)),
            pltpu.SemaphoreType.DMA((2,)),
            pltpu.SemaphoreType.DMA((13,)),
        ],
        compiler_params=params,
        cost_estimate=cost(27),
        name="tail",
    )(
        place, prob, cg, vals, keys, qu, qv, key_pos, sine, cosine, normed, grouped, pooled, res_grad, vecs,
        vec_grads, wa,
    )
    if direct:
        got_a = [links.send(x, 1) for x in send_a]
        totals_a = links.split_core(keep_a, got_a)
    out3, grad3 = pl.pallas_call(
        bytes_kernel,
        out_shape=(sds((rows, 3 * width), BF16), sds((rows, 3 * width), BF16)),
        in_specs=[VMEM] * 8,
        out_specs=[VMEM] * 2,
        scratch_shapes=[pltpu.VMEM((rows, width), F32)],
        compiler_params=params,
        cost_estimate=cost(1),
        name="bytes",
    )(emb, cot, cols, short_out, w_up_abs, vecs, pooled_grad, w_pool_abs)
    if direct:
        totals_a, near_b, out3, grad3 = lax.optimization_barrier((totals_a, near_b, out3, grad3))
        near_a = links.start_near(totals_a)
        deep_b = links.start_deep(links.total_near(near_b))
    block_output = out3.reshape(byte_total, width)
    input_grad = grad3.reshape(byte_total, width)

    if direct:
        near_a, deep_b = lax.optimization_barrier((near_a, deep_b))
        deep_a = links.start_deep(links.total_near(near_a))
        g_out, g_ff1, g_up, g_ff2 = pl.pallas_call(
            finish_b_kernel,
            out_shape=tuple(sds(w.shape, F32) for w in (w_out, w_ff1, w_up, w_ff2)),
            in_specs=[VMEM] * links.dp,
            out_specs=[VMEM] * 4,
            compiler_params=params,
            name="finish_b",
        )(*[in_vmem(x) for x in deep_b])
        g_pool, g_qkv, g_pos, *vec_out = pl.pallas_call(
            finish_a_kernel,
            out_shape=tuple(sds(w.shape, F32) for w in (w_pool, w_qkv, w_pos))
            + tuple(sds((1, n), F32) for n in lengths),
            in_specs=[SMEM] + [VMEM] * links.dp,
            out_specs=[VMEM] * 13,
            compiler_params=params,
            name="finish_a",
        )(me[None], *[in_vmem(x) for x in deep_a])
        vec_out = [v.reshape(-1) for v in vec_out]
    else:

        def owned(keep, send, layout):
            blocks = jnp.concatenate([keep, *send], axis=0)
            outs = []
            for first, rows_, k in layout:
                if k == 0:
                    outs.append(jnp.tile(blocks[:1, first : first + rows_], (n_dev, 1, 1)))
                else:
                    outs.append(reblock(blocks, [(first, rows_, k)], n_dev))
            full = jnp.concatenate(outs, axis=1)
            full = jnp.zeros_like(full).at[links.places(me, True, True)].set(full)
            return links.reduce(full[: n_dev // 2], full[n_dev // 2 :])

        sum_b = owned(keep_b, send_b, layout_b32)
        sum_a = owned(keep_a, send_a, layout_a32)
        vec_sum = sum_a[r_pool : r_pool + 16]
        vec_out = []
        for first, k, n in zip(vec_first, lengths, vec_rows):
            line = vec_sum[first : first + n].reshape(-1)
            vec_out.append(lax.dynamic_slice(line, (me * k,), (k,)))
        g_pool, g_pos, g_out, g_ff2 = sum_a[:r_pool], sum_a[split_a + 3 * r :], sum_b[:r], sum_b[5 * r : 5 * r + r_ff2]
        g_qkv = unfold(sum_a[split_a : split_a + 3 * r], 3)
        g_ff1 = unfold(sum_b[r : 5 * r], 4)
        g_up = unfold(sum_b[5 * r + r_ff2 :], 3)
    (
        out_pool_b,
        out_ln1_gain,
        out_ln1_bias,
        out_u,
        out_v,
        out_ln2_gain,
        out_ln2_bias,
        out_ff2_b,
        out_ff1_b,
        out_up_b,
    ) = vec_out
    return (
        block_output,
        input_grad,
        g_pool,
        out_pool_b,
        out_ln1_gain,
        out_ln1_bias,
        g_qkv,
        out_u,
        out_v,
        g_pos,
        g_out,
        out_ln2_gain,
        out_ln2_bias,
        g_ff1,
        out_ff1_b,
        g_ff2,
        out_ff2_b,
        g_up,
        out_up_b,
    )


def solution(mesh):
    links = Links(mesh.shape["dp"], mesh.shape["fsdp"])
    rows = P(AXES, None)
    flat = P(AXES)
    ranks = (2, 1, 1, 2, 1, 1, 1, 2, 1, 1, 2, 2, 1, 1, 2, 1, 2, 1, 2, 1, 2)
    out_ranks = (2, 2, 2, 1, 1, 1, 2, 1, 1, 2, 2, 1, 1, 2, 1, 2, 1, 2, 1)
    return jax.shard_map(
        lambda *args: per_device(links, *args),
        mesh=mesh,
        in_specs=tuple(rows if k == 2 else flat for k in ranks),
        out_specs=tuple(rows if k == 2 else flat for k in out_ranks),
        check_vma=False,
    )
```

```python
import jax
import jax.numpy as jnp
from jax import lax
from jax.experimental import pallas as pl
from jax.experimental.pallas import tpu as pltpu
from jax.sharding import PartitionSpec as P

H = 8
DH = 64
QBLK = 256
AXES = ("dp", "fsdp")


eps_norm = 1e-05
big_negative = -1e30

F32 = jnp.float32
BF16 = jnp.bfloat16
BLOCKS = 32
PAIRS = 4
CH = 64
VMEM = pl.BlockSpec(memory_space=pltpu.VMEM)
SMEM = pl.BlockSpec(memory_space=pltpu.SMEM)
ANY = pl.BlockSpec(memory_space=pl.ANY)
GELU_C = 0.7978845608028654
ROWS_A = 128
ROWS_B = 192
ROWS_C = 48
VEC = slice(48, 64)


def mm(left, right, cl=1, cr=0):
    return lax.dot_general(left, right, (((cl,), (cr,)), ((), ())), preferred_element_type=F32)


def weight(ref, start, rows):
    block = ref[:, start : start + rows, :]
    return block.reshape(block.shape[0] * rows, block.shape[2])


def weight_ff2(ref, start, j):
    block = ref[8 * j : 8 * j + 8, start : start + 64, :]
    return block.reshape(512, block.shape[2])


def start_copy(source, dest, sem):
    copy = pltpu.make_async_copy(source, dest, sem)
    copy.start()
    return copy


def load_rows(me, plan, refs, dest, first, stop, sem):
    for (start, blocks), ref in zip(plan, refs):
        low, high = max(first, start), min(stop, start + ref.shape[1])
        if low < high:
            for k, (base, mask) in enumerate(blocks):
                pltpu.make_async_copy(
                    ref.at[k, pl.ds(low - start, high - low)],
                    dest.at[base + (me ^ mask), pl.ds(low, high - low)],
                    sem,
                ).start()


def wait_rows(dest, first, stop, sem):
    rows = dest.at[:, pl.ds(first, stop - first)]
    pltpu.make_async_copy(rows, rows, sem).wait()


def lane_half(shape, s):
    return (lax.broadcasted_iota(jnp.int32, shape, len(shape) - 1) // DH) == s


def norm_stats(x):
    width = x.shape[-1]
    mean = jnp.sum(x, axis=-1, keepdims=True) * (1.0 / width)
    centre = x - mean
    var = jnp.sum(centre * centre, axis=-1, keepdims=True) * (1.0 / width)
    rstd = lax.rsqrt(var + eps_norm)
    return centre * rstd, rstd


def norm_back(dy, xhat, rstd, gain):
    width = dy.shape[-1]
    d = dy * gain
    m1 = jnp.sum(d, axis=-1, keepdims=True) * (1.0 / width)
    m2 = jnp.sum(d * xhat, axis=-1, keepdims=True) * (1.0 / width)
    return rstd * (d - m1 - xhat * m2)


def forward_kernel(plan, n_pieces, me_ref, *refs):
    pieces = refs[:n_pieces]
    (grouped_hbm, item_col, item_row, sine_hbm, cosine_hbm, key_pos_hbm) = refs[
        n_pieces : n_pieces + 6
    ]
    hbm = refs[n_pieces + 6 : n_pieces + 14]
    vecs, w_out_hbm = refs[n_pieces + 14 : n_pieces + 16]
    (grouped, sine, cosine, pooled, normed, qu, qv, keys, vals, prob, ctx) = refs[
        n_pieces + 16 : n_pieces + 27
    ]
    (w, w_pos, bias, proj, qcat, kcat, tmp, scores, sem, sem2) = refs[n_pieces + 27 :]
    (pooled_hbm, normed_hbm, qu_hbm, qv_hbm, keys_hbm, vals_hbm, prob_hbm, ctx_hbm) = hbm
    me = me_ref[0]
    rows = grouped.shape[0]
    load_rows(me, plan, pieces, w, 0, 64, sem.at[0])
    get_grouped = start_copy(grouped_hbm, grouped, sem2.at[0])
    load_rows(me, plan, pieces, w, 64, ROWS_A, sem.at[1])
    get_sine = start_copy(sine_hbm, sine, sem2.at[1])
    get_cosine = start_copy(cosine_hbm, cosine, sem2.at[2])
    get_key_pos = start_copy(key_pos_hbm, kcat.at[:, 0:rows], sem2.at[3])
    for r in range(0, rows, CH):
        row = r + lax.broadcasted_iota(jnp.int32, (CH, rows), 0)
        col = lax.broadcasted_iota(jnp.int32, (CH, rows), 1)
        allowed = (item_col[r : r + CH, :] == item_row[...]) & (row >= col)
        bias[r : r + CH, :] = jnp.where(allowed, 0.0, big_negative)
    wait_rows(w, 0, 64, sem.at[0])
    get_grouped.wait()
    vec = jnp.sum(w[:, VEC, :].astype(F32), axis=0)
    vecs[...] = vec
    tmp[...] = mm(grouped[...], weight(w, 0, 48))
    for r in range(0, rows, CH):
        x = tmp[r : r + CH, :] + vec[0:1]
        pooled[r : r + CH, :] = x
        xhat, rstd = norm_stats(x)
        normed[r : r + CH, :] = (xhat * vec[1:2] + vec[2:3]).astype(BF16)
    wait_rows(w, 64, ROWS_A, sem.at[1])
    puts = [
        start_copy(w, w_out_hbm, sem2.at[4]),
        start_copy(pooled, pooled_hbm, sem2.at[5]),
        start_copy(normed, normed_hbm, sem2.at[6]),
    ]
    tmp[...] = mm(normed[...], weight(w, 64, 16))
    for r in range(0, rows, CH):
        x = tmp[r : r + CH, :]
        u = (x + vec[3:4]).astype(BF16)
        v = (x + vec[4:5]).astype(BF16)
        for p in range(PAIRS):
            qu[p, r : r + CH, :] = u[:, 128 * p : 128 * p + 128]
            qv[p, r : r + CH, :] = v[:, 128 * p : 128 * p + 128]
    x = mm(normed[...], weight(w, 80, 16)).astype(BF16)
    for p in range(PAIRS):
        keys[p] = x[:, 128 * p : 128 * p + 128]
    x = mm(normed[...], weight(w, 96, 16)).astype(BF16)
    for p in range(PAIRS):
        vals[p] = x[:, 128 * p : 128 * p + 128]
    x = weight(w, 112, 16)
    for p in range(PAIRS):
        w_pos[p] = x[:, 128 * p : 128 * p + 128]

    puts += [
        start_copy(x, y, sem2.at[7 + j])
        for j, (x, y) in enumerate(((qu, qu_hbm), (qv, qv_hbm), (keys, keys_hbm), (vals, vals_hbm)))
    ]
    get_sine.wait()
    get_cosine.wait()
    get_key_pos.wait()

    def put_prob(p):
        pair = pl.ds(2 * p, 2)
        return pltpu.make_async_copy(prob.at[pair], prob_hbm.at[pair], sem2.at[11])

    @pl.loop(0, PAIRS)
    def _(p):
        kcat[:, rows : rows + 128] = keys[p]
        zero = jnp.zeros((rows, 128), BF16)
        halves = [lane_half((rows, 128), s) for s in range(2)]

        def project(s):
            proj[s] = mm(jnp.where(halves[s], qv[p], zero), w_pos[p], 1, 1)

        def rotate(s):
            for r in range(0, rows, CH):
                a = proj[s, r : r + CH, 0:256]
                b = proj[s, r : r + CH, 256:512]
                si = sine[r : r + CH, :]
                co = cosine[r : r + CH, :]
                qcat[s, r : r + CH, 0:256] = (a * si + b * co).astype(BF16)
                qcat[s, r : r + CH, 256:512] = (b * si - a * co).astype(BF16)
            qcat[s, :, 512:640] = jnp.where(halves[s], qu[p], zero)

        def score(s, q):
            first, stop = q * QBLK, (q + 1) * QBLK
            scores[s, first:stop, 0:stop] = mm(qcat[s, first:stop, :], kcat[0:stop, :], 1, 1)

        def softmax(s, q):
            first, stop = q * QBLK, (q + 1) * QBLK
            for r in range(first, stop, CH):
                x = scores[s, r : r + CH, 0:stop] * (DH ** (-0.5)) + bias[r : r + CH, 0:stop]
                e = jnp.exp(x - jnp.max(x, axis=-1, keepdims=True))
                inv = 1.0 / jnp.sum(e, axis=-1, keepdims=True)
                prob[2 * p + s, r : r + CH, 0:stop] = (e * inv).astype(BF16)

        def context(s, q):
            first, stop = q * QBLK, (q + 1) * QBLK
            out = mm(prob[2 * p + s, first:stop, 0:stop], vals[p, 0:stop, :]).astype(BF16)
            if s == 1:
                out = jnp.where(lane_half((QBLK, 128), 1), out, ctx[p, first:stop, :])
            ctx[p, first:stop, :] = out

        project(0)
        project(1)
        rotate(0)
        score(0, 0)
        score(0, 1)
        rotate(1)
        softmax(0, 0)
        score(1, 0)
        score(1, 1)
        softmax(0, 1)
        context(0, 0)
        softmax(1, 0)
        context(0, 1)
        softmax(1, 1)
        context(1, 0)
        context(1, 1)
        put_prob(p).start()

    puts.append(start_copy(ctx, ctx_hbm, sem2.at[12]))
    pltpu.make_async_copy(prob, prob_hbm, sem2.at[11]).wait()
    for c in puts:
        c.wait()


def join(ref):
    return jnp.concatenate([ref[p] for p in range(PAIRS)], axis=1)


def store_blocks(grads, place_ref, line, grad, first, rows=16, start=0):
    for k in range(grad.shape[0] // rows):
        grads[place_ref[line, start + k], first : first + rows, :] = grad[k * rows : (k + 1) * rows].astype(BF16)


def put_blocks(grads, keep_hbm, send_hbm, first, stop, sem):
    rows = pl.ds(first, stop - first)
    half = BLOCKS // 2
    copies = []
    start = half
    for j, ref in enumerate(send_hbm):
        n = ref.shape[0]
        copies.append(start_copy(grads.at[pl.ds(start, n), rows], ref.at[:, rows], sem.at[1 + j]))
        start += n
    copies.append(start_copy(grads.at[pl.ds(0, half), rows], keep_hbm.at[:, rows], sem.at[0]))
    return copies


def middle_kernel(plan, n_pieces, me_ref, place_ref, *refs):
    pieces = refs[:n_pieces]
    (pooled_hbm, ctx_hbm, up_grad_hbm, vecs) = refs[n_pieces : n_pieces + 4]
    (res_grad_hbm, cg, short_out_hbm, vec_grads, w_up_hbm, keep_hbm, send_hbm) = refs[
        n_pieces + 4 : n_pieces + 11
    ]
    (pooled, ctx, up_grad, res_grad, short_out) = refs[n_pieces + 11 : n_pieces + 16]
    (w, grads, xhat, rstd, n2, hidden, pre, slope, acc, tmp, sgrad, bg, attn, sem, sem2, sem3) = refs[
        n_pieces + 16 :
    ]
    me = me_ref[0]
    rows = pooled.shape[0]
    load_rows(me, plan, pieces, w, 0, 80, sem.at[0])
    get_ctx = start_copy(ctx_hbm, ctx, sem2.at[0])
    get_pooled = start_copy(pooled_hbm, pooled, sem2.at[1])
    load_rows(me, plan, pieces, w, 80, 144, sem.at[1])
    load_rows(me, plan, pieces, w, 144, ROWS_B, sem.at[2])
    get_up_grad = start_copy(up_grad_hbm, up_grad, sem2.at[2])
    get_ctx.wait()
    get_pooled.wait()
    wait_rows(w, 0, 80, sem.at[0])
    gain2, bias2 = vecs[5:6, :], vecs[6:7, :]
    acc[...] = pooled[...] + mm(join(ctx), weight(w, 0, 16))
    for r in range(0, rows, CH):
        xh, rs = norm_stats(acc[r : r + CH, :])
        xhat[r : r + CH, :] = xh
        rstd[r : r + CH, :] = jnp.broadcast_to(rs, (CH, 128))
        n2[r : r + CH, :] = (xh * gain2 + bias2).astype(BF16)

    def first_layer(j):
        tmp[j] = mm(n2[...], weight(w, 16 + 16 * j, 16))

    def activate(j):
        b1 = vecs[8 + j : 9 + j, :]
        for r in range(0, rows, CH):
            x = tmp[j, r : r + CH, :] + b1
            x2 = x * x
            t = jnp.tanh(GELU_C * (x + 0.044715 * (x * x2)))
            hidden[r : r + CH, 512 * j : 512 * j + 512] = (0.5 * x * (1.0 + t)).astype(BF16)
            slope[j, r : r + CH, :] = 0.5 * (1.0 + t) + (0.5 * GELU_C) * x * (1.0 - t * t) * (
                1.0 + (3.0 * 0.044715) * x2
            )

    def up_back(j):
        return mm(up_grad[:, 512 * j : 512 * j + 512], weight(w, 144 + 16 * j, 16), 1, 1)

    def second_layer(j):
        return mm(hidden[:, 512 * j : 512 * j + 512], weight_ff2(w, 80, j))

    first_layer(0)
    first_layer(1)
    activate(0)
    wait_rows(w, 80, 144, sem.at[1])
    first_layer(2)
    activate(1)
    acc[...] += second_layer(0)
    first_layer(3)
    activate(2)
    acc[...] += second_layer(1)
    wait_rows(w, 144, ROWS_B, sem.at[2])
    get_up_grad.wait()
    sgrad[...] = up_back(0) + up_back(1)
    activate(3)
    acc[...] += second_layer(2)
    sgrad[...] += up_back(2)
    acc[...] += second_layer(3)
    bg[...] = sgrad[...].astype(BF16)
    short_out[...] = (acc[...] + vecs[7:8, :]).astype(BF16)
    puts = [
        start_copy(w.at[:, pl.ds(144, 48)], w_up_hbm, sem2.at[3]),
        start_copy(short_out, short_out_hbm, sem2.at[4]),
    ]

    def hidden_back(j):
        tmp[j] = mm(bg[...], weight_ff2(w, 80, j), 1, 1)

    def activate_back(j):
        total = jnp.zeros((1, 512), F32)
        for r in range(0, rows, CH):
            x = (tmp[j, r : r + CH, :] * slope[j, r : r + CH, :]).astype(BF16)
            pre[r : r + CH, 512 * j : 512 * j + 512] = x
            total = total + jnp.sum(x.astype(F32), axis=0, keepdims=True)
        vec_grads[8 + j : 9 + j, :] = total

    def up_weights(j):
        g = mm(short_out[...], up_grad[:, 512 * j : 512 * j + 512], 0, 0)
        store_blocks(grads, place_ref, 0, g, 144 + 16 * j)

    def second_weights(j):
        g = mm(hidden[:, 512 * j : 512 * j + 512], bg[...], 0, 0)
        store_blocks(grads, place_ref, 0, g, 80, 64, 8 * j)

    def first_weights(j):
        g = mm(n2[...], pre[:, 512 * j : 512 * j + 512], 0, 0)
        store_blocks(grads, place_ref, 0, g, 16 + 16 * j)

    def first_back(j):
        return mm(pre[:, 512 * j : 512 * j + 512], weight(w, 16 + 16 * j, 16), 1, 1)

    vec_grads[...] = jnp.zeros(vec_grads.shape, F32)
    hidden_back(0)
    hidden_back(1)
    activate_back(0)
    hidden_back(2)
    activate_back(1)
    acc[...] = first_back(0)
    hidden_back(3)
    activate_back(2)
    acc[...] += first_back(1)
    second_weights(0)
    activate_back(3)
    acc[...] += first_back(2)
    second_weights(1)
    acc[...] += first_back(3)
    second_weights(2)
    second_weights(3)
    dgain = jnp.zeros((1, 512), F32)
    dbias = jnp.zeros((1, 512), F32)
    for r in range(0, rows, CH):
        dy = acc[r : r + CH, :]
        xh = xhat[r : r + CH, :]
        dgain = dgain + jnp.sum(dy * xh, axis=0, keepdims=True)
        dbias = dbias + jnp.sum(dy, axis=0, keepdims=True)
        x = sgrad[r : r + CH, :] + norm_back(dy, xh, rstd[r : r + CH, 0:1], gain2)
        res_grad[r : r + CH, :] = x
        attn[r : r + CH, :] = x.astype(BF16)
    vec_grads[5:6, :] = dgain
    vec_grads[6:7, :] = dbias
    up_weights(0)
    up_weights(1)
    up_weights(2)
    puts += put_blocks(grads, keep_hbm, (send_hbm,), 80, ROWS_B, sem3.at[0])
    first_weights(0)
    first_weights(1)
    first_weights(2)
    first_weights(3)
    puts += put_blocks(grads, keep_hbm, (send_hbm,), 16, 80, sem3.at[1])
    for j in range(3):
        vec_grads[12 + j : 13 + j, :] = jnp.sum(
            up_grad[:, 512 * j : 512 * j + 512].astype(F32), axis=0, keepdims=True
        )
    vec_grads[7:8, :] = jnp.sum(bg[...].astype(F32), axis=0, keepdims=True)
    store_blocks(grads, place_ref, 0, mm(join(ctx), attn[...], 0, 0), 0)
    puts += put_blocks(grads, keep_hbm, (send_hbm,), 0, 16, sem3.at[2])
    puts.append(start_copy(res_grad, res_grad_hbm, sem2.at[5]))
    x = mm(attn[...], weight(w, 0, 16), 1, 1).astype(BF16)
    for p in range(PAIRS):
        cg[p] = x[:, 128 * p : 128 * p + 128]
    for c in puts:
        c.wait()


def tail_kernel(
    place_ref, prob, cg_hbm, vals_hbm, keys_hbm, qu_hbm, qv_hbm, key_pos_hbm, sine_hbm, cosine_hbm,
    normed_hbm, grouped_hbm, pooled_hbm, res_grad_hbm, vecs, vec_in, w_hbm,
    pg, w_pool_out, keep_hbm, send0, send1, send2, send3,
    cg, vals, keys, qu, qv, key_pos, sine, cosine, normed, grouped, pooled, res_grad,
    w_pos, pgrad, sg, posg, qg, qkvg, pos_w_grad, w, grads, acc, vec, prob_v, sem, prob_sem, get_sem,
):
    rows = key_pos.shape[0]
    n_q = rows // QBLK
    pairs = ((cg_hbm, cg), (vals_hbm, vals), (keys_hbm, keys), (qu_hbm, qu), (qv_hbm, qv))
    first_gets = [start_copy(x, y, get_sem.at[j]) for j, (x, y) in enumerate(pairs)]

    def fetch(p):
        return pltpu.make_async_copy(prob.at[pl.ds(2 * p, 2)], prob_v.at[p % 2], prob_sem.at[p % 2])

    fetch(0).start()
    tables = ((key_pos_hbm, key_pos), (sine_hbm, sine), (cosine_hbm, cosine))
    first_gets += [start_copy(x, y, get_sem.at[5 + j]) for j, (x, y) in enumerate(tables)]
    load = start_copy(w_hbm.at[:, pl.ds(112, 16)], w.at[:, pl.ds(112, 16)], sem.at[0])
    late = ((normed_hbm, normed), (grouped_hbm, grouped), (pooled_hbm, pooled), (res_grad_hbm, res_grad))
    late_gets = [start_copy(x, y, get_sem.at[8 + j]) for j, (x, y) in enumerate(late)]
    late_gets.append(start_copy(w_hbm.at[:, pl.ds(0, 112)], w.at[:, pl.ds(0, 112)], get_sem.at[12]))
    vec[...] = vec_in[...]
    load.wait()
    for c in first_gets:
        c.wait()
    x = weight(w, 112, 16)
    for p in range(PAIRS):
        w_pos[p] = x[:, 128 * p : 128 * p + 128]

    @pl.loop(0, PAIRS)
    def _(p):
        @pl.when(p + 1 < PAIRS)
        def _():
            fetch(p + 1).start()

        fetch(p).wait()
        slot = p % 2
        u_sums = []
        v_sums = []
        for s in range(2):
            half = lane_half((rows, 128), s)
            zero = jnp.zeros((rows, 128), BF16)
            cgm = jnp.where(half, cg[p], zero)
            qum = jnp.where(half, qu[p], zero)
            qvm = jnp.where(half, qv[p], zero)
            for q in range(n_q):
                first, stop = q * QBLK, (q + 1) * QBLK
                pgrad[first:stop, 0:stop] = mm(cgm[first:stop], vals[p, 0:stop, :], 1, 1)
                for r in range(first, stop, CH):
                    pr = prob_v[slot, s, r : r + CH, 0:stop].astype(F32)
                    t = pr * pgrad[r : r + CH, 0:stop]
                    inner = jnp.sum(t, axis=-1, keepdims=True)
                    sg[r : r + CH, 0:stop] = ((t - pr * inner) * (DH ** (-0.5))).astype(BF16)
                posg[first:stop, :] = mm(sg[first:stop, 0:stop], key_pos[0:stop, :])
                part = mm(sg[first:stop, 0:stop], keys[p, 0:stop, :])
                if s == 0:
                    qg[p, first:stop, :] = part
                else:
                    qg[p, first:stop, :] = jnp.where(
                        lane_half((QBLK, 128), 1), part, qg[p, first:stop, :]
                    )
                kg = mm(sg[first:stop, 0:stop], qum[first:stop], 0, 0)
                vg = mm(prob_v[slot, s, first:stop, 0:stop], cgm[first:stop], 0, 0)
                if s == 0 and q == 0:
                    qg[PAIRS + p] = jnp.zeros((rows, 128), F32)
                    qg[2 * PAIRS + p] = jnp.zeros((rows, 128), F32)
                qg[PAIRS + p, 0:stop, :] += kg
                qg[2 * PAIRS + p, 0:stop, :] += vg
            for r in range(0, rows, CH):
                a = posg[r : r + CH, 0:256]
                b = posg[r : r + CH, 256:512]
                si = sine[r : r + CH, :]
                co = cosine[r : r + CH, :]
                sg[r : r + CH, 0:256] = (a * si - b * co).astype(BF16)
                sg[r : r + CH, 256:512] = (a * co + b * si).astype(BF16)
            gw = mm(sg[...], qvm, 0, 0)
            if s == 0:
                pos_w_grad[p] = gw
            else:
                pos_w_grad[p] += gw
            qvg = jnp.where(half, mm(sg[...], w_pos[p]), 0.0)
            v_sums.append(jnp.sum(qvg, axis=0, keepdims=True))
            u_sums.append(jnp.sum(jnp.where(half, qg[p], 0.0), axis=0, keepdims=True))
            qg[p] += qvg
        u_row = u_sums[0] + u_sums[1]
        v_row = v_sums[0] + v_sums[1]
        for k in range(PAIRS):

            @pl.when(p == k)
            def _():
                vec[3:4, 128 * k : 128 * k + 128] = u_row
                vec[4:5, 128 * k : 128 * k + 128] = v_row

    for c in late_gets:
        c.wait()
    for j in range(3):
        for p in range(PAIRS):
            qkvg[j, :, 128 * p : 128 * p + 128] = qg[PAIRS * j + p].astype(BF16)
    for j in range(3):
        store_blocks(grads, place_ref, 1, mm(normed[...], qkvg[j], 0, 0), 64 + 16 * j)
    store_blocks(grads, place_ref, 1, join(pos_w_grad), 112)
    sends = (send0, send1, send2, send3)
    puts = put_blocks(grads, keep_hbm, sends, 64, ROWS_A, sem.at[pl.ds(2, 5)])
    keep_pool = pltpu.make_async_copy(w.at[:, 0:48], w_pool_out, sem.at[1])
    keep_pool.start()
    acc[...] = (
        mm(qkvg[0], weight(w, 64, 16), 1, 1)
        + mm(qkvg[1], weight(w, 80, 16), 1, 1)
        + mm(qkvg[2], weight(w, 96, 16), 1, 1)
    )
    gain1 = vecs[1:2, :]
    dgain = jnp.zeros((1, 512), F32)
    dbias = jnp.zeros((1, 512), F32)
    dpool = jnp.zeros((1, 512), F32)
    for r in range(0, rows, CH):
        dy = acc[r : r + CH, :]
        xh, rs = norm_stats(pooled[r : r + CH, :])
        dgain = dgain + jnp.sum(dy * xh, axis=0, keepdims=True)
        dbias = dbias + jnp.sum(dy, axis=0, keepdims=True)
        x = (res_grad[r : r + CH, :] + norm_back(dy, xh, rs, gain1)).astype(BF16)
        pg[r : r + CH, :] = x
        dpool = dpool + jnp.sum(x.astype(F32), axis=0, keepdims=True)
    vec[0:1, :] = dpool
    vec[1:2, :] = dgain
    vec[2:3, :] = dbias
    table = vec[...].astype(BF16)
    for d in range(BLOCKS):
        grads[place_ref[1, d], VEC, :] = table
    for j in range(3):
        g = mm(grouped[:, 512 * j : 512 * j + 512], pg[...], 0, 0)
        for k in range(32):
            granule = 32 * j + k
            d, sub = granule // 3, granule % 3
            grads[place_ref[1, d], 16 * sub : 16 * sub + 16, :] = g[16 * k : 16 * k + 16].astype(BF16)
    puts += put_blocks(grads, keep_hbm, sends, 0, 64, sem.at[pl.ds(7, 5)])
    keep_pool.wait()
    for c in puts:
        c.wait()


def bytes_kernel(emb, cot, cols, short_out, w_up, vecs, pg, w_pool, out, grad, tmp):
    rows = emb.shape[0]
    for j in range(3):
        tmp[...] = mm(short_out[...], weight(w_up, 16 * j, 16))
        up_bias = vecs[12 + j : 13 + j, :]
        for r in range(0, rows, CH):
            x = emb[r : r + CH, 512 * j : 512 * j + 512].astype(F32) + tmp[r : r + CH, :] + up_bias
            out[r : r + CH, 512 * j : 512 * j + 512] = jnp.where(
                cols[r : r + CH, j : j + 1] > 0, x, 0.0
            ).astype(BF16)
    pool = weight(w_pool, 0, 48)
    for j in range(3):
        src = (j + 2) % 3
        tmp[...] = mm(pg[...], pool[512 * src : 512 * src + 512, :], 1, 1)
        if j > 0:
            tmp[...] = pltpu.roll(tmp[...], rows - 1, 0)
        for r in range(0, rows, CH):
            x = tmp[r : r + CH, :]
            if j > 0:
                x = jnp.where(cols[r : r + CH, 3:4] > 0, x, 0.0)
            x = cot[r : r + CH, 512 * j : 512 * j + 512].astype(F32) + x
            grad[r : r + CH, 512 * j : 512 * j + 512] = jnp.where(
                cols[r : r + CH, j : j + 1] > 0, x, 0.0
            ).astype(BF16)


def pack_kernel(me_ref, *refs):
    (w_pool, w_qkv, w_pos, w_out, w_ff1, w_ff2, w_up) = refs[:7]
    vectors = refs[7:17]
    all_a, all_b, out_c, out_a, out_b, sem = refs[17:]
    me = me_ref[0]
    out_a[0:48, :] = w_pool[...]
    for j in range(3):
        out_a[64 + 16 * j : 80 + 16 * j, :] = w_qkv[:, 512 * j : 512 * j + 512]
        out_c[0, 16 * j : 16 + 16 * j, :] = w_up[:, 512 * j : 512 * j + 512]
    out_a[112:128, :] = w_pos[...]
    out_b[0:16, :] = w_out[...]
    for j in range(4):
        out_b[16 + 16 * j : 32 + 16 * j, :] = w_ff1[:, 512 * j : 512 * j + 512]
    out_b[80:144, :] = w_ff2[...]

    def spread(x, first):
        k = x.shape[1]
        lane = first + lax.broadcasted_iota(jnp.int32, (k, 512), 1)
        row = lax.broadcasted_iota(jnp.int32, (k, 512), 0)
        pick = jnp.where(lane % k == row, 1.0, 0.0).astype(BF16)
        own = (first + lax.broadcasted_iota(jnp.int32, (x.shape[0], 512), 1)) // k == me
        return jnp.where(own, mm(x, pick), 0.0)

    lines = [spread(v[...], 0) for v in vectors[:8]]
    lines += [spread(vectors[8][...], 512 * j) for j in range(4)]
    lines += [spread(vectors[9][...], 512 * j) for j in range(3)]
    lines.append(jnp.zeros((1, 512), F32))
    out_a[VEC, :] = jnp.concatenate(lines, axis=0).astype(BF16)
    copies = []
    for j in range(all_a.shape[0]):
        copies.append(pltpu.make_async_copy(out_a, all_a.at[j], sem.at[j]))
    for j in range(all_b.shape[0]):
        copies.append(pltpu.make_async_copy(out_b, all_b.at[j], sem.at[all_a.shape[0] + j]))
    for c in copies:
        c.start()
    for c in copies:
        c.wait()


def finish_b_kernel(*refs):
    out, ff1, up, ff2 = refs[-4:]
    total = refs[0][0].astype(F32)
    for ref in refs[1:-4]:
        total = total + ref[0].astype(F32)
    out[...] = total[0:16]
    for j in range(4):
        ff1[:, 512 * j : 512 * j + 512] = total[16 + 16 * j : 32 + 16 * j]
    for j in range(3):
        up[:, 512 * j : 512 * j + 512] = total[144 + 16 * j : 160 + 16 * j]
    ff2[...] = total[80:144]


def finish_a_kernel(me_ref, *refs):
    me = me_ref[0]
    parts, (pool, qkv, pos), vectors = refs[:-13], refs[-13:-10], refs[-10:]
    total = parts[0][0].astype(F32)
    for ref in parts[1:]:
        total = total + ref[0].astype(F32)
    pool[...] = total[0:48]
    for j in range(3):
        qkv[:, 512 * j : 512 * j + 512] = total[64 + 16 * j : 80 + 16 * j]
    pos[...] = total[112:128]
    table = total[VEC]
    lines = pltpu.roll(table[0:8], 512 - 16 * me, 1)
    for j in range(8):
        vectors[j][...] = lines[j : j + 1, 0:16]
    row = lax.broadcasted_iota(jnp.int32, (16, 512), 0)

    def line(j):
        return jnp.sum(jnp.where(row == j, table, 0.0), axis=0, keepdims=True)

    def part(first, length):
        j, off = first // 512, first % 512
        here = pltpu.roll(jnp.broadcast_to(line(j), (8, 512)), 512 - off, 1)
        there = pltpu.roll(jnp.broadcast_to(line(j + 1), (8, 512)), 512 - off, 1)
        lane = lax.broadcasted_iota(jnp.int32, (8, 512), 1)
        return jnp.where(lane < 512 - off, here, there)[0:1, 0:length]

    vectors[8][...] = part(8 * 512 + 64 * me, 64)
    vectors[9][...] = part(12 * 512 + 48 * me, 48)


class Links:
    def __init__(self, dp, fsdp):
        self.dp = dp
        self.fsdp = fsdp
        self.count = dp * fsdp
        self.near = [2 * m for m in range(fsdp // 2)]

    def send(self, values, mask):
        return lax.ppermute(values, AXES, [(i, i ^ mask) for i in range(self.count)])

    def deep(self, blocks):
        return lax.all_to_all(blocks, "dp", 0, 0, tiled=True)

    def gather_near(self, held):
        return [held] + [self.send(held, m) for m in self.near[1:]]

    def gather_core(self, pieces):
        return pieces + [
            (first, [(z, m ^ 1) for z, m in blocks], self.send(array, 1)) for first, blocks, array in pieces
        ]

    def near_pieces(self, first, near):
        return [(first, [(z, m) for z in range(self.dp)], x) for m, x in zip(self.near, near)]

    def places(self, me, by_place, by_plane):
        owner = jnp.arange(self.count, dtype=jnp.int32)
        place = (owner if by_place else owner ^ me) % self.fsdp // 2
        plane = (owner if by_plane else owner ^ me) // self.fsdp
        return ((owner ^ me) % 2 * (self.fsdp // 2) + place) * self.dp + plane

    def start_deep(self, blocks):
        return [blocks[:1]] + [
            self.send(blocks[m : m + 1], self.fsdp * m) for m in range(self.dp - 1, 0, -1)
        ]

    def split_core(self, keep, got):
        n = self.dp
        return [
            add(keep[k * n : k * n + n], got[k]).astype(BF16)
            for k in range(len(self.near))
        ]

    def start_near(self, totals):
        return totals[:1] + [self.send(t, m) for t, m in zip(totals[1:], self.near[1:])]

    def swap_near(self, blocks):
        groups = [list(range(c, self.fsdp, 2)) for c in range(2)]
        return lax.all_to_all(blocks, "fsdp", 0, 0, axis_index_groups=groups, tiled=True)

    def total_core(self, keep, got):
        outs = []
        first = 0
        for x in got:
            outs.append(add(keep[first : first + x.shape[0]], x).astype(BF16))
            first += x.shape[0]
        return jnp.concatenate(outs, axis=0) if len(outs) > 1 else outs[0]

    def total_near(self, parts):
        if not isinstance(parts, list):
            parts = [parts[k : k + self.dp] for k in range(0, parts.shape[0], self.dp)]
        total = parts[0].astype(F32)
        for x in parts[1:]:
            total = total + x.astype(F32)
        return total.astype(BF16)

    def total_deep(self, parts):
        return jnp.sum(parts.astype(F32), axis=0)

    def reduce(self, keep, send):
        near = self.swap_near(self.total_core(keep, [self.send(send, 1)]))
        return self.total_deep(self.deep(self.total_near(near)))


def in_vmem(x):
    return pltpu.with_memory_space_constraint(x, pltpu.VMEM)


def add(left, right):
    return left.astype(F32) + right.astype(F32)


def cost(us):
    return pl.CostEstimate(flops=us * 10**9, transcendentals=0, bytes_accessed=us * 10**6)


def in_vmem(x):
    return pltpu.with_memory_space_constraint(x, pltpu.VMEM)


def add(left, right):
    return left.astype(F32) + right.astype(F32)


def fold(shard, width):
    return jnp.concatenate(
        [shard[..., j : j + width] for j in range(0, shard.shape[-1], width)], axis=-2
    )


def unfold(block, count):
    rows = block.shape[-2] // count
    return jnp.concatenate(
        [block[..., j * rows : (j + 1) * rows, :] for j in range(count)], axis=-1
    )


def reblock(blocks, layout, count):
    m = blocks.shape[0]
    outs = []
    for first, rows, k in layout:
        x = unfold(blocks[:, first : first + rows], k)
        x = x.reshape(m * x.shape[1], x.shape[2]).reshape(count, -1, x.shape[2])
        outs.append(fold(x, blocks.shape[2]))
    return jnp.concatenate(outs, axis=1)


def layout_of(parts):
    out = []
    first = 0
    for rows, k in parts:
        out.append((first, rows, k))
        first += rows
    return out


def per_device(links, *args):
    (
        byte_embeddings,
        byte_item,
        byte_mask,
        w_pool,
        b_pool,
        ln1_gain,
        ln1_bias,
        w_qkv,
        pos_u,
        pos_v,
        w_pos,
        w_out,
        ln2_gain,
        ln2_bias,
        w_ff1,
        b_ff1,
        w_ff2,
        b_ff2,
        w_up,
        b_up,
        cotangent,
    ) = args
    n_dev = links.count
    me = lax.axis_index(AXES).astype(jnp.int32)
    width = w_pos.shape[1]
    r_pool, r, r_ff2 = w_pool.shape[0], w_pos.shape[0], w_ff2.shape[0]
    direct = n_dev == BLOCKS
    vectors = [b_pool, ln1_gain, ln1_bias, pos_u, pos_v, ln2_gain, ln2_bias, b_ff2, b_ff1, b_up]
    lengths = [v.shape[0] for v in vectors]
    vec_rows = [v * n_dev // width for v in lengths]
    vec_first = [sum(vec_rows[:i]) for i in range(len(vec_rows))]

    params = pltpu.CompilerParams(vmem_limit_bytes=60 << 20)
    sds = jax.ShapeDtypeStruct
    if direct:
        shard_a, shard_b, shard_c = pl.pallas_call(
            pack_kernel,
            out_shape=(
                sds((links.dp, ROWS_A, width), BF16),
                sds((links.dp, ROWS_B - ROWS_C, width), BF16),
                sds((1, ROWS_C, width), BF16),
            ),
            in_specs=[SMEM] + [VMEM] * 17,
            out_specs=[ANY] * 2 + [VMEM],
            scratch_shapes=[
                pltpu.VMEM((ROWS_A, width), BF16),
                pltpu.VMEM((ROWS_B - ROWS_C, width), BF16),
                pltpu.SemaphoreType.DMA((2 * links.dp,)),
            ],
            compiler_params=params,
            cost_estimate=cost(3),
        name="pack",
        )(me[None], w_pool, w_qkv, w_pos, w_out, w_ff1, w_ff2, w_up, *[v[None] for v in vectors])
    else:
        flat = jnp.arange(n_dev * lengths[8])
        table = []
        for v in vectors:
            k = v.shape[0]
            spread = jnp.where(flat[: n_dev * k] // k == me, jnp.tile(v, n_dev), jnp.zeros((), v.dtype))
            table.append(spread.reshape(-1, width))
        table.append(jnp.zeros((16 - sum(vec_rows), width), BF16))
        shard_a = jnp.concatenate([w_pool] + table + [fold(w_qkv, width), w_pos], axis=0)
        shard_b = jnp.concatenate([w_out, fold(w_ff1, width), w_ff2], axis=0)
        shard_c = fold(w_up, width)[None]
        shard_a, shard_b = [
            jnp.broadcast_to(x[None], (links.dp,) + x.shape) for x in (shard_a, shard_b)
        ]
    split_a = r_pool + 16
    byte_total = byte_embeddings.shape[0]
    rows = byte_total // 3
    emb = byte_embeddings.reshape(rows, 3 * width)
    cot = cotangent.reshape(rows, 3 * width)
    mask3 = byte_mask.reshape(rows, 3)
    item = byte_item.reshape(rows, 3)[:, 0]
    same = item[1:] == item[:-1]
    no = jnp.zeros((1,), jnp.bool_)
    same_before = jnp.concatenate([no, same])[:, None]
    same_after = jnp.concatenate([same, no])[:, None]
    cols = jnp.concatenate([mask3, same_after.astype(jnp.int32)], axis=1)
    item_f = item.astype(F32)
    live = [mask3[:, j : j + 1] > 0 for j in range(3)]
    zero = jnp.zeros((), jnp.bfloat16)
    masked = [jnp.where(live[j], emb[:, j * width : (j + 1) * width], zero) for j in range(3)]
    up_grad = jnp.concatenate(
        [jnp.where(live[j], cot[:, j * width : (j + 1) * width], zero) for j in range(3)], axis=1
    )

    def down(x):
        moved = jnp.concatenate([jnp.zeros((1, width), x.dtype), x[:-1]], axis=0)
        return jnp.where(same_before, moved, zero)

    grouped = jnp.concatenate([down(masked[1]), down(masked[2]), masked[0]], axis=1)
    places = jnp.arange(rows).astype(F32)
    frequency = 10000.0 ** (-(2.0 * jnp.arange(width // 2).astype(F32)) / width)
    angles = places[:, None] * frequency[None, :]
    sine, cosine = jnp.sin(angles), jnp.cos(angles)
    key_pos = jnp.concatenate([cosine, sine], axis=1).astype(BF16)

    held_a = links.deep(shard_a)
    held_c = jnp.concatenate(links.gather_near(shard_c), axis=0)
    item_col, item_row = item_f[:, None], item_f[None, :]
    if direct:
        place = jnp.stack([links.places(me, True, False), links.places(me, False, False)])
    else:
        place = jnp.tile(jnp.arange(BLOCKS, dtype=jnp.int32)[None], (2, 1))
    held_a, held_c, shard_b = lax.optimization_barrier((held_a, held_c, shard_b))
    near_a = links.gather_near(held_a)
    given = (emb, cot, cols, up_grad, grouped, sine, cosine, key_pos, item_col, item_row, place)
    near_a, given = lax.optimization_barrier((near_a, given))
    emb, cot, cols, up_grad, grouped, sine, cosine, key_pos, item_col, item_row, place = given
    pieces_a = links.gather_core(links.near_pieces(0, near_a))
    held_b = links.deep(shard_b)
    grouped, held_b = lax.optimization_barrier((grouped, held_b))
    near_b = links.gather_near(held_b)
    copies_c = jnp.concatenate([held_c] * links.dp, axis=0)
    copies_c, arrays = lax.optimization_barrier((copies_c, [x for _, _, x in pieces_a]))
    pieces_a = [(first, blocks, x) for (first, blocks, _), x in zip(pieces_a, arrays)]
    deep_c = links.deep(copies_c)
    layout_a = layout_of([(r_pool, 1), (16, 0), (3 * r, 3), (r, 1)])
    layout_b = layout_of([(r, 1), (4 * r, 4), (r_ff2, 1), (3 * r, 3)])
    layout_a32 = layout_of([(48, 1), (16, 0), (48, 3), (16, 1)])
    layout_b32 = layout_of([(16, 1), (64, 4), (64, 1), (48, 3)])

    if direct:
        base = (me % links.fsdp)[None]
    else:

        def canonical(pieces, layout):
            lines = {}
            for first, blocks, array in pieces:
                for j, (z, m) in enumerate(blocks):
                    lines.setdefault(first, {})[m, z] = array[j]
            parts = []
            for first in sorted(lines):
                arr = jnp.stack(
                    [jnp.stack([lines[first][m, z] for m in range(links.fsdp)]) for z in range(links.dp)]
                )
                arr = jnp.take(arr, jnp.arange(links.fsdp) ^ (me % links.fsdp), axis=1)
                parts.append(arr.reshape((n_dev,) + arr.shape[2:]))
            blocks = jnp.concatenate(parts, axis=1)
            outs = []
            for first, rows_, k in layout:
                if k == 0:
                    total = jnp.sum(blocks[:, first : first + rows_].astype(F32), axis=0)
                    outs.append(
                        jnp.concatenate(
                            [total[None], jnp.zeros((BLOCKS - 1,) + total.shape, F32)], axis=0
                        ).astype(BF16)
                    )
                else:
                    outs.append(reblock(blocks, [(first, rows_, k)], BLOCKS))
            return [(0, [(d, 0) for d in range(BLOCKS)], jnp.concatenate(outs, axis=1))]

        pieces_a = canonical(pieces_a, layout_a)
        base = jnp.zeros((1,), jnp.int32)

    pair_bf = sds((PAIRS, rows, 128), BF16)
    pair_f = sds((PAIRS, rows, 128), F32)
    square = sds((rows, width), F32)
    table_f = sds((16, width), F32)

    step = links.fsdp if direct else 1
    plan_a = [(first, [(z * step, m) for z, m in blocks]) for first, blocks, _ in pieces_a]
    n_a = len(plan_a)
    forward = pl.pallas_call(
        lambda *refs: forward_kernel(plan_a, n_a, *refs),
        out_shape=(
            square,
            sds((rows, width), BF16),
            pair_bf,
            pair_bf,
            pair_bf,
            pair_bf,
            sds((H, rows, rows), BF16),
            pair_bf,
            table_f,
            sds((BLOCKS, ROWS_A, width), BF16),
        ),
        in_specs=[SMEM] + [ANY] * n_a + [ANY, VMEM, VMEM, ANY, ANY, ANY],
        out_specs=[ANY] * 8 + [VMEM, ANY],
        scratch_shapes=[
            pltpu.VMEM((rows, 3 * width), BF16),
            pltpu.VMEM((rows, width // 2), F32),
            pltpu.VMEM((rows, width // 2), F32),
            pltpu.VMEM((rows, width), F32),
            pltpu.VMEM((rows, width), BF16),
        ]
        + [pltpu.VMEM((PAIRS, rows, 128), BF16)] * 4
        + [
            pltpu.VMEM((H, rows, rows), BF16),
            pltpu.VMEM((PAIRS, rows, 128), BF16),
            pltpu.VMEM((BLOCKS, ROWS_A, width), BF16),
            pltpu.VMEM((PAIRS, width, 128), BF16),
            pltpu.VMEM((rows, rows), F32),
            pltpu.VMEM((2, rows, width), F32),
            pltpu.VMEM((2, rows, width + 128), BF16),
            pltpu.VMEM((rows, width + 128), BF16),
            pltpu.VMEM((rows, width), F32),
            pltpu.VMEM((2, rows, rows), F32),
            pltpu.SemaphoreType.DMA((2,)),
            pltpu.SemaphoreType.DMA((13,)),
        ],
        compiler_params=params,
        cost_estimate=cost(20),
        name="forward",
    )
    pooled, normed, qu, qv, keys, vals, prob, ctx, vecs, wa = forward(base, *[a for _, _, a in pieces_a], grouped, item_col, item_row, sine, cosine, key_pos)
    pooled, far_b, deep_c = lax.optimization_barrier((pooled, near_b[1:], deep_c))
    near_b = near_b[:1] + far_b
    blocks_c = [(z, m) for z in range(links.dp) for m in links.near]
    pieces_b = links.gather_core(links.near_pieces(0, near_b) + [(shard_b.shape[1], blocks_c, deep_c)])
    if not direct:
        pieces_b = canonical(pieces_b, layout_b)

    plan_b = [(first, [(z * step, m) for z, m in blocks]) for first, blocks, _ in pieces_b]
    n_b = len(plan_b)
    half = BLOCKS // 2
    res_grad, cg, short_out, vec_grads, w_up_abs, keep_b, *send_b = pl.pallas_call(
        lambda *refs: middle_kernel(plan_b, n_b, *refs),
        out_shape=(
            square,
            pair_bf,
            sds((rows, width), BF16),
            table_f,
            sds((BLOCKS, 48, width), BF16),
            sds((half, ROWS_B, width), BF16),
        )
        + (sds((half, ROWS_B, width), BF16),),
        in_specs=[SMEM, SMEM] + [ANY] * n_b + [ANY, ANY, ANY, VMEM],
        out_specs=[ANY, VMEM, ANY, VMEM] + [ANY] * 3,
        scratch_shapes=[
            pltpu.VMEM((rows, width), F32),
            pltpu.VMEM((PAIRS, rows, 128), BF16),
            pltpu.VMEM((rows, 3 * width), BF16),
            pltpu.VMEM((rows, width), F32),
            pltpu.VMEM((rows, width), BF16),
            pltpu.VMEM((BLOCKS, ROWS_B, width), BF16),
            pltpu.VMEM((BLOCKS, ROWS_B, width), BF16),
            pltpu.VMEM((rows, width), F32),
            pltpu.VMEM((rows, 128), F32),
            pltpu.VMEM((rows, width), BF16),
            pltpu.VMEM((rows, 4 * 512), BF16),
            pltpu.VMEM((rows, 4 * 512), BF16),
            pltpu.VMEM((4, rows, 512), F32),
            pltpu.VMEM((rows, width), F32),
            pltpu.VMEM((4, rows, width), F32),
            pltpu.VMEM((rows, width), F32),
            pltpu.VMEM((rows, width), BF16),
            pltpu.VMEM((rows, width), BF16),
            pltpu.SemaphoreType.DMA((3,)),
            pltpu.SemaphoreType.DMA((6,)),
            pltpu.SemaphoreType.DMA((3, 2)),
        ],
        compiler_params=params,
        cost_estimate=cost(20),
        name="middle",
    )(base, place, *[a for _, _, a in pieces_b], pooled, ctx, up_grad, vecs)

    if direct:
        total_b = links.total_core(keep_b, [links.send(x, 1) for x in send_b])
        cg, total_b = lax.optimization_barrier((cg, total_b))
        near_b = links.swap_near(total_b)

    pooled_grad, w_pool_abs, keep_a, *send_a = pl.pallas_call(
        tail_kernel,
        out_shape=(
            sds((rows, width), BF16),
            sds((BLOCKS, 48, width), BF16),
            sds((half, ROWS_A, width), BF16),
        )
        + (sds((half // 4, ROWS_A, width), BF16),) * 4,
        in_specs=[SMEM] + [ANY] * 13 + [VMEM] * 2 + [ANY],
        out_specs=[VMEM] + [ANY] * 6,
        scratch_shapes=[pltpu.VMEM((PAIRS, rows, 128), BF16)] * 5
        + [
            pltpu.VMEM((rows, width), BF16),
            pltpu.VMEM((rows, width // 2), F32),
            pltpu.VMEM((rows, width // 2), F32),
            pltpu.VMEM((rows, width), BF16),
            pltpu.VMEM((rows, 3 * width), BF16),
            pltpu.VMEM((rows, width), F32),
            pltpu.VMEM((rows, width), F32),
            pltpu.VMEM((PAIRS, width, 128), BF16),
            pltpu.VMEM((rows, width), F32),
            pltpu.VMEM((rows, rows), BF16),
            pltpu.VMEM((rows, width), F32),
            pltpu.VMEM((3 * PAIRS, rows, 128), F32),
            pltpu.VMEM((3, rows, width), BF16),
            pltpu.VMEM((PAIRS, width, 128), F32),
            pltpu.VMEM((BLOCKS, ROWS_A, width), BF16),
            pltpu.VMEM((BLOCKS, ROWS_A, width), BF16),
            pltpu.VMEM((rows, width), F32),
            pltpu.VMEM((16, width), F32),
            pltpu.VMEM((2, 2, rows, rows), BF16),
            pltpu.SemaphoreType.DMA((12,)),
            pltpu.SemaphoreType.DMA((2,)),
            pltpu.SemaphoreType.DMA((13,)),
        ],
        compiler_params=params,
        cost_estimate=cost(27),
        name="tail",
    )(
        place, prob, cg, vals, keys, qu, qv, key_pos, sine, cosine, normed, grouped, pooled, res_grad, vecs,
        vec_grads, wa,
    )
    if direct:
        got_a = [links.send(x, 1) for x in send_a]
        totals_a = links.split_core(keep_a, got_a)
    out3, grad3 = pl.pallas_call(
        bytes_kernel,
        out_shape=(sds((rows, 3 * width), BF16), sds((rows, 3 * width), BF16)),
        in_specs=[VMEM] * 8,
        out_specs=[VMEM] * 2,
        scratch_shapes=[pltpu.VMEM((rows, width), F32)],
        compiler_params=params,
        cost_estimate=cost(1),
        name="bytes",
    )(emb, cot, cols, short_out, w_up_abs, vecs, pooled_grad, w_pool_abs)
    if direct:
        totals_a, near_b, out3, grad3 = lax.optimization_barrier((totals_a, near_b, out3, grad3))
        near_a = links.start_near(totals_a)
        deep_b = links.start_deep(links.total_near(near_b))
    block_output = out3.reshape(byte_total, width)
    input_grad = grad3.reshape(byte_total, width)

    if direct:
        near_a, deep_b = lax.optimization_barrier((near_a, deep_b))
        deep_a = links.start_deep(links.total_near(near_a))
        g_out, g_ff1, g_up, g_ff2 = pl.pallas_call(
            finish_b_kernel,
            out_shape=tuple(sds(w.shape, F32) for w in (w_out, w_ff1, w_up, w_ff2)),
            in_specs=[VMEM] * links.dp,
            out_specs=[VMEM] * 4,
            compiler_params=params,
            name="finish_b",
        )(*[in_vmem(x) for x in deep_b])
        g_pool, g_qkv, g_pos, *vec_out = pl.pallas_call(
            finish_a_kernel,
            out_shape=tuple(sds(w.shape, F32) for w in (w_pool, w_qkv, w_pos))
            + tuple(sds((1, n), F32) for n in lengths),
            in_specs=[SMEM] + [VMEM] * links.dp,
            out_specs=[VMEM] * 13,
            compiler_params=params,
            name="finish_a",
        )(me[None], *[in_vmem(x) for x in deep_a])
        vec_out = [v.reshape(-1) for v in vec_out]
    else:

        def owned(keep, send, layout):
            blocks = jnp.concatenate([keep, *send], axis=0)
            outs = []
            for first, rows_, k in layout:
                if k == 0:
                    outs.append(jnp.tile(blocks[:1, first : first + rows_], (n_dev, 1, 1)))
                else:
                    outs.append(reblock(blocks, [(first, rows_, k)], n_dev))
            full = jnp.concatenate(outs, axis=1)
            full = jnp.zeros_like(full).at[links.places(me, True, True)].set(full)
            return links.reduce(full[: n_dev // 2], full[n_dev // 2 :])

        sum_b = owned(keep_b, send_b, layout_b32)
        sum_a = owned(keep_a, send_a, layout_a32)
        vec_sum = sum_a[r_pool : r_pool + 16]
        vec_out = []
        for first, k, n in zip(vec_first, lengths, vec_rows):
            line = vec_sum[first : first + n].reshape(-1)
            vec_out.append(lax.dynamic_slice(line, (me * k,), (k,)))
        g_pool, g_pos, g_out, g_ff2 = sum_a[:r_pool], sum_a[split_a + 3 * r :], sum_b[:r], sum_b[5 * r : 5 * r + r_ff2]
        g_qkv = unfold(sum_a[split_a : split_a + 3 * r], 3)
        g_ff1 = unfold(sum_b[r : 5 * r], 4)
        g_up = unfold(sum_b[5 * r + r_ff2 :], 3)
    (
        out_pool_b,
        out_ln1_gain,
        out_ln1_bias,
        out_u,
        out_v,
        out_ln2_gain,
        out_ln2_bias,
        out_ff2_b,
        out_ff1_b,
        out_up_b,
    ) = vec_out
    return (
        block_output,
        input_grad,
        g_pool,
        out_pool_b,
        out_ln1_gain,
        out_ln1_bias,
        g_qkv,
        out_u,
        out_v,
        g_pos,
        g_out,
        out_ln2_gain,
        out_ln2_bias,
        g_ff1,
        out_ff1_b,
        g_ff2,
        out_ff2_b,
        g_up,
        out_up_b,
    )


def solution(mesh):
    links = Links(mesh.shape["dp"], mesh.shape["fsdp"])
    rows = P(AXES, None)
    flat = P(AXES)
    ranks = (2, 1, 1, 2, 1, 1, 1, 2, 1, 1, 2, 2, 1, 1, 2, 1, 2, 1, 2, 1, 2)
    out_ranks = (2, 2, 2, 1, 1, 1, 2, 1, 1, 2, 2, 1, 1, 2, 1, 2, 1, 2, 1)
    return jax.shard_map(
        lambda *args: per_device(links, *args),
        mesh=mesh,
        in_specs=tuple(rows if k == 2 else flat for k in ranks),
        out_specs=tuple(rows if k == 2 else flat for k in out_ranks),
        check_vma=False,
    )
```
